128 devices in a mesh: det: 16 (over z_lo, x, core), strip: 8 (over y, z_hi).
Axes of the slice: x: 4, y: 4, z: 4 (z_hi: 2, z_lo: 2; z = z_hi * 2 + z_lo), core: 2. Of those that a mesh axis runs over, the one named last changes fastest.
Arguments:
- science: float32 [16, 256, 4096], P('det', 'strip'), may hold values from -17 to 17
- template: float32 [16, 256, 4096], P(None, 'strip', 'det'), may hold values from -8 to 8
- row_taps: float32 [12, 21], replicated, may hold values from -1.25 to 1.25
- col_taps: float32 [12, 21], replicated, may hold values from -1.25 to 1.25
- stamp_rows: int32 [16, 32], P('det'), may hold values from 17 to 238
- stamp_cols: int32 [16, 32], P('det'), may hold values from 17 to 4078
Outputs:
- difference: float32 [16, 256, 4096], P('det', 'strip')
- kernel_coeffs: float32 [16, 37], P('det')
The draws below stay inside these ranges and needn't reach their ends.
All inputs are finite; a program needn't handle non-finite values.
Results may differ from the reference program's by a relative error of at most 0.0003.
Values sent between devices are 32-bit elements; how exact they have to be, the bound alone decides.
A program may use at most 128 MiB of HBM per device.

```python
import jax
import jax.numpy as jnp
from jax import lax

COLS = 4096
NB = 12
KS = 21
HS = 17
NSTAMP = 32
KH = 10
NU = 37
DETS = 16
ROWS = 256


def sky_pair(key):
    shape = (DETS, ROWS, COLS)
    rough = jnp.clip(jax.random.normal(jax.random.fold_in(key, 11), shape, jnp.float32), -6.0, 6.0)
    template = rough
    offsets = 0.3 + 0.6 * jax.random.uniform(jax.random.fold_in(key, 13), (DETS, 1, 1), jnp.float32)
    noise = jnp.clip(jax.random.normal(jax.random.fold_in(key, 14), shape, jnp.float32), -6.0, 6.0)
    x_coord = (2.0 * jnp.arange(COLS, dtype=jnp.float32) / COLS - 1.0)[None, None, :]
    science = offsets + (0.7 + 0.3 * x_coord) * template + 0.3 * jnp.roll(template, 1, axis=2) + 0.2 * jnp.roll(template, -1, axis=1) + 0.5 * noise
    return (science, template)


def draw_science(key, part):
    return sky_pair(key)[0]


def draw_template(key, part):
    return sky_pair(key)[1]


def touch_ends(entries, rng, low, largest):
    extent = entries.shape
    index_at = [jax.random.randint(jax.random.fold_in(rng, axis), (), 0, extent[axis]) for axis in range(len(extent))]
    entries = entries.at[tuple(index_at)].set(low)
    longest = extent.index(max(extent))
    index_at[longest] = (index_at[longest] + 1) % extent[longest]
    return entries.at[tuple(index_at)].set(largest)


def centred(stream_key, extent, deviation, reach, held_as=jnp.bfloat16):
    return jnp.clip(deviation * jax.random.normal(stream_key, extent, jnp.float32), -reach, reach).astype(held_as)


def setup_inputs(seed: int = 0) -> dict:
    splits = jax.random.split(jax.random.key(seed), 7)
    science = draw_science(jax.random.fold_in(splits[6], 71), 0)
    template = draw_template(jax.random.fold_in(splits[6], 71), 0)
    row_taps = centred(splits[2], (NB, KS), KS ** -0.5, 1.25, jnp.float32)
    col_taps = centred(splits[3], (NB, KS), KS ** -0.5, 1.25, jnp.float32)
    stamp_rows = touch_ends(jax.random.randint(splits[4], (DETS, NSTAMP), HS, ROWS - HS), jax.random.fold_in(splits[4], 1), HS, (ROWS - HS) - 1).astype(jnp.int32)
    stamp_cols = touch_ends(jax.random.randint(splits[5], (DETS, NSTAMP), HS, COLS - HS), jax.random.fold_in(splits[5], 1), HS, (COLS - HS) - 1).astype(jnp.int32)
    return {"science": science, "template": template, "row_taps": row_taps, "col_taps": col_taps, "stamp_rows": stamp_rows, "stamp_cols": stamp_cols}


RIDGE_WEIGHT = 1.0
HIGHEST_MODE = lax.Precision.HIGHEST

def correlate(picture, row_taps, col_taps):
    planes = picture[None, None]
    across = lax.conv_general_dilated(planes, col_taps[:, None, None, :], (1, 1), ((0, 0), (KH, KH)), precision=HIGHEST_MODE)
    return lax.conv_general_dilated(across, row_taps[:, None, :, None], (1, 1), ((KH, KH), (0, 0)), feature_group_count=NB, precision=HIGHEST_MODE)[0]

def features(responses, y_coord, x_coord):
    flat = responses.reshape(NB, -1)
    y_flat = jnp.broadcast_to(y_coord, responses.shape[1:]).reshape(1, -1)
    x_flat = jnp.broadcast_to(x_coord, responses.shape[1:]).reshape(1, -1)
    unity = jnp.ones((1, flat.shape[1]), jnp.float32)
    return jnp.concatenate([flat, flat * x_flat, flat * y_flat, unity], axis=0)

def apply_model(responses, coeffs, y_coord, x_coord):
    base_part = jnp.tensordot(coeffs[:NB], responses, axes=1, precision=HIGHEST_MODE)
    x_part = jnp.tensordot(coeffs[NB:2 * NB], responses, axes=1, precision=HIGHEST_MODE)
    y_part = jnp.tensordot(coeffs[2 * NB:3 * NB], responses, axes=1, precision=HIGHEST_MODE)
    return base_part + x_coord * x_part + y_coord * y_part + coeffs[NU - 1]

def reference(science, template, row_taps, col_taps, stamp_rows, stamp_cols):
    y_coord = (2.0 * jnp.arange(ROWS, dtype=jnp.float32) / ROWS - 1.0)[:, None]
    x_coord = (2.0 * jnp.arange(COLS, dtype=jnp.float32) / COLS - 1.0)[None, :]
    stamp_side = 2 * HS + 1

    def one_detector(inputs):
        picture, observed, rows_at, cols_at = inputs
        responses = correlate(picture, row_taps, col_taps)

        def one_stamp(centre):
            top_row = (centre[0] - HS).astype(jnp.int32)
            left_col = (centre[1] - HS).astype(jnp.int32)
            anchor = jnp.zeros((), jnp.int32)
            window = lax.dynamic_slice(responses, (anchor, top_row, left_col), (NB, stamp_side, stamp_side))
            y_window = lax.dynamic_slice(y_coord, (top_row, anchor), (stamp_side, 1))
            x_window = lax.dynamic_slice(x_coord, (anchor, left_col), (1, stamp_side))
            sci_window = lax.dynamic_slice(observed, (top_row, left_col), (stamp_side, stamp_side))
            feats = features(window, y_window, x_window)
            normal = jnp.dot(feats.astype(jnp.float32), feats.T.astype(jnp.float32), precision=HIGHEST_MODE, preferred_element_type=jnp.float32)
            target = jnp.dot(feats.astype(jnp.float32), sci_window.reshape(-1).astype(jnp.float32), precision=HIGHEST_MODE, preferred_element_type=jnp.float32)
            return (normal, target)
        normals, targets = lax.map(one_stamp, jnp.stack([rows_at, cols_at], axis=1))
        normal = jnp.sum(normals, axis=0) + RIDGE_WEIGHT * jnp.eye(NU, dtype=jnp.float32)
        coeffs = jnp.linalg.solve(normal, jnp.sum(targets, axis=0))
        return (observed - apply_model(responses, coeffs, y_coord, x_coord), coeffs)
    difference, kernel_coeffs = lax.map(one_detector, (template, science, stamp_rows, stamp_cols))
    return (difference, kernel_coeffs)
```

```python
import functools

import jax
import jax.numpy as jnp
from jax import lax
from jax.experimental import pallas as pl
from jax.experimental.pallas import tpu as pltpu
from jax.sharding import PartitionSpec as P

NB = 12
KS = 21
HS = 17
KH = 10
NU = 37
LW = 128
HALO = 16
SLOT = 42
PLANES = 16
ONE_PLANE = 12
SCI_PLANE = 13
RIDGE_WEIGHT = 1.0
HIGHEST_MODE = lax.Precision.HIGHEST
MESH = pl.DeviceIdType.MESH
BF = jnp.bfloat16
F32 = jnp.float32


def iota(shape, dim):
    return lax.broadcasted_iota(jnp.int32, shape, dim)


def split(value):
    high = value.astype(BF)
    return high, (value - high.astype(F32)).astype(BF)


def build_row_table(taps_ref, pad_ref, table_ref, rows):
    pad_ref[...] = jnp.zeros_like(pad_ref)
    pad_ref[:NB, :KS] = taps_ref[...]
    for b in range(NB):
        wide = jnp.broadcast_to(pad_ref[b : b + 1, :], (rows, LW))
        moved = pltpu.roll(wide, HALO - KH, 1, stride=1, stride_axis=0)
        high, low = split(moved)
        high, low = high.astype(F32), low.astype(F32)
        high = high + pltpu.roll(high, 64, 1)
        low = low + pltpu.roll(low, 64, 1)
        table_ref[b * rows : (b + 1) * rows, :LW] = high.astype(BF)
        table_ref[b * rows : (b + 1) * rows, LW:] = low.astype(BF)


def build_col_tables(taps_ref, pad_ref, table_ref):
    pad_ref[...] = jnp.zeros_like(pad_ref)
    pad_ref[:NB, :KS] = taps_ref[...]
    lane, sub = iota((LW, LW), 1), iota((LW, LW), 0)
    for b in range(NB):
        wide = jnp.broadcast_to(pad_ref[b : b + 1, :], (LW, LW))
        moved = pltpu.roll(wide, 0, 1, stride=1, stride_axis=0)
        near = jnp.where(lane >= sub, moved, 0.0).T
        far = jnp.where(lane < sub, moved, 0.0).T
        for part, at in ((near, 0), (far, LW)):
            high, low = split(part)
            table_ref[b, at : at + LW, :LW] = high
            table_ref[b, at : at + LW, LW:] = low


def row_stage(frame_ref, row_table_ref, win_hi_ref, win_lo_ref, chunk, rows, cols):
    width = 256 if chunk * 256 < cols else LW
    start = chunk * 256
    lane = iota((64, LW), 1)
    pieces = []
    for at in range(start, start + width, LW):
        here = pltpu.roll(frame_ref[:, at : at + LW], KH, 1) if at < cols else jnp.zeros((64, LW), F32)
        prev = pltpu.roll(frame_ref[:, at - LW : at], KH, 1) if at > 0 else jnp.zeros((64, LW), F32)
        pieces.append(jnp.where(lane < KH, prev, here))
    moved = jnp.concatenate(pieces, axis=1) if len(pieces) > 1 else pieces[0]
    high, low = split(moved)
    stacked = jnp.concatenate([high, low, high, low], axis=0)
    blocks = cols // LW
    first = start // LW
    for b in range(NB):
        out = jnp.dot(row_table_ref[b * rows : (b + 1) * rows, :], stacked, preferred_element_type=F32)
        hi, lo = split(out)
        for ref, val in ((win_hi_ref, hi), (win_lo_ref, lo)):
            for i in range(width // LW):
                part = val[:, i * LW : (i + 1) * LW]
                k = first + i
                if k < blocks:
                    ref[b, k, :, :LW] = part
                if k > 0:
                    ref[b, k - 1, :, LW:] = part


def col_stage(win_hi_ref, win_lo_ref, col_table_ref, resp_ref, rows, cols):
    blocks = cols // LW
    per = 8

    def body(b, carry):
        table = col_table_ref[b]
        for k in range(0, blocks, per):
            hi = win_hi_ref[b, k : k + per].reshape(per * rows, 2 * LW)
            lo = win_lo_ref[b, k : k + per].reshape(per * rows, 2 * LW)
            out = jnp.dot(hi, table, preferred_element_type=F32) + jnp.dot(lo, table, preferred_element_type=F32)
            resp_ref[b, k : k + per] = (out[:, :LW] + out[:, LW:]).reshape(per, rows, LW)
        return carry

    lax.fori_loop(0, NB, body, 0)


def pack_stamps(resp_ref, rows_ref, cols_ref, left_ref, right_ref, first_row, rows, cols, stamps):
    groups = rows // 8
    lane3 = iota((1, 1, LW), 2)
    lane2 = iota((8, LW), 1)

    def body(q, carry):
        packed = None
        rowv = jnp.full((8, LW), -(1 << 20), jnp.int32)
        colv = jnp.zeros((8, LW), jnp.int32)
        for t in range(3):
            s = q * 3 + t
            held = jnp.minimum(s, stamps - 1)
            left = jnp.clip(cols_ref[0, held] - HS, 0, cols - 1)
            row = jnp.where(s < stamps, rows_ref[0, held], -(1 << 20))
            k = left // LW
            off = left - k * LW
            near, far = resp_ref[:, k], resp_ref[:, k + 1]
            both = jnp.where(lane3 >= off, near, far)
            shift = lax.rem(SLOT * t - off + LW, LW)
            flat = pltpu.roll(both.reshape(SCI_PLANE + 1 - 0, rows, LW).reshape(-1, LW), shift, 1)
            flat = flat.reshape(SCI_PLANE + 1, rows, LW)
            packed = flat if packed is None else jnp.where(lane3 >= SLOT * t, flat, packed)
            inside = (lane2 >= SLOT * t) & (lane2 < SLOT * t + 2 * HS + 1)
            rowv = jnp.where(inside, row, rowv)
            colv = jnp.where(inside, left + lane2 - SLOT * t, colv)
        xv = colv.astype(F32) * (2.0 / cols) - 1.0
        at = pl.multiple_of(q * LW, LW)
        tail = jnp.zeros((PLANES - SCI_PLANE - 1, 8, LW), F32)
        for g in range(groups):
            yv = first_row + 8 * g + iota((8, LW), 0)
            hit = (jnp.abs(yv - rowv) <= HS).astype(F32)
            planes = jnp.concatenate([packed[:, 8 * g : 8 * g + 8, :], tail], axis=0)
            high, low = split(planes.reshape(PLANES * 8, LW))
            right_ref[g, : PLANES * 8, pl.ds(at, LW)] = high
            right_ref[g, PLANES * 8 :, pl.ds(at, LW)] = low
            moment = planes * hit[None]
            for m in range(3):
                if m:
                    moment = moment * xv[None]
                high, low = split(moment.reshape(PLANES * 8, LW))
                left_ref[g, m * PLANES * 8 : (m + 1) * PLANES * 8, pl.ds(at, LW)] = high
                left_ref[g, (m + 3) * PLANES * 8 : (m + 4) * PLANES * 8, pl.ds(at, LW)] = low
        return carry

    lax.fori_loop(0, (stamps + 2) // 3, body, 0)


def normal_part(left_ref, right_ref, first_row, rows, total_rows):
    groups = rows // 8
    span = PLANES * 8
    same_y = (lax.rem(iota((8, span), 1), 8) == iota((8, span), 0)).astype(F32)
    plane, col = iota((span, LW), 0) // 8, iota((span, LW), 1)
    kind, base = col // 16, lax.rem(col, 16)
    match = plane == base
    real = match & (plane < NB)
    total = None
    for g in range(groups):
        out = lax.dot_general(left_ref[g], right_ref[g], (((1,), (1,)), ((), ())), preferred_element_type=F32)
        folded = out[: 3 * span, :span] + out[: 3 * span, span:] + out[3 * span :, :span]
        picked = jnp.sum(folded.reshape(3 * PLANES, 8, span) * same_y[None], axis=1)
        y = (2.0 / total_rows) * (first_row + 8 * g + lax.rem(iota((span, LW), 0), 8)).astype(F32) - 1.0
        zero = jnp.zeros((span, LW), F32)
        plain = jnp.where(match & (kind == 0), 1.0, zero)
        in_x = jnp.where(real & (kind == 1), 1.0, zero)
        in_y = jnp.where(real & (kind == 2), y, zero)
        maps = jnp.concatenate([plain + in_y, in_x, (plain + in_y) * y, in_x * y], axis=1)
        part = jnp.dot(picked, maps, precision=HIGHEST_MODE, preferred_element_type=F32)
        total = part if total is None else total + part
    return jnp.concatenate(
        [
            total[0:16, 0:LW] + total[16:32, LW : 2 * LW],
            total[16:32, 0:LW] + total[32:48, LW : 2 * LW],
            total[0:16, 2 * LW : 3 * LW] + total[16:32, 3 * LW :],
        ],
        axis=0,
    )


PIVOTS = [*range(0, 13), *range(16, 28), *range(32, 44)]


def solve(normal):
    sub, lane = iota((48, LW), 0), iota((48, LW), 1)
    live = (lax.rem(sub, 16) < NB) | (sub == ONE_PLANE)
    mat = jnp.where((sub == lane) & live, normal + RIDGE_WEIGHT, normal)
    for k in PIVOTS:
        column = jnp.broadcast_to(mat[:, k : k + 1], (48, LW))
        pivot = column[k : k + 1, :]
        row = mat[k : k + 1, :] / pivot
        mat = jnp.where(sub == k, row, mat - column * row)
    return mat[:, SCI_PLANE : SCI_PLANE + 1]


def coeff_row(answer):
    sub, lane = iota((48, LW), 0), iota((48, LW), 1)
    kind, base = sub // 16, lax.rem(sub, 16)
    goes = jnp.where(base < NB, kind * NB + base, jnp.where(sub == ONE_PLANE, NU - 1, -1))
    return jnp.sum(jnp.where(goes == lane, answer, 0.0), axis=0, keepdims=True)


def apply_model(answer, resp_ref, out_ref, first_row, rows, total_rows, cols):
    wide = jnp.broadcast_to(answer, (48, LW))
    lift = lambda i: jnp.broadcast_to(wide[i : i + 1, :], (8, LW))
    blocks = cols // LW
    const = lift(ONE_PLANE)
    for g in range(rows // 8):
        y = (2.0 / total_rows) * (first_row + 8 * g + iota((8, LW), 0)).astype(F32) - 1.0
        level = [lift(b) + y * lift(32 + b) for b in range(NB)]
        slope = [lift(16 + b) for b in range(NB)]

        def body(k, carry):
            flat = const
            tilt = jnp.zeros((8, LW), F32)
            for b in range(NB):
                r = resp_ref[b, k, 8 * g : 8 * g + 8, :]
                flat = flat + level[b] * r
                tilt = tilt + slope[b] * r
            at = pl.multiple_of(k * LW, LW)
            x = (k * LW + iota((8, LW), 1)).astype(F32) * (2.0 / cols) - 1.0
            out_ref[0, 8 * g : 8 * g + 8, pl.ds(at, LW)] = resp_ref[SCI_PLANE, k, 8 * g : 8 * g + 8, :] - (flat + x * tilt)
            return carry

        lax.fori_loop(0, blocks, body, 0, unroll=4)


def kernel(
    dets, strips,
    sci_ref, tmpl_ref, row_ref, col_ref, srow_ref, scol_ref,
    out_ref, coef_ref,
    frame, pad, row_table, col_table, win_hi, win_lo, resp, left, right, parts, sci_buf,
    main_send, main_recv, up_send, up_recv, down_send, down_recv, part_send, part_recv, own_sem, sci_sem,
):
    _, rows, cols = sci_ref.shape
    width = tmpl_ref.shape[2]
    total_rows = rows * strips
    det, strip = lax.axis_index("det"), lax.axis_index("strip")
    above, below = strip > 0, strip < strips - 1
    first_row = strip * rows

    frame[0:HALO, :] = jnp.zeros((HALO, cols), F32)
    frame[HALO + rows :, :] = jnp.zeros((HALO, cols), F32)

    barrier = pltpu.get_barrier_semaphore()

    def greet(target_det, target_strip):
        pl.semaphore_signal(barrier, inc=1, device_id=(target_det, target_strip), device_id_type=MESH)

    for i in range(1, dets):
        greet(lax.rem(det + i, dets), strip)

    @pl.when(above)
    def _():
        for i in range(dets):
            greet(lax.rem(det + i, dets), strip - 1)

    @pl.when(below)
    def _():
        for i in range(dets):
            greet(lax.rem(det + i, dets), strip + 1)

    for i in range(2, strips - 1):
        other = lax.rem(strip + i, strips)

        @pl.when((other != strip - 1) & (other != strip + 1))
        def _():
            greet(det, other)

    @pl.when(strip == 0)
    def _():
        greet(det, strips - 1)

    @pl.when(strip == strips - 1)
    def _():
        greet(det, 0)

    ends = jnp.where(above & below, 0, 1)
    count = (dets - 1) + dets * (2 - ends) + (strips - 3 + ends)
    pl.semaphore_wait(barrier, count)

    def main_copy(i):
        target = lax.rem(det + i, dets)
        return pltpu.make_async_remote_copy(
            tmpl_ref.at[target], frame.at[pl.ds(HALO, rows), pl.ds(pl.multiple_of(det * width, width), width)],
            main_send.at[i], main_recv.at[i], device_id=(target, strip), device_id_type=MESH,
        )

    def up_copy(i):
        target = lax.rem(det + i, dets)
        return pltpu.make_async_remote_copy(
            tmpl_ref.at[target, pl.ds(0, HALO), :],
            frame.at[pl.ds(HALO + rows, HALO), pl.ds(pl.multiple_of(det * width, width), width)],
            up_send.at[i], up_recv.at[i], device_id=(target, strip - 1), device_id_type=MESH,
        )

    def down_copy(i):
        target = lax.rem(det + i, dets)
        return pltpu.make_async_remote_copy(
            tmpl_ref.at[target, pl.ds(rows - HALO, HALO), :],
            frame.at[pl.ds(0, HALO), pl.ds(pl.multiple_of(det * width, width), width)],
            down_send.at[i], down_recv.at[i], device_id=(target, strip + 1), device_id_type=MESH,
        )

    own = pltpu.make_async_copy(
        tmpl_ref.at[det], frame.at[pl.ds(HALO, rows), pl.ds(pl.multiple_of(det * width, width), width)], own_sem
    )
    own.start()
    sci_copy = pltpu.make_async_copy(sci_ref.at[0], sci_buf, sci_sem)
    sci_copy.start()
    for i in range(dets):
        if i:
            main_copy(i).start()

        @pl.when(above)
        def _():
            up_copy(i).start()

        @pl.when(below)
        def _():
            down_copy(i).start()

    build_row_table(row_ref, pad, row_table, rows)
    build_col_tables(col_ref, pad, col_table)
    blocks = cols // LW
    sci_copy.wait()
    for k in range(blocks):
        resp[SCI_PLANE, k] = sci_buf[:, k * LW : (k + 1) * LW]
    resp[ONE_PLANE] = jnp.ones((blocks + 1, rows, LW), F32)
    resp[:ONE_PLANE, blocks] = jnp.zeros((NB, rows, LW), F32)
    resp[SCI_PLANE, blocks] = jnp.zeros((rows, LW), F32)

    own.wait()
    for i in range(dets):
        if i:
            main_copy(i).wait()

        @pl.when(above)
        def _():
            up_copy(i).wait_send()
            down_copy(i).wait_recv()

        @pl.when(below)
        def _():
            down_copy(i).wait_send()
            up_copy(i).wait_recv()

    for chunk in range(cols // 256 + 1):
        row_stage(frame, row_table, win_hi, win_lo, chunk, rows, cols)
    col_stage(win_hi, win_lo, col_table, resp, rows, cols)
    pack_stamps(resp, srow_ref, scol_ref, left, right, first_row, rows, cols, srow_ref.shape[1])
    parts[strip] = normal_part(left, right, first_row, rows, total_rows)

    def part_copy(i):
        return pltpu.make_async_remote_copy(
            parts.at[strip], parts.at[strip], part_send.at[i], part_recv.at[i],
            device_id=(det, lax.rem(strip + i, strips)), device_id_type=MESH,
        )

    for i in range(1, strips):
        part_copy(i).start()
    for i in range(1, strips):
        source = lax.rem(strip + strips - i, strips)
        part_copy(i).wait_send()
        pltpu.make_async_remote_copy(
            parts.at[source], parts.at[source], part_send.at[i], part_recv.at[i],
            device_id=(det, source), device_id_type=MESH,
        ).wait_recv()
    normal = parts[0]
    for i in range(1, strips):
        normal = normal + parts[i]
    answer = solve(normal)
    coef_ref[...] = coeff_row(answer)[:, :NU]
    apply_model(answer, resp, out_ref, first_row, rows, total_rows, cols)


def local(dets, strips, science, template, row_taps, col_taps, stamp_rows, stamp_cols):
    _, rows, cols = science.shape
    blocks = cols // LW
    stamps = stamp_rows.shape[1]
    packed = (stamps + 2) // 3 * LW
    any_space = pl.BlockSpec(memory_space=pl.ANY)
    vmem = pl.BlockSpec(memory_space=pltpu.VMEM)
    smem = pl.BlockSpec(memory_space=pltpu.SMEM)
    dma = pltpu.SemaphoreType.DMA
    return pl.pallas_call(
        functools.partial(kernel, dets, strips),
        out_shape=(jax.ShapeDtypeStruct(science.shape, F32), jax.ShapeDtypeStruct((1, NU), F32)),
        in_specs=[any_space, any_space, vmem, vmem, smem, smem],
        out_specs=(vmem, vmem),
        scratch_shapes=[
            pltpu.VMEM((rows + 2 * HALO, cols), F32),
            pltpu.VMEM((16, LW), F32),
            pltpu.VMEM((NB * rows, 256), BF),
            pltpu.VMEM((NB, 256, 256), BF),
            pltpu.VMEM((NB, blocks, rows, 256), BF),
            pltpu.VMEM((NB, blocks, rows, 256), BF),
            pltpu.VMEM((SCI_PLANE + 1, blocks + 1, rows, LW), F32),
            pltpu.VMEM((rows // 8, 6 * PLANES * 8, packed), BF),
            pltpu.VMEM((rows // 8, 2 * PLANES * 8, packed), BF),
            pltpu.VMEM((strips, 48, LW), F32),
            pltpu.VMEM((rows, cols), F32),
            dma((dets,)), dma((dets,)), dma((dets,)), dma((dets,)), dma((dets,)), dma((dets,)),
            dma((strips,)), dma((strips,)), dma, dma,
        ],
        compiler_params=pltpu.CompilerParams(
            collective_id=0, has_side_effects=True, vmem_limit_bytes=56 * 1024 * 1024
        ),
    )(science, template, row_taps, col_taps, stamp_rows, stamp_cols)


def solution(mesh):
    return jax.shard_map(
        functools.partial(local, mesh.shape["det"], mesh.shape["strip"]),
        mesh=mesh,
        in_specs=(
            P("det", "strip", None),
            P(None, "strip", "det"),
            P(),
            P(),
            P("det", None),
            P("det", None),
        ),
        out_specs=(P("det", "strip", None), P("det", None)),
        check_vma=False,
    )
```

```python
import functools

import jax
import jax.numpy as jnp
from jax import lax
from jax.experimental import pallas as pl
from jax.experimental.pallas import tpu as pltpu
from jax.sharding import PartitionSpec as P

NB = 12
KS = 21
HS = 17
KH = 10
NU = 37
LW = 128
HALO = 16
SLOT = 42
PLANES = 16
ONE_PLANE = 12
SCI_PLANE = 13
RIDGE_WEIGHT = 1.0
HIGHEST_MODE = lax.Precision.HIGHEST
MESH = pl.DeviceIdType.MESH
BF = jnp.bfloat16
F32 = jnp.float32


def iota(shape, dim):
    return lax.broadcasted_iota(jnp.int32, shape, dim)


def split(value):
    high = value.astype(BF)
    return high, (value - high.astype(F32)).astype(BF)


def build_row_table(taps_ref, pad_ref, table_ref, rows):
    pad_ref[...] = jnp.zeros_like(pad_ref)
    pad_ref[:NB, :KS] = taps_ref[...]
    for b in range(NB):
        wide = jnp.broadcast_to(pad_ref[b : b + 1, :], (rows, LW))
        moved = pltpu.roll(wide, HALO - KH, 1, stride=1, stride_axis=0)
        high, low = split(moved)
        high, low = high.astype(F32), low.astype(F32)
        high = high + pltpu.roll(high, 64, 1)
        low = low + pltpu.roll(low, 64, 1)
        table_ref[b * rows : (b + 1) * rows, :LW] = high.astype(BF)
        table_ref[b * rows : (b + 1) * rows, LW:] = low.astype(BF)


def build_col_tables(taps_ref, pad_ref, table_ref):
    pad_ref[...] = jnp.zeros_like(pad_ref)
    pad_ref[:NB, :KS] = taps_ref[...]
    lane, sub = iota((LW, LW), 1), iota((LW, LW), 0)
    for b in range(NB):
        wide = jnp.broadcast_to(pad_ref[b : b + 1, :], (LW, LW))
        moved = pltpu.roll(wide, 0, 1, stride=1, stride_axis=0)
        near = jnp.where(lane >= sub, moved, 0.0).T
        far = jnp.where(lane < sub, moved, 0.0).T
        for part, at in ((near, 0), (far, LW)):
            high, low = split(part)
            table_ref[b, at : at + LW, :LW] = high
            table_ref[b, at : at + LW, LW:] = low


def row_stage(frame_ref, row_table_ref, win_hi_ref, win_lo_ref, chunk, first_row, rows, cols, total_rows):
    width = 256 if chunk * 256 < cols else LW
    start = chunk * 256
    lane = iota((64, LW), 1)
    pieces = []
    for at in range(start, start + width, LW):
        here = pltpu.roll(frame_ref[:, at : at + LW], KH, 1) if at < cols else jnp.zeros((64, LW), F32)
        prev = pltpu.roll(frame_ref[:, at - LW : at], KH, 1) if at > 0 else jnp.zeros((64, LW), F32)
        pieces.append(jnp.where(lane < KH, prev, here))
    moved = jnp.concatenate(pieces, axis=1) if len(pieces) > 1 else pieces[0]
    sub = iota(moved.shape, 0)
    sky = first_row - HALO + sub
    held = (sub >= HALO - KH) & (sub < HALO + rows + KH) & (sky >= 0) & (sky < total_rows)
    moved = jnp.where(held, moved, 0.0)
    high, low = split(moved)
    stacked = jnp.concatenate([high, low, high, low], axis=0)
    blocks = cols // LW
    first = start // LW
    for b in range(NB):
        out = jnp.dot(row_table_ref[b * rows : (b + 1) * rows, :], stacked, preferred_element_type=F32)
        hi, lo = split(out)
        for ref, val in ((win_hi_ref, hi), (win_lo_ref, lo)):
            for i in range(width // LW):
                part = val[:, i * LW : (i + 1) * LW]
                k = first + i
                if k < blocks:
                    ref[b, k, :, :LW] = part
                if k > 0:
                    ref[b, k - 1, :, LW:] = part


def col_stage(win_hi_ref, win_lo_ref, col_table_ref, resp_ref, rows, cols):
    blocks = cols // LW
    per = 8

    def body(b, carry):
        table = col_table_ref[b]
        for k in range(0, blocks, per):
            hi = win_hi_ref[b, k : k + per].reshape(per * rows, 2 * LW)
            lo = win_lo_ref[b, k : k + per].reshape(per * rows, 2 * LW)
            out = jnp.dot(hi, table, preferred_element_type=F32) + jnp.dot(lo, table, preferred_element_type=F32)
            resp_ref[b, k : k + per] = (out[:, :LW] + out[:, LW:]).reshape(per, rows, LW)
        return carry

    lax.fori_loop(0, NB, body, 0)


def pack_stamps(resp_ref, rows_ref, cols_ref, left_ref, right_ref, first_row, rows, cols, stamps):
    groups = rows // 8
    lane3 = iota((1, 1, LW), 2)
    lane2 = iota((8, LW), 1)

    def body(q, carry):
        packed = None
        rowv = jnp.full((8, LW), -(1 << 20), jnp.int32)
        colv = jnp.zeros((8, LW), jnp.int32)
        for t in range(3):
            s = q * 3 + t
            held = jnp.minimum(s, stamps - 1)
            left = jnp.clip(cols_ref[0, held] - HS, 0, cols - 1)
            row = jnp.where(s < stamps, rows_ref[0, held], -(1 << 20))
            k = left // LW
            off = left - k * LW
            near, far = resp_ref[:, k], resp_ref[:, k + 1]
            both = jnp.where(lane3 >= off, near, far)
            shift = lax.rem(SLOT * t - off + LW, LW)
            flat = pltpu.roll(both.reshape(SCI_PLANE + 1 - 0, rows, LW).reshape(-1, LW), shift, 1)
            flat = flat.reshape(SCI_PLANE + 1, rows, LW)
            packed = flat if packed is None else jnp.where(lane3 >= SLOT * t, flat, packed)
            inside = (lane2 >= SLOT * t) & (lane2 < SLOT * t + 2 * HS + 1)
            rowv = jnp.where(inside, row, rowv)
            colv = jnp.where(inside, left + lane2 - SLOT * t, colv)
        xv = colv.astype(F32) * (2.0 / cols) - 1.0
        at = pl.multiple_of(q * LW, LW)
        tail = jnp.zeros((PLANES - SCI_PLANE - 1, 8, LW), F32)
        for g in range(groups):
            yv = first_row + 8 * g + iota((8, LW), 0)
            hit = (jnp.abs(yv - rowv) <= HS).astype(F32)
            planes = jnp.concatenate([packed[:, 8 * g : 8 * g + 8, :], tail], axis=0)
            high, low = split(planes.reshape(PLANES * 8, LW))
            right_ref[g, : PLANES * 8, pl.ds(at, LW)] = high
            right_ref[g, PLANES * 8 :, pl.ds(at, LW)] = low
            moment = planes * hit[None]
            for m in range(3):
                if m:
                    moment = moment * xv[None]
                high, low = split(moment.reshape(PLANES * 8, LW))
                left_ref[g, m * PLANES * 8 : (m + 1) * PLANES * 8, pl.ds(at, LW)] = high
                left_ref[g, (m + 3) * PLANES * 8 : (m + 4) * PLANES * 8, pl.ds(at, LW)] = low
        return carry

    lax.fori_loop(0, (stamps + 2) // 3, body, 0)


def normal_part(left_ref, right_ref, first_row, rows, total_rows):
    groups = rows // 8
    span = PLANES * 8
    same_y = (lax.rem(iota((8, span), 1), 8) == iota((8, span), 0)).astype(F32)
    plane, col = iota((span, LW), 0) // 8, iota((span, LW), 1)
    kind, base = col // 16, lax.rem(col, 16)
    match = plane == base
    real = match & (plane < NB)
    total = None
    for g in range(groups):
        out = lax.dot_general(left_ref[g], right_ref[g], (((1,), (1,)), ((), ())), preferred_element_type=F32)
        folded = out[: 3 * span, :span] + out[: 3 * span, span:] + out[3 * span :, :span]
        picked = jnp.sum(folded.reshape(3 * PLANES, 8, span) * same_y[None], axis=1)
        y = (2.0 / total_rows) * (first_row + 8 * g + lax.rem(iota((span, LW), 0), 8)).astype(F32) - 1.0
        zero = jnp.zeros((span, LW), F32)
        plain = jnp.where(match & (kind == 0), 1.0, zero)
        in_x = jnp.where(real & (kind == 1), 1.0, zero)
        in_y = jnp.where(real & (kind == 2), y, zero)
        maps = jnp.concatenate([plain + in_y, in_x, (plain + in_y) * y, in_x * y], axis=1)
        part = jnp.dot(picked, maps, precision=HIGHEST_MODE, preferred_element_type=F32)
        total = part if total is None else total + part
    return jnp.concatenate(
        [
            total[0:16, 0:LW] + total[16:32, LW : 2 * LW],
            total[16:32, 0:LW] + total[32:48, LW : 2 * LW],
            total[0:16, 2 * LW : 3 * LW] + total[16:32, 3 * LW :],
        ],
        axis=0,
    )


PIVOTS = [*range(0, 13), *range(16, 28), *range(32, 44)]


def solve(normal):
    sub, lane = iota((48, LW), 0), iota((48, LW), 1)
    live = (lax.rem(sub, 16) < NB) | (sub == ONE_PLANE)
    mat = jnp.where((sub == lane) & live, normal + RIDGE_WEIGHT, normal)
    for k in PIVOTS:
        column = jnp.broadcast_to(mat[:, k : k + 1], (48, LW))
        pivot = column[k : k + 1, :]
        row = mat[k : k + 1, :] / pivot
        mat = jnp.where(sub == k, row, mat - column * row)
    return mat[:, SCI_PLANE : SCI_PLANE + 1]


def coeff_row(answer):
    sub, lane = iota((48, LW), 0), iota((48, LW), 1)
    kind, base = sub // 16, lax.rem(sub, 16)
    goes = jnp.where(base < NB, kind * NB + base, jnp.where(sub == ONE_PLANE, NU - 1, -1))
    return jnp.sum(jnp.where(goes == lane, answer, 0.0), axis=0, keepdims=True)


def apply_model(answer, resp_ref, out_ref, first_row, rows, total_rows, cols):
    wide = jnp.broadcast_to(answer, (48, LW))
    lift = lambda i: jnp.broadcast_to(wide[i : i + 1, :], (8, LW))
    blocks = cols // LW
    const = lift(ONE_PLANE)
    for g in range(rows // 8):
        y = (2.0 / total_rows) * (first_row + 8 * g + iota((8, LW), 0)).astype(F32) - 1.0
        level = [lift(b) + y * lift(32 + b) for b in range(NB)]
        slope = [lift(16 + b) for b in range(NB)]

        def body(k, carry):
            flat = const
            tilt = jnp.zeros((8, LW), F32)
            for b in range(NB):
                r = resp_ref[b, k, 8 * g : 8 * g + 8, :]
                flat = flat + level[b] * r
                tilt = tilt + slope[b] * r
            at = pl.multiple_of(k * LW, LW)
            x = (k * LW + iota((8, LW), 1)).astype(F32) * (2.0 / cols) - 1.0
            out_ref[0, 8 * g : 8 * g + 8, pl.ds(at, LW)] = resp_ref[SCI_PLANE, k, 8 * g : 8 * g + 8, :] - (flat + x * tilt)
            return carry

        lax.fori_loop(0, blocks, body, 0, unroll=4)


def kernel(
    dets, strips,
    sci_ref, tmpl_ref, row_ref, col_ref, srow_ref, scol_ref,
    out_ref, coef_ref,
    frame, pad, row_table, col_table, win_hi, win_lo, resp, left, right, parts, sci_buf,
    main_send, main_recv, up_send, up_recv, down_send, down_recv, part_send, part_recv, own_sem, sci_sem,
):
    _, rows, cols = sci_ref.shape
    width = tmpl_ref.shape[2]
    total_rows = rows * strips
    det, strip = lax.axis_index("det"), lax.axis_index("strip")
    above, below = strip > 0, strip < strips - 1
    first_row = strip * rows

    def main_copy(i):
        target = lax.rem(det + i, dets)
        return pltpu.make_async_remote_copy(
            tmpl_ref.at[target], frame.at[pl.ds(HALO, rows), pl.ds(pl.multiple_of(det * width, width), width)],
            main_send.at[i], main_recv.at[i], device_id=(target, strip), device_id_type=MESH,
        )

    here = pl.ds(pl.multiple_of(det * width, width), width)
    ups = ((0, 8), (8, KH - 8))
    downs = ((rows - 8, 8), (rows - KH, KH - 8))

    def up_copy(i, p):
        target = lax.rem(det + i, dets)
        at, size = ups[p]
        return pltpu.make_async_remote_copy(
            tmpl_ref.at[target, pl.ds(at, size), :], frame.at[pl.ds(HALO + rows + at, size), here],
            up_send.at[p, i], up_recv.at[p, i], device_id=(target, strip - 1), device_id_type=MESH,
        )

    def down_copy(i, p):
        target = lax.rem(det + i, dets)
        at, size = downs[p]
        return pltpu.make_async_remote_copy(
            tmpl_ref.at[target, pl.ds(at, size), :], frame.at[pl.ds(HALO - rows + at, size), here],
            down_send.at[p, i], down_recv.at[p, i], device_id=(target, strip + 1), device_id_type=MESH,
        )

    own = pltpu.make_async_copy(
        tmpl_ref.at[det], frame.at[pl.ds(HALO, rows), pl.ds(pl.multiple_of(det * width, width), width)], own_sem
    )
    own.start()
    sci_copy = pltpu.make_async_copy(sci_ref.at[0], sci_buf, sci_sem)
    sci_copy.start()
    for i in range(dets):
        if i:
            main_copy(i).start()

        @pl.when(above)
        def _():
            up_copy(i, 0).start()
            up_copy(i, 1).start()

        @pl.when(below)
        def _():
            down_copy(i, 0).start()
            down_copy(i, 1).start()

    build_row_table(row_ref, pad, row_table, rows)
    build_col_tables(col_ref, pad, col_table)
    blocks = cols // LW
    sci_copy.wait()
    for k in range(blocks):
        resp[SCI_PLANE, k] = sci_buf[:, k * LW : (k + 1) * LW]
    resp[ONE_PLANE] = jnp.ones((blocks + 1, rows, LW), F32)
    resp[:ONE_PLANE, blocks] = jnp.zeros((NB, rows, LW), F32)
    resp[SCI_PLANE, blocks] = jnp.zeros((rows, LW), F32)

    own.wait()
    for i in range(dets):
        if i:
            main_copy(i).wait()

        @pl.when(above)
        def _():
            for p in range(2):
                up_copy(i, p).wait_send()
                down_copy(i, p).wait_recv()

        @pl.when(below)
        def _():
            for p in range(2):
                down_copy(i, p).wait_send()
                up_copy(i, p).wait_recv()

    for chunk in range(cols // 256 + 1):
        row_stage(frame, row_table, win_hi, win_lo, chunk, first_row, rows, cols, total_rows)
    col_stage(win_hi, win_lo, col_table, resp, rows, cols)
    pack_stamps(resp, srow_ref, scol_ref, left, right, first_row, rows, cols, srow_ref.shape[1])
    parts[strip] = normal_part(left, right, first_row, rows, total_rows)

    def part_copy(i):
        return pltpu.make_async_remote_copy(
            parts.at[strip], parts.at[strip], part_send.at[i], part_recv.at[i],
            device_id=(det, lax.rem(strip + i, strips)), device_id_type=MESH,
        )

    for i in range(1, strips):
        part_copy(i).start()
    for i in range(1, strips):
        source = lax.rem(strip + strips - i, strips)
        part_copy(i).wait_send()
        pltpu.make_async_remote_copy(
            parts.at[source], parts.at[source], part_send.at[i], part_recv.at[i],
            device_id=(det, source), device_id_type=MESH,
        ).wait_recv()
    normal = parts[0]
    for i in range(1, strips):
        normal = normal + parts[i]
    answer = solve(normal)
    coef_ref[...] = coeff_row(answer)[:, :NU]
    apply_model(answer, resp, out_ref, first_row, rows, total_rows, cols)


def local(dets, strips, science, template, row_taps, col_taps, stamp_rows, stamp_cols):
    _, rows, cols = science.shape
    blocks = cols // LW
    stamps = stamp_rows.shape[1]
    packed = (stamps + 2) // 3 * LW
    any_space = pl.BlockSpec(memory_space=pl.ANY)
    vmem = pl.BlockSpec(memory_space=pltpu.VMEM)
    smem = pl.BlockSpec(memory_space=pltpu.SMEM)
    dma = pltpu.SemaphoreType.DMA
    return pl.pallas_call(
        functools.partial(kernel, dets, strips),
        out_shape=(jax.ShapeDtypeStruct(science.shape, F32), jax.ShapeDtypeStruct((1, NU), F32)),
        in_specs=[any_space, any_space, vmem, vmem, smem, smem],
        out_specs=(vmem, vmem),
        scratch_shapes=[
            pltpu.VMEM((rows + 2 * HALO, cols), F32),
            pltpu.VMEM((16, LW), F32),
            pltpu.VMEM((NB * rows, 256), BF),
            pltpu.VMEM((NB, 256, 256), BF),
            pltpu.VMEM((NB, blocks, rows, 256), BF),
            pltpu.VMEM((NB, blocks, rows, 256), BF),
            pltpu.VMEM((SCI_PLANE + 1, blocks + 1, rows, LW), F32),
            pltpu.VMEM((rows // 8, 6 * PLANES * 8, packed), BF),
            pltpu.VMEM((rows // 8, 2 * PLANES * 8, packed), BF),
            pltpu.VMEM((strips, 48, LW), F32),
            pltpu.VMEM((rows, cols), F32),
            dma((dets,)), dma((dets,)), dma((2, dets)), dma((2, dets)), dma((2, dets)), dma((2, dets)),
            dma((strips,)), dma((strips,)), dma, dma,
        ],
        compiler_params=pltpu.CompilerParams(
            has_side_effects=True, vmem_limit_bytes=56 * 1024 * 1024
        ),
    )(science, template, row_taps, col_taps, stamp_rows, stamp_cols)


def solution(mesh):
    return jax.shard_map(
        functools.partial(local, mesh.shape["det"], mesh.shape["strip"]),
        mesh=mesh,
        in_specs=(
            P("det", "strip", None),
            P(None, "strip", "det"),
            P(),
            P(),
            P("det", None),
            P("det", None),
        ),
        out_specs=(P("det", "strip", None), P("det", None)),
        check_vma=False,
    )
```

```python
import functools

import jax
import jax.numpy as jnp
from jax import lax
from jax.experimental import pallas as pl
from jax.experimental.pallas import tpu as pltpu
from jax.sharding import PartitionSpec as P

NB = 12
KS = 21
HS = 17
KH = 10
NU = 37
LW = 128
HALO = 16
SLOT = 64
PLANES = 16
ONE_PLANE = 12
SCI_PLANE = 13
RIDGE_WEIGHT = 1.0
HIGHEST_MODE = lax.Precision.HIGHEST
MESH = pl.DeviceIdType.MESH
BF = jnp.bfloat16
F32 = jnp.float32


def iota(shape, dim):
    return lax.broadcasted_iota(jnp.int32, shape, dim)


def split(value):
    high = value.astype(BF)
    return high, (value - high.astype(F32)).astype(BF)


def build_row_table(taps_ref, pad_ref, table_ref, rows):
    pad_ref[...] = jnp.zeros_like(pad_ref)
    pad_ref[:NB, :KS] = taps_ref[...]
    for b in range(NB):
        wide = jnp.broadcast_to(pad_ref[b : b + 1, :], (rows, LW))
        moved = pltpu.roll(wide, HALO - KH, 1, stride=1, stride_axis=0)
        high, low = split(moved)
        high, low = high.astype(F32), low.astype(F32)
        high = high + pltpu.roll(high, 64, 1)
        low = low + pltpu.roll(low, 64, 1)
        table_ref[b * rows : (b + 1) * rows, :LW] = high.astype(BF)
        table_ref[b * rows : (b + 1) * rows, LW:] = low.astype(BF)


def build_col_tables(taps_ref, pad_ref, table_ref, stamp_table_ref):
    pad_ref[...] = jnp.zeros_like(pad_ref)
    pad_ref[:NB, :KS] = taps_ref[...]
    lane, sub = iota((LW, LW), 1), iota((LW, LW), 0)
    same_slot = lane // SLOT == sub // SLOT
    for b in range(NB):
        wide = jnp.broadcast_to(pad_ref[b : b + 1, :], (LW, LW))
        moved = pltpu.roll(wide, 0, 1, stride=1, stride_axis=0)
        near = jnp.where(lane >= sub, moved, 0.0).T
        far = jnp.where(lane < sub, moved, 0.0).T
        for part, at in ((near, 0), (far, LW)):
            high, low = split(part)
            table_ref[b, at : at + LW, :LW] = high
            table_ref[b, at : at + LW, LW:] = low
        high, low = split(jnp.where(same_slot, near, 0.0))
        for at in (0, LW):
            stamp_table_ref[b, at : at + LW, :LW] = high
            stamp_table_ref[b, at : at + LW, LW:] = low


def row_filtered(row_table_ref, moved, rows):
    high, low = split(moved)
    stacked = jnp.concatenate([high, low, high, low], axis=0)
    size = NB // 2
    for base in (0, size):
        out = jnp.dot(row_table_ref[base * rows : (base + size) * rows, :], stacked, preferred_element_type=F32)
        yield base, [v.reshape(size, rows, moved.shape[1]) for v in split(out)]


def held_rows(width, first_row, rows, total_rows):
    sub = iota((2 * HALO + rows, width), 0)
    sky = first_row - HALO + sub
    return (sub >= HALO - KH) & (sub < HALO + rows + KH) & (sky >= 0) & (sky < total_rows)


def row_stage(sky_ref, row_table_ref, windows, first, count, rows):
    size = NB // 2
    lane = iota((2 * HALO + rows, LW), 1)
    loaded = [pltpu.roll(sky_ref[first + i], KH, 1) for i in range(count + 1)]
    moved = [jnp.where(lane < KH, loaded[i], loaded[i + 1]) for i in range(count)]
    moved = jnp.concatenate(moved, axis=1) if count > 1 else moved[0]
    for base, pair in row_filtered(row_table_ref, moved, rows):
        for ref, val in zip(windows, pair):
            for i in range(count):
                part = val[:, :, i * LW : (i + 1) * LW]
                ref[base : base + size, first + i + 1, :, :LW] = part
                ref[base : base + size, first + i, :, LW:] = part


def col_stage(windows, col_table_ref, resp_ref, rows, cols):
    blocks = cols // LW
    per = 8

    def body(b, carry):
        table = col_table_ref[b]
        for k in range(0, blocks, per):
            hi, lo = [ref[b, k + 1 : k + 1 + per].reshape(per * rows, 2 * LW) for ref in windows]
            out = jnp.dot(hi, table, preferred_element_type=F32) + jnp.dot(lo, table, preferred_element_type=F32)
            resp_ref[b, k : k + per] = (out[:, :LW] + out[:, LW:]).reshape(per, rows, LW)
        return carry

    lax.fori_loop(0, NB, body, 0)


def gather(ref, starts):
    picked = []
    for t, start in enumerate(starts):
        k = start // LW
        off = start - k * LW
        near, far = ref[k], ref[k + 1]
        both = jnp.where(iota(near.shape, 1) >= off, near, far)
        picked.append(pltpu.roll(both, lax.rem(SLOT * t - off + LW, LW), 1))
    return jnp.where(iota(picked[0].shape, 1) < SLOT, *picked)


def stamp_left(cols_ref, s, cols):
    return jnp.clip(cols_ref[0, s] - HS, 0, cols - 1)


def stamp_responses(sky_ref, row_table_ref, stamp_table_ref, win_ref, resp_ref, cols_ref, rows, cols):
    pairs = resp_ref.shape[1]
    size = NB // 2

    def body(u, carry):
        lefts = [stamp_left(cols_ref, 4 * u + t, cols) + (LW - KH) for t in range(4)]
        moved = jnp.concatenate([gather(sky_ref, lefts[:2]), gather(sky_ref, lefts[2:])], axis=1)
        for base, pair in row_filtered(row_table_ref, moved, rows):
            for part, val in enumerate(pair):
                for i in range(2):
                    win_ref[base : base + size, 2 * u + i, :, part * LW : (part + 1) * LW] = val[:, :, i * LW : (i + 1) * LW]
        return carry

    lax.fori_loop(0, pairs // 2, body, 0)

    def filt(b, carry):
        out = jnp.dot(win_ref[b].reshape(pairs * rows, 2 * LW), stamp_table_ref[b], preferred_element_type=F32)
        resp_ref[b] = (out[:, :LW] + out[:, LW:]).reshape(pairs, rows, LW)
        return carry

    lax.fori_loop(0, NB, filt, 0)


def pack_stamps(resp_ref, sci_ref, rows_ref, cols_ref, left_ref, right_ref, first_row, rows, cols):
    groups = rows // 8
    lane = iota((8, LW), 1)

    def body(q, carry):
        lefts = [stamp_left(cols_ref, 2 * q + t, cols) for t in range(2)]
        second = lane >= SLOT
        inside = lane - jnp.where(second, SLOT, 0)
        rowv = jnp.where(second, rows_ref[0, 2 * q + 1], rows_ref[0, 2 * q])
        xv = (jnp.where(second, lefts[1], lefts[0]) + inside).astype(F32) * (2.0 / cols) - 1.0
        sci = gather(sci_ref, lefts)
        at = pl.multiple_of(q * LW, LW)
        ones, zeros = jnp.ones((1, 8, LW), F32), jnp.zeros((PLANES - SCI_PLANE - 1, 8, LW), F32)
        for g in range(groups):
            near = slice(8 * g, 8 * g + 8)
            yv = first_row + 8 * g + iota((8, LW), 0)
            hit = ((jnp.abs(yv - rowv) <= HS) & (inside < 2 * HS + 1)).astype(F32)
            planes = jnp.concatenate([resp_ref[:, q, near, :], ones, sci[None, near, :], zeros], axis=0)
            high, low = split(planes.reshape(PLANES * 8, LW))
            right_ref[g, : PLANES * 8, pl.ds(at, LW)] = high
            right_ref[g, PLANES * 8 :, pl.ds(at, LW)] = low
            moment = planes * hit[None]
            for m in range(3):
                if m:
                    moment = moment * xv[None]
                high, low = split(moment.reshape(PLANES * 8, LW))
                left_ref[g, m * PLANES * 8 : (m + 1) * PLANES * 8, pl.ds(at, LW)] = high
                left_ref[g, (m + 3) * PLANES * 8 : (m + 4) * PLANES * 8, pl.ds(at, LW)] = low
        return carry

    lax.fori_loop(0, resp_ref.shape[1], body, 0)


def build_maps(maps_ref, first_row, rows, total_rows):
    span = PLANES * 8
    plane, col = iota((span, LW), 0) // 8, iota((span, LW), 1)
    kind, base = col // 16, lax.rem(col, 16)
    match = plane == base
    real = match & (plane < NB)
    zero = jnp.zeros((span, LW), F32)
    plain = jnp.where(match & (kind == 0), 1.0, zero)
    in_x = jnp.where(real & (kind == 1), 1.0, zero)
    for g in range(rows // 8):
        y = (2.0 / total_rows) * (first_row + 8 * g + lax.rem(iota((span, LW), 0), 8)).astype(F32) - 1.0
        level = plain + jnp.where(real & (kind == 2), y, zero)
        for i, part in enumerate((level, in_x, level * y, in_x * y)):
            maps_ref[g * span : (g + 1) * span, i * LW : (i + 1) * LW] = part


def normal_part(left_ref, right_ref, maps_ref, rows):
    span = PLANES * 8
    same_y = (lax.rem(iota((8, span), 1), 8) == iota((8, span), 0)).astype(F32)
    picked = []
    for g in range(rows // 8):
        out = lax.dot_general(left_ref[g], right_ref[g], (((1,), (1,)), ((), ())), preferred_element_type=F32)
        folded = out[: 3 * span, :span] + out[: 3 * span, span:] + out[3 * span :, :span]
        picked.append(jnp.sum(folded.reshape(3 * PLANES, 8, span) * same_y[None], axis=1))
    total = jnp.dot(
        jnp.concatenate(picked, axis=1), maps_ref[...], precision=HIGHEST_MODE, preferred_element_type=F32
    )
    return jnp.concatenate(
        [
            total[0:16, 0:LW] + total[16:32, LW : 2 * LW],
            total[16:32, 0:LW] + total[32:48, LW : 2 * LW],
            total[0:16, 2 * LW : 3 * LW] + total[16:32, 3 * LW :],
        ],
        axis=0,
    )


PIVOTS = [*range(0, 13), *range(16, 28), *range(32, 44)]


def solve(normal):
    sub, lane = iota((48, LW), 0), iota((48, LW), 1)
    live = (lax.rem(sub, 16) < NB) | (sub == ONE_PLANE)
    mat = jnp.where((sub == lane) & live, normal + RIDGE_WEIGHT, normal)
    at = lambda value, k: value[k : k + 1, :]
    for i in range(0, NU - 1, 2):
        j, k = PIVOTS[i], PIVOTS[i + 1]
        cj = jnp.broadcast_to(mat[:, j : j + 1], (48, LW))
        ck = jnp.broadcast_to(mat[:, k : k + 1], (48, LW))
        jj, jk, kj, kk = at(cj, j), at(ck, j), at(cj, k), at(ck, k)
        scale = 1.0 / (jj * kk - jk * kj)
        rj, rk = at(mat, j), at(mat, k)
        nj = (kk * rj - jk * rk) * scale
        nk = (jj * rk - kj * rj) * scale
        mat = jnp.where(sub == j, nj, jnp.where(sub == k, nk, mat - cj * nj - ck * nk))
    k = PIVOTS[-1]
    column = jnp.broadcast_to(mat[:, k : k + 1], (48, LW))
    row = at(mat, k) / at(column, k)
    mat = jnp.where(sub == k, row, mat - column * row)
    return mat[:, SCI_PLANE : SCI_PLANE + 1]


def coeff_row(answer):
    sub, lane = iota((48, LW), 0), iota((48, LW), 1)
    kind, base = sub // 16, lax.rem(sub, 16)
    goes = jnp.where(base < NB, kind * NB + base, jnp.where(sub == ONE_PLANE, NU - 1, -1))
    return jnp.sum(jnp.where(goes == lane, answer, 0.0), axis=0, keepdims=True)


def apply_model(answer, resp_ref, sci_ref, out_ref, first_row, rows, total_rows, cols):
    wide = jnp.broadcast_to(answer, (48, LW))
    lift = lambda i: jnp.broadcast_to(wide[i : i + 1, :], (8, LW))
    blocks = cols // LW
    const = lift(ONE_PLANE)
    for g in range(rows // 8):
        y = (2.0 / total_rows) * (first_row + 8 * g + iota((8, LW), 0)).astype(F32) - 1.0
        level = [lift(b) + y * lift(32 + b) for b in range(NB)]
        slope = [lift(16 + b) for b in range(NB)]

        def body(k, carry):
            flat = const
            tilt = jnp.zeros((8, LW), F32)
            for b in range(NB):
                r = resp_ref[b, k, 8 * g : 8 * g + 8, :]
                flat = flat + level[b] * r
                tilt = tilt + slope[b] * r
            at = pl.multiple_of(k * LW, LW)
            x = (k * LW + iota((8, LW), 1)).astype(F32) * (2.0 / cols) - 1.0
            out_ref[0, 8 * g : 8 * g + 8, pl.ds(at, LW)] = sci_ref[k, 8 * g : 8 * g + 8, :] - (flat + x * tilt)
            return carry

        lax.fori_loop(0, blocks, body, 0, unroll=4)


def kernel(
    dets, strips,
    sci_ref, tmpl_ref, row_ref, col_ref, srow_ref, scol_ref,
    out_ref, coef_ref,
    frame, pad, row_table, col_table, stamp_table, win_hi, win_lo, resp, stamp_win, stamp_resp, left, right, maps, parts, sci_buf, sky, sci,
    main_send, main_recv, up_send, up_recv, down_send, down_recv, part_send, part_recv, own_sem, sci_sem,
):
    _, rows, cols = sci_ref.shape
    width = tmpl_ref.shape[2]
    total_rows = rows * strips
    det, strip = lax.axis_index("det"), lax.axis_index("strip")
    above, below = strip > 0, strip < strips - 1
    first_row = strip * rows

    barrier = pltpu.get_barrier_semaphore()

    def greet(target_det, target_strip):
        pl.semaphore_signal(barrier, inc=1, device_id=(target_det, target_strip), device_id_type=MESH)

    for i in range(1, dets):
        greet(lax.rem(det + i, dets), strip)

    @pl.when(above)
    def _():
        for i in range(dets):
            greet(lax.rem(det + i, dets), strip - 1)

    @pl.when(below)
    def _():
        for i in range(dets):
            greet(lax.rem(det + i, dets), strip + 1)

    for i in range(2, strips - 1):
        other = lax.rem(strip + i, strips)

        @pl.when((other != strip - 1) & (other != strip + 1))
        def _():
            greet(det, other)

    @pl.when(strip == 0)
    def _():
        greet(det, strips - 1)

    @pl.when(strip == strips - 1)
    def _():
        greet(det, 0)

    ends = jnp.where(above & below, 0, 1)
    count = (dets - 1) + dets * (2 - ends) + (strips - 3 + ends)
    pl.semaphore_wait(barrier, count)

    here = pl.ds(pl.multiple_of(det * width, width), width)

    def main_copy(i):
        target = lax.rem(det + dets - i, dets)
        return pltpu.make_async_remote_copy(
            tmpl_ref.at[target], frame.at[pl.ds(HALO, rows), here],
            main_send.at[i], main_recv.at[i], device_id=(target, strip), device_id_type=MESH,
        )

    ups = ((0, 8), (8, KH - 8))
    downs = ((rows - 8, 8), (rows - KH, KH - 8))

    def up_copy(i, p):
        target = lax.rem(det + dets - i, dets)
        at, size = ups[p]
        return pltpu.make_async_remote_copy(
            tmpl_ref.at[target, pl.ds(at, size), :], frame.at[pl.ds(HALO + rows + at, size), here],
            up_send.at[p, i], up_recv.at[p, i], device_id=(target, strip - 1), device_id_type=MESH,
        )

    def down_copy(i, p):
        target = lax.rem(det + dets - i, dets)
        at, size = downs[p]
        return pltpu.make_async_remote_copy(
            tmpl_ref.at[target, pl.ds(at, size), :], frame.at[pl.ds(HALO - rows + at, size), here],
            down_send.at[p, i], down_recv.at[p, i], device_id=(target, strip + 1), device_id_type=MESH,
        )

    own = pltpu.make_async_copy(
        tmpl_ref.at[det], frame.at[pl.ds(HALO, rows), here], own_sem
    )
    own.start()
    sci_copy = pltpu.make_async_copy(sci_ref.at[0], sci_buf, sci_sem)
    sci_copy.start()
    for i in range(dets):
        if i:
            main_copy(i).start()

        @pl.when(above)
        def _():
            up_copy(i, 0).start()
            up_copy(i, 1).start()

        @pl.when(below)
        def _():
            down_copy(i, 0).start()
            down_copy(i, 1).start()

    blocks = cols // LW
    sky[0] = jnp.zeros((2 * HALO + rows, LW), F32)
    sky[blocks + 1] = jnp.zeros((2 * HALO + rows, LW), F32)
    sci[blocks] = jnp.zeros((rows, LW), F32)
    build_row_table(row_ref, pad, row_table, rows)
    build_col_tables(col_ref, pad, col_table, stamp_table)
    build_maps(maps, first_row, rows, total_rows)
    sci_copy.wait()
    for k in range(blocks):
        sci[k] = sci_buf[:, k * LW : (k + 1) * LW]
    own.wait()
    for i in range(dets):
        if i:
            main_copy(i).wait_recv()

        @pl.when(above)
        def _():
            for p in range(2):
                down_copy(i, p).wait_recv()

        @pl.when(below)
        def _():
            for p in range(2):
                up_copy(i, p).wait_recv()

    held = held_rows(LW, first_row, rows, total_rows)
    for k in range(blocks):
        sky[k + 1] = jnp.where(held, frame[:, k * LW : (k + 1) * LW], 0.0)
    stamp_responses(sky, row_table, stamp_table, stamp_win, stamp_resp, scol_ref, rows, cols)
    pack_stamps(stamp_resp, sci, srow_ref, scol_ref, left, right, first_row, rows, cols)
    parts[strip] = normal_part(left, right, maps, rows)

    def part_copy(i):
        return pltpu.make_async_remote_copy(
            parts.at[strip], parts.at[strip], part_send.at[i], part_recv.at[i],
            device_id=(det, lax.rem(strip + i, strips)), device_id_type=MESH,
        )

    for i in range(1, strips):
        part_copy(i).start()
    windows = (win_hi, win_lo)

    def chunk(j, carry):
        row_stage(sky, row_table, windows, 2 * j, 2, rows)
        return carry

    lax.fori_loop(0, blocks // 2, chunk, 0)
    row_stage(sky, row_table, windows, blocks, 1, rows)
    col_stage(windows, col_table, resp, rows, cols)
    for i in range(1, strips):
        source = lax.rem(strip + strips - i, strips)
        part_copy(i).wait_send()
        pltpu.make_async_remote_copy(
            parts.at[source], parts.at[source], part_send.at[i], part_recv.at[i],
            device_id=(det, source), device_id_type=MESH,
        ).wait_recv()
    for i in range(dets):
        if i:
            main_copy(i).wait_send()

        @pl.when(above)
        def _():
            for p in range(2):
                up_copy(i, p).wait_send()

        @pl.when(below)
        def _():
            for p in range(2):
                down_copy(i, p).wait_send()

    normal = parts[0]
    for i in range(1, strips):
        normal = normal + parts[i]
    answer = solve(normal)
    coef_ref[...] = coeff_row(answer)[:, :NU]
    apply_model(answer, resp, sci, out_ref, first_row, rows, total_rows, cols)


def local(dets, strips, science, template, row_taps, col_taps, stamp_rows, stamp_cols):
    _, rows, cols = science.shape
    blocks = cols // LW
    stamps = stamp_rows.shape[1]
    packed = stamps // 2 * LW
    any_space = pl.BlockSpec(memory_space=pl.ANY)
    vmem = pl.BlockSpec(memory_space=pltpu.VMEM)
    smem = pl.BlockSpec(memory_space=pltpu.SMEM)
    dma = pltpu.SemaphoreType.DMA
    return pl.pallas_call(
        functools.partial(kernel, dets, strips),
        out_shape=(jax.ShapeDtypeStruct(science.shape, F32), jax.ShapeDtypeStruct((1, NU), F32)),
        in_specs=[any_space, any_space, vmem, vmem, smem, smem],
        out_specs=(vmem, vmem),
        scratch_shapes=[
            pltpu.VMEM((rows + 2 * HALO, cols), F32),
            pltpu.VMEM((16, LW), F32),
            pltpu.VMEM((NB * rows, 256), BF),
            pltpu.VMEM((NB, 256, 256), BF),
            pltpu.VMEM((NB, 256, 256), BF),
            pltpu.VMEM((NB, blocks + 2, rows, 256), BF),
            pltpu.VMEM((NB, blocks + 2, rows, 256), BF),
            pltpu.VMEM((NB, blocks, rows, LW), F32),
            pltpu.VMEM((NB, stamps // 2, rows, 256), BF),
            pltpu.VMEM((NB, stamps // 2, rows, LW), F32),
            pltpu.VMEM((rows // 8, 6 * PLANES * 8, packed), BF),
            pltpu.VMEM((rows // 8, 2 * PLANES * 8, packed), BF),
            pltpu.VMEM((rows * PLANES, 4 * LW), F32),
            pltpu.VMEM((strips, 48, LW), F32),
            pltpu.VMEM((rows, cols), F32),
            pltpu.VMEM((blocks + 2, rows + 2 * HALO, LW), F32),
            pltpu.VMEM((blocks + 1, rows, LW), F32),
            dma((dets,)), dma((dets,)), dma((2, dets)), dma((2, dets)), dma((2, dets)), dma((2, dets)),
            dma((strips,)), dma((strips,)), dma, dma,
        ],
        compiler_params=pltpu.CompilerParams(
            collective_id=0, has_side_effects=True, vmem_limit_bytes=56 * 1024 * 1024
        ),
    )(science, template, row_taps, col_taps, stamp_rows, stamp_cols)


def solution(mesh):
    return jax.shard_map(
        functools.partial(local, mesh.shape["det"], mesh.shape["strip"]),
        mesh=mesh,
        in_specs=(
            P("det", "strip", None),
            P(None, "strip", "det"),
            P(),
            P(),
            P("det", None),
            P("det", None),
        ),
        out_specs=(P("det", "strip", None), P("det", None)),
        check_vma=False,
    )
```

```python
import functools

import jax
import jax.numpy as jnp
from jax import lax
from jax.experimental import pallas as pl
from jax.experimental.pallas import tpu as pltpu
from jax.sharding import PartitionSpec as P

NB = 12
KS = 21
HS = 17
KH = 10
NU = 37
LW = 128
HALO = 16
SLOT = 64
PLANES = 16
ONE_PLANE = 12
SCI_PLANE = 13
RIDGE_WEIGHT = 1.0
HIGHEST_MODE = lax.Precision.HIGHEST
MESH = pl.DeviceIdType.MESH
BF = jnp.bfloat16
F32 = jnp.float32


def iota(shape, dim):
    return lax.broadcasted_iota(jnp.int32, shape, dim)


def split(value):
    high = value.astype(BF)
    return high, (value - high.astype(F32)).astype(BF)


def build_row_table(taps_ref, pad_ref, table_ref, rows):
    pad_ref[...] = jnp.zeros_like(pad_ref)
    pad_ref[:NB, :KS] = taps_ref[...]
    for b in range(NB):
        wide = jnp.broadcast_to(pad_ref[b : b + 1, :], (rows, LW))
        moved = pltpu.roll(wide, HALO - KH, 1, stride=1, stride_axis=0)
        high, low = split(moved)
        high, low = high.astype(F32), low.astype(F32)
        high = high + pltpu.roll(high, 64, 1)
        low = low + pltpu.roll(low, 64, 1)
        table_ref[b * rows : (b + 1) * rows, :LW] = high.astype(BF)
        table_ref[b * rows : (b + 1) * rows, LW:] = low.astype(BF)


def build_col_tables(taps_ref, pad_ref, table_ref, stamp_table_ref):
    pad_ref[...] = jnp.zeros_like(pad_ref)
    pad_ref[:NB, :KS] = taps_ref[...]
    lane, sub = iota((LW, LW), 1), iota((LW, LW), 0)
    same_slot = lane // SLOT == sub // SLOT
    for b in range(NB):
        wide = jnp.broadcast_to(pad_ref[b : b + 1, :], (LW, LW))
        moved = pltpu.roll(wide, 0, 1, stride=1, stride_axis=0)
        near = jnp.where(lane >= sub, moved, 0.0).T
        far = jnp.where(lane < sub, moved, 0.0).T
        for part, at in ((near, 0), (far, LW)):
            high, low = split(part)
            table_ref[b, at : at + LW, :LW] = high
            table_ref[b, at : at + LW, LW:] = low
        high, low = split(jnp.where(same_slot, near, 0.0))
        for at in (0, LW):
            stamp_table_ref[b, at : at + LW, :LW] = high
            stamp_table_ref[b, at : at + LW, LW:] = low


def row_filtered(row_table_ref, moved, rows):
    high, low = split(moved)
    stacked = jnp.concatenate([high, low, high, low], axis=0)
    size = NB // 2
    for base in (0, size):
        out = jnp.dot(row_table_ref[base * rows : (base + size) * rows, :], stacked, preferred_element_type=F32)
        yield base, [v.reshape(size, rows, moved.shape[1]) for v in split(out)]


def held_rows(width, first_row, rows, total_rows):
    sub = iota((2 * HALO + rows, width), 0)
    sky = first_row - HALO + sub
    return (sub >= HALO - KH) & (sub < HALO + rows + KH) & (sky >= 0) & (sky < total_rows)


def row_stage(sky_ref, row_table_ref, windows, places, rows):
    size = NB // 2
    lane = iota((2 * HALO + rows, LW), 1)
    moved = [pltpu.roll(jnp.where(lane < LW - KH, sky_ref[m + 1], sky_ref[m]), KH, 1) for m in places]
    moved = jnp.concatenate(moved, axis=1) if len(places) > 1 else moved[0]
    for base, pair in row_filtered(row_table_ref, moved, rows):
        for ref, val in zip(windows, pair):
            for i, m in enumerate(places):
                part = val[:, :, i * LW : (i + 1) * LW]
                ref[base : base + size, m + 1, :, :LW] = part
                ref[base : base + size, m, :, LW:] = part


def col_stage(windows, col_table_ref, resp_ref, rows, cols):
    blocks = cols // LW
    per = 8

    def body(b, carry):
        table = col_table_ref[b]
        for k in range(0, blocks, per):
            hi, lo = [ref[b, k + 1 : k + 1 + per].reshape(per * rows, 2 * LW) for ref in windows]
            out = jnp.dot(hi, table, preferred_element_type=F32) + jnp.dot(lo, table, preferred_element_type=F32)
            resp_ref[b, k : k + per] = (out[:, :LW] + out[:, LW:]).reshape(per, rows, LW)
        return carry

    lax.fori_loop(0, NB, body, 0)


def gather(ref, starts):
    picked = []
    for t, start in enumerate(starts):
        k = start // LW
        off = start - k * LW
        near, far = ref[k], ref[k + 1]
        both = jnp.where(iota(near.shape, 1) >= off, near, far)
        picked.append(pltpu.roll(both, lax.rem(SLOT * t - off + LW, LW), 1))
    return jnp.where(iota(picked[0].shape, 1) < SLOT, *picked)


def stamp_left(cols_ref, s, cols):
    return jnp.clip(cols_ref[0, s] - HS, 0, cols - 1)


def stamp_responses(sky_ref, row_table_ref, stamp_table_ref, win_ref, resp_ref, cols_ref, rows, cols):
    pairs = resp_ref.shape[1]
    size = NB // 2

    def body(u, carry):
        lefts = [stamp_left(cols_ref, 4 * u + t, cols) + (LW - KH) for t in range(4)]
        moved = jnp.concatenate([gather(sky_ref, lefts[:2]), gather(sky_ref, lefts[2:])], axis=1)
        for base, pair in row_filtered(row_table_ref, moved, rows):
            for part, val in enumerate(pair):
                for i in range(2):
                    win_ref[base : base + size, 2 * u + i, :, part * LW : (part + 1) * LW] = val[:, :, i * LW : (i + 1) * LW]
        return carry

    lax.fori_loop(0, pairs // 2, body, 0)

    def filt(b, carry):
        out = jnp.dot(win_ref[b].reshape(pairs * rows, 2 * LW), stamp_table_ref[b], preferred_element_type=F32)
        resp_ref[b] = (out[:, :LW] + out[:, LW:]).reshape(pairs, rows, LW)
        return carry

    lax.fori_loop(0, NB, filt, 0)


def pack_stamps(resp_ref, sci_ref, rows_ref, cols_ref, left_ref, right_ref, first_row, rows, cols):
    groups = rows // 8
    lane = iota((8, LW), 1)

    def body(q, carry):
        lefts = [stamp_left(cols_ref, 2 * q + t, cols) for t in range(2)]
        second = lane >= SLOT
        inside = lane - jnp.where(second, SLOT, 0)
        rowv = jnp.where(second, rows_ref[0, 2 * q + 1], rows_ref[0, 2 * q])
        xv = (jnp.where(second, lefts[1], lefts[0]) + inside).astype(F32) * (2.0 / cols) - 1.0
        sci = gather(sci_ref, lefts)
        at = pl.multiple_of(q * LW, LW)
        ones, zeros = jnp.ones((1, 8, LW), F32), jnp.zeros((PLANES - SCI_PLANE - 1, 8, LW), F32)
        for g in range(groups):
            near = slice(8 * g, 8 * g + 8)
            yv = first_row + 8 * g + iota((8, LW), 0)
            hit = ((jnp.abs(yv - rowv) <= HS) & (inside < 2 * HS + 1)).astype(F32)
            planes = jnp.concatenate([resp_ref[:, q, near, :], ones, sci[None, near, :], zeros], axis=0)
            high, low = split(planes.reshape(PLANES * 8, LW))
            right_ref[g, : PLANES * 8, pl.ds(at, LW)] = high
            right_ref[g, PLANES * 8 :, pl.ds(at, LW)] = low
            moment = planes * hit[None]
            for m in range(3):
                if m:
                    moment = moment * xv[None]
                high, low = split(moment.reshape(PLANES * 8, LW))
                left_ref[g, m * PLANES * 8 : (m + 1) * PLANES * 8, pl.ds(at, LW)] = high
                left_ref[g, (m + 3) * PLANES * 8 : (m + 4) * PLANES * 8, pl.ds(at, LW)] = low
        return carry

    lax.fori_loop(0, resp_ref.shape[1], body, 0)


def build_maps(maps_ref, first_row, rows, total_rows):
    span = PLANES * 8
    plane, col = iota((span, LW), 0) // 8, iota((span, LW), 1)
    kind, base = col // 16, lax.rem(col, 16)
    match = plane == base
    real = match & (plane < NB)
    zero = jnp.zeros((span, LW), F32)
    plain = jnp.where(match & (kind == 0), 1.0, zero)
    in_x = jnp.where(real & (kind == 1), 1.0, zero)
    for g in range(rows // 8):
        y = (2.0 / total_rows) * (first_row + 8 * g + lax.rem(iota((span, LW), 0), 8)).astype(F32) - 1.0
        level = plain + jnp.where(real & (kind == 2), y, zero)
        for i, part in enumerate((level, in_x, level * y, in_x * y)):
            maps_ref[g * span : (g + 1) * span, i * LW : (i + 1) * LW] = part


def normal_part(left_ref, right_ref, maps_ref, rows):
    span = PLANES * 8
    same_y = (lax.rem(iota((8, span), 1), 8) == iota((8, span), 0)).astype(F32)
    picked = []
    for g in range(rows // 8):
        out = lax.dot_general(left_ref[g], right_ref[g], (((1,), (1,)), ((), ())), preferred_element_type=F32)
        folded = out[: 3 * span, :span] + out[: 3 * span, span:] + out[3 * span :, :span]
        picked.append(jnp.sum(folded.reshape(3 * PLANES, 8, span) * same_y[None], axis=1))
    total = jnp.dot(
        jnp.concatenate(picked, axis=1), maps_ref[...], precision=HIGHEST_MODE, preferred_element_type=F32
    )
    return jnp.concatenate(
        [
            total[0:16, 0:LW] + total[16:32, LW : 2 * LW],
            total[16:32, 0:LW] + total[32:48, LW : 2 * LW],
            total[0:16, 2 * LW : 3 * LW] + total[16:32, 3 * LW :],
        ],
        axis=0,
    )


PIVOTS = [*range(0, 13), *range(16, 28), *range(32, 44)]


def solve(normal):
    sub, lane = iota((48, LW), 0), iota((48, LW), 1)
    live = (lax.rem(sub, 16) < NB) | (sub == ONE_PLANE)
    mat = jnp.where((sub == lane) & live, normal + RIDGE_WEIGHT, normal)
    at = lambda value, k: value[k : k + 1, :]
    for i in range(0, NU - 1, 2):
        j, k = PIVOTS[i], PIVOTS[i + 1]
        cj = jnp.broadcast_to(mat[:, j : j + 1], (48, LW))
        ck = jnp.broadcast_to(mat[:, k : k + 1], (48, LW))
        jj, jk, kj, kk = at(cj, j), at(ck, j), at(cj, k), at(ck, k)
        scale = 1.0 / (jj * kk - jk * kj)
        rj, rk = at(mat, j), at(mat, k)
        nj = (kk * rj - jk * rk) * scale
        nk = (jj * rk - kj * rj) * scale
        mat = jnp.where(sub == j, nj, jnp.where(sub == k, nk, mat - cj * nj - ck * nk))
    k = PIVOTS[-1]
    column = jnp.broadcast_to(mat[:, k : k + 1], (48, LW))
    row = at(mat, k) / at(column, k)
    mat = jnp.where(sub == k, row, mat - column * row)
    return mat[:, SCI_PLANE : SCI_PLANE + 1]


def coeff_row(answer):
    sub, lane = iota((48, LW), 0), iota((48, LW), 1)
    kind, base = sub // 16, lax.rem(sub, 16)
    goes = jnp.where(base < NB, kind * NB + base, jnp.where(sub == ONE_PLANE, NU - 1, -1))
    return jnp.sum(jnp.where(goes == lane, answer, 0.0), axis=0, keepdims=True)


def apply_model(answer, resp_ref, sci_ref, out_ref, first_row, rows, total_rows, cols):
    wide = jnp.broadcast_to(answer, (48, LW))
    lift = lambda i: jnp.broadcast_to(wide[i : i + 1, :], (8, LW))
    blocks = cols // LW
    const = lift(ONE_PLANE)
    for g in range(rows // 8):
        y = (2.0 / total_rows) * (first_row + 8 * g + iota((8, LW), 0)).astype(F32) - 1.0
        level = [lift(b) + y * lift(32 + b) for b in range(NB)]
        slope = [lift(16 + b) for b in range(NB)]

        def body(k, carry):
            flat = const
            tilt = jnp.zeros((8, LW), F32)
            for b in range(NB):
                r = resp_ref[b, k, 8 * g : 8 * g + 8, :]
                flat = flat + level[b] * r
                tilt = tilt + slope[b] * r
            at = pl.multiple_of(k * LW, LW)
            x = (k * LW + iota((8, LW), 1)).astype(F32) * (2.0 / cols) - 1.0
            out_ref[0, 8 * g : 8 * g + 8, pl.ds(at, LW)] = sci_ref[k, 8 * g : 8 * g + 8, :] - (flat + x * tilt)
            return carry

        lax.fori_loop(0, blocks, body, 0, unroll=4)


def kernel(
    dets, strips,
    sci_ref, tmpl_ref, row_ref, col_ref, srow_ref, scol_ref,
    out_ref, coef_ref,
    frame, pad, row_table, col_table, stamp_table, win_hi, win_lo, resp, stamp_win, stamp_resp, left, right, maps, parts, sci_buf, sky, sci,
    main_send, main_recv, up_send, up_recv, down_send, down_recv, part_send, part_recv, own_sem, sci_sem,
):
    _, rows, cols = sci_ref.shape
    width = tmpl_ref.shape[2]
    total_rows = rows * strips
    det, strip = lax.axis_index("det"), lax.axis_index("strip")
    above, below = strip > 0, strip < strips - 1
    first_row = strip * rows

    barrier = pltpu.get_barrier_semaphore()

    def greet(target_det, target_strip):
        pl.semaphore_signal(barrier, inc=1, device_id=(target_det, target_strip), device_id_type=MESH)

    for i in range(1, dets):
        greet(lax.rem(det + i, dets), strip)

    @pl.when(above)
    def _():
        for i in range(dets):
            greet(lax.rem(det + i, dets), strip - 1)

    @pl.when(below)
    def _():
        for i in range(dets):
            greet(lax.rem(det + i, dets), strip + 1)

    for i in range(2, strips - 1):
        other = lax.rem(strip + i, strips)

        @pl.when((other != strip - 1) & (other != strip + 1))
        def _():
            greet(det, other)

    @pl.when(strip == 0)
    def _():
        greet(det, strips - 1)

    @pl.when(strip == strips - 1)
    def _():
        greet(det, 0)

    ends = jnp.where(above & below, 0, 1)
    count = (dets - 1) + dets * (2 - ends) + (strips - 3 + ends)
    pl.semaphore_wait(barrier, count)

    here = pl.ds(pl.multiple_of(det * width, width), width)

    def main_copy(i):
        target = lax.rem(det + dets - i, dets)
        return pltpu.make_async_remote_copy(
            tmpl_ref.at[target], frame.at[pl.ds(HALO, rows), here],
            main_send.at[i], main_recv.at[i], device_id=(target, strip), device_id_type=MESH,
        )

    ups = ((0, 8), (8, KH - 8))
    downs = ((rows - 8, 8), (rows - KH, KH - 8))

    def up_copy(i, p):
        target = lax.rem(det + dets - i, dets)
        at, size = ups[p]
        return pltpu.make_async_remote_copy(
            tmpl_ref.at[target, pl.ds(at, size), :], frame.at[pl.ds(HALO + rows + at, size), here],
            up_send.at[p, i], up_recv.at[p, i], device_id=(target, strip - 1), device_id_type=MESH,
        )

    def down_copy(i, p):
        target = lax.rem(det + dets - i, dets)
        at, size = downs[p]
        return pltpu.make_async_remote_copy(
            tmpl_ref.at[target, pl.ds(at, size), :], frame.at[pl.ds(HALO - rows + at, size), here],
            down_send.at[p, i], down_recv.at[p, i], device_id=(target, strip + 1), device_id_type=MESH,
        )

    own = pltpu.make_async_copy(
        tmpl_ref.at[det], frame.at[pl.ds(HALO, rows), here], own_sem
    )
    own.start()
    sci_copy = pltpu.make_async_copy(sci_ref.at[0], sci_buf, sci_sem)
    sci_copy.start()
    for i in range(dets):
        if i:
            main_copy(i).start()

        @pl.when(above)
        def _():
            up_copy(i, 0).start()
            up_copy(i, 1).start()

        @pl.when(below)
        def _():
            down_copy(i, 0).start()
            down_copy(i, 1).start()

    blocks = cols // LW
    sky[0] = jnp.zeros((2 * HALO + rows, LW), F32)
    sky[blocks + 1] = jnp.zeros((2 * HALO + rows, LW), F32)
    sci[blocks] = jnp.zeros((rows, LW), F32)
    build_row_table(row_ref, pad, row_table, rows)
    build_col_tables(col_ref, pad, col_table, stamp_table)
    build_maps(maps, first_row, rows, total_rows)
    sci_copy.wait()
    for k in range(blocks):
        sci[k] = sci_buf[:, k * LW : (k + 1) * LW]
    held = held_rows(LW, first_row, rows, total_rows)
    windows = (win_hi, win_lo)
    half = width // LW

    def received(i):
        @pl.when(above)
        def _():
            for p in range(2):
                down_copy(i, p).wait_recv()

        @pl.when(below)
        def _():
            for p in range(2):
                up_copy(i, p).wait_recv()

        first = half * lax.rem(det + i, dets)
        for t in range(half):
            sky[first + t + 1] = jnp.where(held, frame[:, pl.ds(pl.multiple_of((first + t) * LW, LW), LW)], 0.0)

    def place(n):
        return lax.rem(half * det + 1 + n, blocks + 1)

    def arrive(i, carry):
        main_copy(i).wait_recv()
        received(i)
        row_stage(sky, row_table, windows, [place(half * (i - 1) + t) for t in range(half)], rows)
        return carry

    own.wait()
    received(0)
    lax.fori_loop(1, dets - 1, arrive, 0)
    main_copy(dets - 1).wait_recv()
    received(dets - 1)
    stamp_responses(sky, row_table, stamp_table, stamp_win, stamp_resp, scol_ref, rows, cols)
    pack_stamps(stamp_resp, sci, srow_ref, scol_ref, left, right, first_row, rows, cols)
    parts[strip] = normal_part(left, right, maps, rows)

    def part_copy(i):
        return pltpu.make_async_remote_copy(
            parts.at[strip], parts.at[strip], part_send.at[i], part_recv.at[i],
            device_id=(det, lax.rem(strip + i, strips)), device_id_type=MESH,
        )

    for i in range(1, strips):
        part_copy(i).start()
    done = half * (dets - 2)
    row_stage(sky, row_table, windows, [place(done + t) for t in range(2)], rows)
    row_stage(sky, row_table, windows, [place(done + 2 + t) for t in range(2)], rows)
    row_stage(sky, row_table, windows, [place(blocks)], rows)
    col_stage(windows, col_table, resp, rows, cols)
    for i in range(1, strips):
        source = lax.rem(strip + strips - i, strips)
        part_copy(i).wait_send()
        pltpu.make_async_remote_copy(
            parts.at[source], parts.at[source], part_send.at[i], part_recv.at[i],
            device_id=(det, source), device_id_type=MESH,
        ).wait_recv()
    for i in range(dets):
        if i:
            main_copy(i).wait_send()

        @pl.when(above)
        def _():
            for p in range(2):
                up_copy(i, p).wait_send()

        @pl.when(below)
        def _():
            for p in range(2):
                down_copy(i, p).wait_send()

    normal = parts[0]
    for i in range(1, strips):
        normal = normal + parts[i]
    answer = solve(normal)
    coef_ref[...] = coeff_row(answer)[:, :NU]
    apply_model(answer, resp, sci, out_ref, first_row, rows, total_rows, cols)


def local(dets, strips, science, template, row_taps, col_taps, stamp_rows, stamp_cols):
    _, rows, cols = science.shape
    blocks = cols // LW
    stamps = stamp_rows.shape[1]
    packed = stamps // 2 * LW
    any_space = pl.BlockSpec(memory_space=pl.ANY)
    vmem = pl.BlockSpec(memory_space=pltpu.VMEM)
    smem = pl.BlockSpec(memory_space=pltpu.SMEM)
    dma = pltpu.SemaphoreType.DMA
    return pl.pallas_call(
        functools.partial(kernel, dets, strips),
        out_shape=(jax.ShapeDtypeStruct(science.shape, F32), jax.ShapeDtypeStruct((1, NU), F32)),
        in_specs=[any_space, any_space, vmem, vmem, smem, smem],
        out_specs=(vmem, vmem),
        scratch_shapes=[
            pltpu.VMEM((rows + 2 * HALO, cols), F32),
            pltpu.VMEM((16, LW), F32),
            pltpu.VMEM((NB * rows, 256), BF),
            pltpu.VMEM((NB, 256, 256), BF),
            pltpu.VMEM((NB, 256, 256), BF),
            pltpu.VMEM((NB, blocks + 2, rows, 256), BF),
            pltpu.VMEM((NB, blocks + 2, rows, 256), BF),
            pltpu.VMEM((NB, blocks, rows, LW), F32),
            pltpu.VMEM((NB, stamps // 2, rows, 256), BF),
            pltpu.VMEM((NB, stamps // 2, rows, LW), F32),
            pltpu.VMEM((rows // 8, 6 * PLANES * 8, packed), BF),
            pltpu.VMEM((rows // 8, 2 * PLANES * 8, packed), BF),
            pltpu.VMEM((rows * PLANES, 4 * LW), F32),
            pltpu.VMEM((strips, 48, LW), F32),
            pltpu.VMEM((rows, cols), F32),
            pltpu.VMEM((blocks + 2, rows + 2 * HALO, LW), F32),
            pltpu.VMEM((blocks + 1, rows, LW), F32),
            dma((dets,)), dma((dets,)), dma((2, dets)), dma((2, dets)), dma((2, dets)), dma((2, dets)),
            dma((strips,)), dma((strips,)), dma, dma,
        ],
        compiler_params=pltpu.CompilerParams(
            collective_id=0, has_side_effects=True, vmem_limit_bytes=56 * 1024 * 1024
        ),
    )(science, template, row_taps, col_taps, stamp_rows, stamp_cols)


def solution(mesh):
    return jax.shard_map(
        functools.partial(local, mesh.shape["det"], mesh.shape["strip"]),
        mesh=mesh,
        in_specs=(
            P("det", "strip", None),
            P(None, "strip", "det"),
            P(),
            P(),
            P("det", None),
            P("det", None),
        ),
        out_specs=(P("det", "strip", None), P("det", None)),
        check_vma=False,
    )
```

```python
import functools

import jax
import jax.numpy as jnp
from jax import lax
from jax.experimental import pallas as pl
from jax.experimental.pallas import tpu as pltpu
from jax.sharding import PartitionSpec as P

NB = 12
KS = 21
HS = 17
KH = 10
NU = 37
LW = 128
HALO = 16
SLOT = 64
PLANES = 16
ONE_PLANE = 12
SCI_PLANE = 13
RIDGE_WEIGHT = 1.0
HIGHEST_MODE = lax.Precision.HIGHEST
MESH = pl.DeviceIdType.MESH
BF = jnp.bfloat16
F32 = jnp.float32


def iota(shape, dim):
    return lax.broadcasted_iota(jnp.int32, shape, dim)


def split(value):
    high = value.astype(BF)
    return high, (value - high.astype(F32)).astype(BF)


def build_row_table(taps_ref, pad_ref, table_ref, rows):
    pad_ref[...] = jnp.zeros_like(pad_ref)
    pad_ref[:NB, :KS] = taps_ref[...]
    for b in range(NB):
        wide = jnp.broadcast_to(pad_ref[b : b + 1, :], (rows, LW))
        moved = pltpu.roll(wide, HALO - KH, 1, stride=1, stride_axis=0)
        high, low = split(moved)
        high, low = high.astype(F32), low.astype(F32)
        high = high + pltpu.roll(high, 64, 1)
        low = low + pltpu.roll(low, 64, 1)
        table_ref[b * rows : (b + 1) * rows, :LW] = high.astype(BF)
        table_ref[b * rows : (b + 1) * rows, LW:] = low.astype(BF)


def build_col_tables(taps_ref, pad_ref, table_ref, stamp_table_ref):
    pad_ref[...] = jnp.zeros_like(pad_ref)
    pad_ref[:NB, :KS] = taps_ref[...]
    lane, sub = iota((LW, LW), 1), iota((LW, LW), 0)
    same_slot = lane // SLOT == sub // SLOT
    for b in range(NB):
        wide = jnp.broadcast_to(pad_ref[b : b + 1, :], (LW, LW))
        moved = pltpu.roll(wide, 0, 1, stride=1, stride_axis=0)
        near = jnp.where(lane >= sub, moved, 0.0).T
        far = jnp.where(lane < sub, moved, 0.0).T
        for part, at in ((near, 0), (far, LW)):
            high, low = split(part)
            table_ref[b, at : at + LW, :LW] = high
            table_ref[b, at : at + LW, LW:] = low
        high, low = split(jnp.where(same_slot, near, 0.0))
        for at in (0, LW):
            stamp_table_ref[b, at : at + LW, :LW] = high
            stamp_table_ref[b, at : at + LW, LW:] = low


def row_filtered(row_table_ref, moved, rows):
    high, low = split(moved)
    stacked = jnp.concatenate([high, low, high, low], axis=0)
    size = NB // 2
    for base in (0, size):
        out = jnp.dot(row_table_ref[base * rows : (base + size) * rows, :], stacked, preferred_element_type=F32)
        yield base, [v.reshape(size, rows, moved.shape[1]) for v in split(out)]


def held_rows(width, first_row, rows, total_rows):
    sub = iota((2 * HALO + rows, width), 0)
    sky = first_row - HALO + sub
    return (sub >= HALO - KH) & (sub < HALO + rows + KH) & (sky >= 0) & (sky < total_rows)


def row_stage(sky_ref, row_table_ref, windows, places, rows):
    size = NB // 2
    lane = iota((2 * HALO + rows, LW), 1)
    moved = [pltpu.roll(jnp.where(lane < LW - KH, sky_ref[m + 1], sky_ref[m]), KH, 1) for m in places]
    moved = jnp.concatenate(moved, axis=1) if len(places) > 1 else moved[0]
    for base, pair in row_filtered(row_table_ref, moved, rows):
        for ref, val in zip(windows, pair):
            for i, m in enumerate(places):
                part = val[:, :, i * LW : (i + 1) * LW]
                ref[base : base + size, m + 1, :, :LW] = part
                ref[base : base + size, m, :, LW:] = part


def col_stage(windows, col_table_ref, resp_ref, rows, cols):
    blocks = cols // LW
    per = 8

    def body(b, carry):
        table = col_table_ref[b]
        for k in range(0, blocks, per):
            hi, lo = [ref[b, k + 1 : k + 1 + per].reshape(per * rows, 2 * LW) for ref in windows]
            out = jnp.dot(hi, table, preferred_element_type=F32) + jnp.dot(lo, table, preferred_element_type=F32)
            resp_ref[b, k : k + per] = (out[:, :LW] + out[:, LW:]).reshape(per, rows, LW)
        return carry

    lax.fori_loop(0, NB, body, 0)


def gather(ref, starts):
    picked = []
    for t, start in enumerate(starts):
        k = start // LW
        off = start - k * LW
        near, far = ref[k], ref[k + 1]
        both = jnp.where(iota(near.shape, 1) >= off, near, far)
        picked.append(pltpu.roll(both, lax.rem(SLOT * t - off + LW, LW), 1))
    return jnp.where(iota(picked[0].shape, 1) < SLOT, *picked)


def stamp_left(cols_ref, s, cols):
    return jnp.clip(cols_ref[0, s] - HS, 0, cols - 1)


def stamp_responses(sky_ref, row_table_ref, stamp_table_ref, win_ref, resp_ref, cols_ref, rows, cols):
    pairs = resp_ref.shape[1]
    size = NB // 2

    def body(u, carry):
        lefts = [stamp_left(cols_ref, 4 * u + t, cols) + (LW - KH) for t in range(4)]
        moved = jnp.concatenate([gather(sky_ref, lefts[:2]), gather(sky_ref, lefts[2:])], axis=1)
        for base, pair in row_filtered(row_table_ref, moved, rows):
            for part, val in enumerate(pair):
                for i in range(2):
                    win_ref[base : base + size, 2 * u + i, :, part * LW : (part + 1) * LW] = val[:, :, i * LW : (i + 1) * LW]
        return carry

    lax.fori_loop(0, pairs // 2, body, 0)

    def filt(b, carry):
        out = jnp.dot(win_ref[b].reshape(pairs * rows, 2 * LW), stamp_table_ref[b], preferred_element_type=F32)
        resp_ref[b] = (out[:, :LW] + out[:, LW:]).reshape(pairs, rows, LW)
        return carry

    lax.fori_loop(0, NB, filt, 0)


def pack_stamps(resp_ref, sci_ref, rows_ref, cols_ref, left_ref, right_ref, first_row, rows, cols):
    groups = rows // 8
    lane = iota((8, LW), 1)

    def body(q, carry):
        lefts = [stamp_left(cols_ref, 2 * q + t, cols) for t in range(2)]
        second = lane >= SLOT
        inside = lane - jnp.where(second, SLOT, 0)
        rowv = jnp.where(second, rows_ref[0, 2 * q + 1], rows_ref[0, 2 * q])
        xv = (jnp.where(second, lefts[1], lefts[0]) + inside).astype(F32) * (2.0 / cols) - 1.0
        sci = gather(sci_ref, lefts)
        at = pl.multiple_of(q * LW, LW)
        ones, zeros = jnp.ones((1, 8, LW), F32), jnp.zeros((PLANES - SCI_PLANE - 1, 8, LW), F32)
        for g in range(groups):
            near = slice(8 * g, 8 * g + 8)
            yv = first_row + 8 * g + iota((8, LW), 0)
            hit = ((jnp.abs(yv - rowv) <= HS) & (inside < 2 * HS + 1)).astype(F32)
            planes = jnp.concatenate([resp_ref[:, q, near, :], ones, sci[None, near, :], zeros], axis=0)
            high, low = split(planes.reshape(PLANES * 8, LW))
            right_ref[g, : PLANES * 8, pl.ds(at, LW)] = high
            right_ref[g, PLANES * 8 :, pl.ds(at, LW)] = low
            moment = planes * hit[None]
            for m in range(3):
                if m:
                    moment = moment * xv[None]
                high, low = split(moment.reshape(PLANES * 8, LW))
                left_ref[g, m * PLANES * 8 : (m + 1) * PLANES * 8, pl.ds(at, LW)] = high
                left_ref[g, (m + 3) * PLANES * 8 : (m + 4) * PLANES * 8, pl.ds(at, LW)] = low
        return carry

    lax.fori_loop(0, resp_ref.shape[1], body, 0)


def build_maps(maps_ref, first_row, rows, total_rows):
    span = PLANES * 8
    plane, col = iota((span, LW), 0) // 8, iota((span, LW), 1)
    kind, base = col // 16, lax.rem(col, 16)
    match = plane == base
    real = match & (plane < NB)
    zero = jnp.zeros((span, LW), F32)
    plain = jnp.where(match & (kind == 0), 1.0, zero)
    in_x = jnp.where(real & (kind == 1), 1.0, zero)
    for g in range(rows // 8):
        y = (2.0 / total_rows) * (first_row + 8 * g + lax.rem(iota((span, LW), 0), 8)).astype(F32) - 1.0
        level = plain + jnp.where(real & (kind == 2), y, zero)
        for i, part in enumerate((level, in_x, level * y, in_x * y)):
            maps_ref[g * span : (g + 1) * span, i * LW : (i + 1) * LW] = part


def normal_part(left_ref, right_ref, maps_ref, rows):
    span = PLANES * 8
    same_y = (lax.rem(iota((8, span), 1), 8) == iota((8, span), 0)).astype(F32)
    picked = []
    for g in range(rows // 8):
        out = lax.dot_general(left_ref[g], right_ref[g], (((1,), (1,)), ((), ())), preferred_element_type=F32)
        folded = out[: 3 * span, :span] + out[: 3 * span, span:] + out[3 * span :, :span]
        picked.append(jnp.sum(folded.reshape(3 * PLANES, 8, span) * same_y[None], axis=1))
    total = jnp.dot(
        jnp.concatenate(picked, axis=1), maps_ref[...], precision=HIGHEST_MODE, preferred_element_type=F32
    )
    return jnp.concatenate(
        [
            total[0:16, 0:LW] + total[16:32, LW : 2 * LW],
            total[16:32, 0:LW] + total[32:48, LW : 2 * LW],
            total[0:16, 2 * LW : 3 * LW] + total[16:32, 3 * LW :],
        ],
        axis=0,
    )


PIVOTS = [*range(0, 13), *range(16, 28), *range(32, 44)]


def solve(normal):
    sub, lane = iota((48, LW), 0), iota((48, LW), 1)
    live = (lax.rem(sub, 16) < NB) | (sub == ONE_PLANE)
    mat = jnp.where((sub == lane) & live, normal + RIDGE_WEIGHT, normal)
    at = lambda value, k: value[k : k + 1, :]
    for i in range(0, NU - 1, 2):
        j, k = PIVOTS[i], PIVOTS[i + 1]
        cj = jnp.broadcast_to(mat[:, j : j + 1], (48, LW))
        ck = jnp.broadcast_to(mat[:, k : k + 1], (48, LW))
        jj, jk, kj, kk = at(cj, j), at(ck, j), at(cj, k), at(ck, k)
        scale = 1.0 / (jj * kk - jk * kj)
        rj, rk = at(mat, j), at(mat, k)
        nj = (kk * rj - jk * rk) * scale
        nk = (jj * rk - kj * rj) * scale
        mat = jnp.where(sub == j, nj, jnp.where(sub == k, nk, mat - cj * nj - ck * nk))
    k = PIVOTS[-1]
    column = jnp.broadcast_to(mat[:, k : k + 1], (48, LW))
    row = at(mat, k) / at(column, k)
    mat = jnp.where(sub == k, row, mat - column * row)
    return mat[:, SCI_PLANE : SCI_PLANE + 1]


def coeff_row(answer):
    sub, lane = iota((48, LW), 0), iota((48, LW), 1)
    kind, base = sub // 16, lax.rem(sub, 16)
    goes = jnp.where(base < NB, kind * NB + base, jnp.where(sub == ONE_PLANE, NU - 1, -1))
    return jnp.sum(jnp.where(goes == lane, answer, 0.0), axis=0, keepdims=True)


def apply_model(answer, resp_ref, sci_ref, out_ref, first_row, rows, total_rows, cols):
    wide = jnp.broadcast_to(answer, (48, LW))
    lift = lambda i: jnp.broadcast_to(wide[i : i + 1, :], (8, LW))
    blocks = cols // LW
    const = lift(ONE_PLANE)
    for g in range(rows // 8):
        y = (2.0 / total_rows) * (first_row + 8 * g + iota((8, LW), 0)).astype(F32) - 1.0
        level = [lift(b) + y * lift(32 + b) for b in range(NB)]
        slope = [lift(16 + b) for b in range(NB)]

        def body(k, carry):
            flat = const
            tilt = jnp.zeros((8, LW), F32)
            for b in range(NB):
                r = resp_ref[b, k, 8 * g : 8 * g + 8, :]
                flat = flat + level[b] * r
                tilt = tilt + slope[b] * r
            at = pl.multiple_of(k * LW, LW)
            x = (k * LW + iota((8, LW), 1)).astype(F32) * (2.0 / cols) - 1.0
            out_ref[0, 8 * g : 8 * g + 8, pl.ds(at, LW)] = sci_ref[k, 8 * g : 8 * g + 8, :] - (flat + x * tilt)
            return carry

        lax.fori_loop(0, blocks, body, 0, unroll=4)


def kernel(
    dets, strips,
    sci_ref, tmpl_ref, row_in, col_in, srow_in, scol_in,
    out_ref, coef_ref,
    row_ref, col_ref, srow_ref, scol_ref,
    frame, pad, row_table, col_table, stamp_table, win_hi, win_lo, resp, stamp_win, stamp_resp, left, right, maps, parts, sci_buf, sky, sci,
    main_send, main_recv, up_send, up_recv, down_send, down_recv, part_send, part_recv, own_sem, sci_sem, small_sem,
):
    _, rows, cols = sci_ref.shape
    width = tmpl_ref.shape[2]
    total_rows = rows * strips
    det, strip = lax.axis_index("det"), lax.axis_index("strip")
    above, below = strip > 0, strip < strips - 1
    first_row = strip * rows

    small = [
        pltpu.make_async_copy(a, b, small_sem.at[i])
        for i, (a, b) in enumerate(((row_in, row_ref), (col_in, col_ref), (srow_in, srow_ref), (scol_in, scol_ref)))
    ]
    for copy in small:
        copy.start()

    barrier = pltpu.get_barrier_semaphore()

    def greet(target_det, target_strip):
        pl.semaphore_signal(barrier, inc=1, device_id=(target_det, target_strip), device_id_type=MESH)

    for i in range(1, dets):
        greet(lax.rem(det + i, dets), strip)

    @pl.when(above)
    def _():
        for i in range(dets):
            greet(lax.rem(det + i, dets), strip - 1)

    @pl.when(below)
    def _():
        for i in range(dets):
            greet(lax.rem(det + i, dets), strip + 1)

    for i in range(2, strips - 1):
        other = lax.rem(strip + i, strips)

        @pl.when((other != strip - 1) & (other != strip + 1))
        def _():
            greet(det, other)

    @pl.when(strip == 0)
    def _():
        greet(det, strips - 1)

    @pl.when(strip == strips - 1)
    def _():
        greet(det, 0)

    ends = jnp.where(above & below, 0, 1)
    count = (dets - 1) + dets * (2 - ends) + (strips - 3 + ends)
    pl.semaphore_wait(barrier, count)

    here = pl.ds(pl.multiple_of(det * width, width), width)

    def main_copy(i):
        target = lax.rem(det + dets - i, dets)
        return pltpu.make_async_remote_copy(
            tmpl_ref.at[target], frame.at[pl.ds(HALO, rows), here],
            main_send.at[i], main_recv.at[i], device_id=(target, strip), device_id_type=MESH,
        )

    ups = ((0, 8), (8, KH - 8))
    downs = ((rows - 8, 8), (rows - KH, KH - 8))

    def up_copy(i, p):
        target = lax.rem(det + dets - i, dets)
        at, size = ups[p]
        return pltpu.make_async_remote_copy(
            tmpl_ref.at[target, pl.ds(at, size), :], frame.at[pl.ds(HALO + rows + at, size), here],
            up_send.at[p, i], up_recv.at[p, i], device_id=(target, strip - 1), device_id_type=MESH,
        )

    def down_copy(i, p):
        target = lax.rem(det + dets - i, dets)
        at, size = downs[p]
        return pltpu.make_async_remote_copy(
            tmpl_ref.at[target, pl.ds(at, size), :], frame.at[pl.ds(HALO - rows + at, size), here],
            down_send.at[p, i], down_recv.at[p, i], device_id=(target, strip + 1), device_id_type=MESH,
        )

    own = pltpu.make_async_copy(
        tmpl_ref.at[det], frame.at[pl.ds(HALO, rows), here], own_sem
    )
    own.start()
    sci_copy = pltpu.make_async_copy(sci_ref.at[0], sci_buf, sci_sem)
    sci_copy.start()
    for i in range(dets):
        if i:
            main_copy(i).start()

        @pl.when(above)
        def _():
            up_copy(i, 0).start()
            up_copy(i, 1).start()

        @pl.when(below)
        def _():
            down_copy(i, 0).start()
            down_copy(i, 1).start()

    blocks = cols // LW
    sky[0] = jnp.zeros((2 * HALO + rows, LW), F32)
    sky[blocks + 1] = jnp.zeros((2 * HALO + rows, LW), F32)
    sci[blocks] = jnp.zeros((rows, LW), F32)
    for copy in small:
        copy.wait()
    build_row_table(row_ref, pad, row_table, rows)
    build_col_tables(col_ref, pad, col_table, stamp_table)
    build_maps(maps, first_row, rows, total_rows)
    sci_copy.wait()
    for k in range(blocks):
        sci[k] = sci_buf[:, k * LW : (k + 1) * LW]
    held = held_rows(LW, first_row, rows, total_rows)
    windows = (win_hi, win_lo)
    half = width // LW

    def received(i):
        @pl.when(above)
        def _():
            for p in range(2):
                down_copy(i, p).wait_recv()

        @pl.when(below)
        def _():
            for p in range(2):
                up_copy(i, p).wait_recv()

        first = half * lax.rem(det + i, dets)
        for t in range(half):
            sky[first + t + 1] = jnp.where(held, frame[:, pl.ds(pl.multiple_of((first + t) * LW, LW), LW)], 0.0)

    def place(n):
        return lax.rem(half * det + 1 + n, blocks + 1)

    def arrive(i, carry):
        main_copy(i).wait_recv()
        received(i)
        row_stage(sky, row_table, windows, [place(half * (i - 1) + t) for t in range(half)], rows)
        return carry

    own.wait()
    received(0)
    lax.fori_loop(1, dets - 1, arrive, 0)
    main_copy(dets - 1).wait_recv()
    received(dets - 1)
    stamp_responses(sky, row_table, stamp_table, stamp_win, stamp_resp, scol_ref, rows, cols)
    pack_stamps(stamp_resp, sci, srow_ref, scol_ref, left, right, first_row, rows, cols)
    parts[strip] = normal_part(left, right, maps, rows)

    def part_copy(i):
        return pltpu.make_async_remote_copy(
            parts.at[strip], parts.at[strip], part_send.at[i], part_recv.at[i],
            device_id=(det, lax.rem(strip + i, strips)), device_id_type=MESH,
        )

    for i in range(1, strips):
        part_copy(i).start()
    done = half * (dets - 2)
    row_stage(sky, row_table, windows, [place(done + t) for t in range(2)], rows)
    row_stage(sky, row_table, windows, [place(done + 2 + t) for t in range(2)], rows)
    row_stage(sky, row_table, windows, [place(blocks)], rows)
    col_stage(windows, col_table, resp, rows, cols)
    for i in range(1, strips):
        source = lax.rem(strip + strips - i, strips)
        part_copy(i).wait_send()
        pltpu.make_async_remote_copy(
            parts.at[source], parts.at[source], part_send.at[i], part_recv.at[i],
            device_id=(det, source), device_id_type=MESH,
        ).wait_recv()
    for i in range(dets):
        if i:
            main_copy(i).wait_send()

        @pl.when(above)
        def _():
            for p in range(2):
                up_copy(i, p).wait_send()

        @pl.when(below)
        def _():
            for p in range(2):
                down_copy(i, p).wait_send()

    normal = parts[0]
    for i in range(1, strips):
        normal = normal + parts[i]
    answer = solve(normal)
    coef_ref[...] = coeff_row(answer)[:, :NU]
    apply_model(answer, resp, sci, out_ref, first_row, rows, total_rows, cols)


def local(dets, strips, science, template, row_taps, col_taps, stamp_rows, stamp_cols):
    _, rows, cols = science.shape
    blocks = cols // LW
    stamps = stamp_rows.shape[1]
    packed = stamps // 2 * LW
    any_space = pl.BlockSpec(memory_space=pl.ANY)
    vmem = pl.BlockSpec(memory_space=pltpu.VMEM)
    hbm = pl.BlockSpec(memory_space=pltpu.HBM)
    dma = pltpu.SemaphoreType.DMA
    results = (jax.ShapeDtypeStruct(science.shape, F32), jax.ShapeDtypeStruct((1, NU), F32))
    return pl.pallas_call(
        functools.partial(kernel, dets, strips),
        out_shape=(pltpu.VMEM(science.shape, F32), pltpu.VMEM((1, NU), F32)),
        in_specs=[hbm] * 6,
        out_specs=(vmem, vmem),
        scratch_shapes=[
            pltpu.VMEM((NB, KS), F32),
            pltpu.VMEM((NB, KS), F32),
            pltpu.SMEM((1, stamps), jnp.int32),
            pltpu.SMEM((1, stamps), jnp.int32),
            pltpu.VMEM((rows + 2 * HALO, cols), F32),
            pltpu.VMEM((16, LW), F32),
            pltpu.VMEM((NB * rows, 256), BF),
            pltpu.VMEM((NB, 256, 256), BF),
            pltpu.VMEM((NB, 256, 256), BF),
            pltpu.VMEM((NB, blocks + 2, rows, 256), BF),
            pltpu.VMEM((NB, blocks + 2, rows, 256), BF),
            pltpu.VMEM((NB, blocks, rows, LW), F32),
            pltpu.VMEM((NB, stamps // 2, rows, 256), BF),
            pltpu.VMEM((NB, stamps // 2, rows, LW), F32),
            pltpu.VMEM((rows // 8, 6 * PLANES * 8, packed), BF),
            pltpu.VMEM((rows // 8, 2 * PLANES * 8, packed), BF),
            pltpu.VMEM((rows * PLANES, 4 * LW), F32),
            pltpu.VMEM((strips, 48, LW), F32),
            pltpu.VMEM((rows, cols), F32),
            pltpu.VMEM((blocks + 2, rows + 2 * HALO, LW), F32),
            pltpu.VMEM((blocks + 1, rows, LW), F32),
            dma((dets,)), dma((dets,)), dma((2, dets)), dma((2, dets)), dma((2, dets)), dma((2, dets)),
            dma((strips,)), dma((strips,)), dma, dma, dma((4,)),
        ],
        compiler_params=pltpu.CompilerParams(
            collective_id=0, has_side_effects=True, vmem_limit_bytes=53 * 1024 * 1024
        ),
    )(
        science,
        template,
        *[pltpu.with_memory_space_constraint(v, pltpu.HBM) for v in (row_taps, col_taps, stamp_rows, stamp_cols)],
    )


def solution(mesh):
    return jax.shard_map(
        functools.partial(local, mesh.shape["det"], mesh.shape["strip"]),
        mesh=mesh,
        in_specs=(
            P("det", "strip", None),
            P(None, "strip", "det"),
            P(),
            P(),
            P("det", None),
            P("det", None),
        ),
        out_specs=(P("det", "strip", None), P("det", None)),
        check_vma=False,
    )
```

```python
import functools

import jax
import jax.numpy as jnp
from jax import lax
from jax.experimental import pallas as pl
from jax.experimental.pallas import tpu as pltpu
from jax.sharding import PartitionSpec as P

NB = 12
KS = 21
HS = 17
KH = 10
NU = 37
LW = 128
HALO = 16
SLOT = 64
PLANES = 16
ONE_PLANE = 12
SCI_PLANE = 13
RIDGE_WEIGHT = 1.0
HIGHEST_MODE = lax.Precision.HIGHEST
MESH = pl.DeviceIdType.MESH
BF = jnp.bfloat16
F32 = jnp.float32


def iota(shape, dim):
    return lax.broadcasted_iota(jnp.int32, shape, dim)


def split(value):
    high = value.astype(BF)
    return high, (value - high.astype(F32)).astype(BF)


def build_row_table(taps_ref, pad_ref, table_ref, rows):
    pad_ref[...] = jnp.zeros_like(pad_ref)
    pad_ref[:NB, :KS] = taps_ref[...]
    for b in range(NB):
        wide = jnp.broadcast_to(pad_ref[b : b + 1, :], (rows, LW))
        moved = pltpu.roll(wide, HALO - KH, 1, stride=1, stride_axis=0)
        high, low = split(moved)
        high, low = high.astype(F32), low.astype(F32)
        high = high + pltpu.roll(high, 64, 1)
        low = low + pltpu.roll(low, 64, 1)
        table_ref[b * rows : (b + 1) * rows, :LW] = high.astype(BF)
        table_ref[b * rows : (b + 1) * rows, LW:] = low.astype(BF)


def build_col_tables(taps_ref, pad_ref, table_ref, stamp_table_ref):
    pad_ref[...] = jnp.zeros_like(pad_ref)
    pad_ref[:NB, :KS] = taps_ref[...]
    lane, sub = iota((LW, LW), 1), iota((LW, LW), 0)
    same_slot = lane // SLOT == sub // SLOT
    for b in range(NB):
        wide = jnp.broadcast_to(pad_ref[b : b + 1, :], (LW, LW))
        moved = pltpu.roll(wide, 0, 1, stride=1, stride_axis=0)
        near = jnp.where(lane >= sub, moved, 0.0).T
        far = jnp.where(lane < sub, moved, 0.0).T
        for part, at in ((near, 0), (far, LW)):
            high, low = split(part)
            table_ref[b, at : at + LW, :LW] = high
            table_ref[b, at : at + LW, LW:] = low
        high, low = split(jnp.where(same_slot, near, 0.0))
        for at in (0, LW):
            stamp_table_ref[b, at : at + LW, :LW] = high
            stamp_table_ref[b, at : at + LW, LW:] = low


def row_filtered(row_table_ref, moved, rows):
    high, low = split(moved)
    stacked = jnp.concatenate([high, low, high, low], axis=0)
    size = NB // 2
    for base in (0, size):
        out = jnp.dot(row_table_ref[base * rows : (base + size) * rows, :], stacked, preferred_element_type=F32)
        yield base, [v.reshape(size, rows, moved.shape[1]) for v in split(out)]


def held_rows(width, first_row, rows, total_rows):
    sub = iota((2 * HALO + rows, width), 0)
    sky = first_row - HALO + sub
    return (sub >= HALO - KH) & (sub < HALO + rows + KH) & (sky >= 0) & (sky < total_rows)


def row_stage(sky_ref, row_table_ref, windows, places, rows):
    size = NB // 2
    lane = iota((2 * HALO + rows, LW), 1)
    moved = [pltpu.roll(jnp.where(lane < LW - KH, sky_ref[m + 1], sky_ref[m]), KH, 1) for m in places]
    moved = jnp.concatenate(moved, axis=1) if len(places) > 1 else moved[0]
    for base, pair in row_filtered(row_table_ref, moved, rows):
        for ref, val in zip(windows, pair):
            for i, m in enumerate(places):
                part = val[:, :, i * LW : (i + 1) * LW]
                ref[base : base + size, m + 1, :, :LW] = part
                ref[base : base + size, m, :, LW:] = part


def col_stage(windows, col_table_ref, resp_ref, rows, cols):
    blocks = cols // LW
    per = 8

    def body(b, carry):
        table = col_table_ref[b]
        for k in range(0, blocks, per):
            hi, lo = [ref[b, k + 1 : k + 1 + per].reshape(per * rows, 2 * LW) for ref in windows]
            out = jnp.dot(hi, table, preferred_element_type=F32) + jnp.dot(lo, table, preferred_element_type=F32)
            resp_ref[b, k : k + per] = (out[:, :LW] + out[:, LW:]).reshape(per, rows, LW)
        return carry

    lax.fori_loop(0, NB, body, 0, unroll=True)


def gather(ref, starts):
    picked = []
    for t, start in enumerate(starts):
        k = start // LW
        off = start - k * LW
        near, far = ref[k], ref[k + 1]
        both = jnp.where(iota(near.shape, 1) >= off, near, far)
        picked.append(pltpu.roll(both, lax.rem(SLOT * t - off + LW, LW), 1))
    return jnp.where(iota(picked[0].shape, 1) < SLOT, *picked)


def stamp_left(cols_ref, s, cols):
    return jnp.clip(cols_ref[0, s] - HS, 0, cols - 1)


def stamp_responses(sky_ref, row_table_ref, stamp_table_ref, win_ref, resp_ref, cols_ref, rows, cols):
    pairs = resp_ref.shape[1]
    size = NB // 2

    def body(u, carry):
        lefts = [stamp_left(cols_ref, 4 * u + t, cols) + (LW - KH) for t in range(4)]
        moved = jnp.concatenate([gather(sky_ref, lefts[:2]), gather(sky_ref, lefts[2:])], axis=1)
        for base, pair in row_filtered(row_table_ref, moved, rows):
            for part, val in enumerate(pair):
                for i in range(2):
                    win_ref[base : base + size, 2 * u + i, :, part * LW : (part + 1) * LW] = val[:, :, i * LW : (i + 1) * LW]
        return carry

    lax.fori_loop(0, pairs // 2, body, 0, unroll=True)

    def filt(b, carry):
        out = jnp.dot(win_ref[b].reshape(pairs * rows, 2 * LW), stamp_table_ref[b], preferred_element_type=F32)
        resp_ref[b] = (out[:, :LW] + out[:, LW:]).reshape(pairs, rows, LW)
        return carry

    lax.fori_loop(0, NB, filt, 0, unroll=True)


def pack_stamps(resp_ref, sci_ref, rows_ref, cols_ref, left_ref, right_ref, first_row, rows, cols):
    groups = rows // 8
    lane = iota((8, LW), 1)

    def body(q, carry):
        lefts = [stamp_left(cols_ref, 2 * q + t, cols) for t in range(2)]
        second = lane >= SLOT
        inside = lane - jnp.where(second, SLOT, 0)
        rowv = jnp.where(second, rows_ref[0, 2 * q + 1], rows_ref[0, 2 * q])
        xv = (jnp.where(second, lefts[1], lefts[0]) + inside).astype(F32) * (2.0 / cols) - 1.0
        sci = gather(sci_ref, lefts)
        at = pl.multiple_of(q * LW, LW)
        ones, zeros = jnp.ones((1, 8, LW), F32), jnp.zeros((PLANES - SCI_PLANE - 1, 8, LW), F32)
        for g in range(groups):
            near = slice(8 * g, 8 * g + 8)
            yv = first_row + 8 * g + iota((8, LW), 0)
            hit = ((jnp.abs(yv - rowv) <= HS) & (inside < 2 * HS + 1)).astype(F32)
            planes = jnp.concatenate([resp_ref[:, q, near, :], ones, sci[None, near, :], zeros], axis=0)
            high, low = split(planes.reshape(PLANES * 8, LW))
            right_ref[g, : PLANES * 8, pl.ds(at, LW)] = high
            right_ref[g, PLANES * 8 :, pl.ds(at, LW)] = low
            moment = planes * hit[None]
            for m in range(3):
                if m:
                    moment = moment * xv[None]
                high, low = split(moment.reshape(PLANES * 8, LW))
                left_ref[g, m * PLANES * 8 : (m + 1) * PLANES * 8, pl.ds(at, LW)] = high
                left_ref[g, (m + 3) * PLANES * 8 : (m + 4) * PLANES * 8, pl.ds(at, LW)] = low
        return carry

    lax.fori_loop(0, resp_ref.shape[1], body, 0, unroll=4)


def build_maps(maps_ref, first_row, rows, total_rows):
    span = PLANES * 8
    plane, col = iota((span, LW), 0) // 8, iota((span, LW), 1)
    kind, base = col // 16, lax.rem(col, 16)
    match = plane == base
    real = match & (plane < NB)
    zero = jnp.zeros((span, LW), F32)
    plain = jnp.where(match & (kind == 0), 1.0, zero)
    in_x = jnp.where(real & (kind == 1), 1.0, zero)
    for g in range(rows // 8):
        y = (2.0 / total_rows) * (first_row + 8 * g + lax.rem(iota((span, LW), 0), 8)).astype(F32) - 1.0
        level = plain + jnp.where(real & (kind == 2), y, zero)
        for i, part in enumerate((level, in_x, level * y, in_x * y)):
            maps_ref[g * span : (g + 1) * span, i * LW : (i + 1) * LW] = part


def normal_part(left_ref, right_ref, maps_ref, rows):
    span = PLANES * 8
    same_y = (lax.rem(iota((8, span), 1), 8) == iota((8, span), 0)).astype(F32)
    picked = []
    for g in range(rows // 8):
        out = lax.dot_general(left_ref[g], right_ref[g], (((1,), (1,)), ((), ())), preferred_element_type=F32)
        folded = out[: 3 * span, :span] + out[: 3 * span, span:] + out[3 * span :, :span]
        picked.append(jnp.sum(folded.reshape(3 * PLANES, 8, span) * same_y[None], axis=1))
    total = jnp.dot(
        jnp.concatenate(picked, axis=1), maps_ref[...], precision=HIGHEST_MODE, preferred_element_type=F32
    )
    return jnp.concatenate(
        [
            total[0:16, 0:LW] + total[16:32, LW : 2 * LW],
            total[16:32, 0:LW] + total[32:48, LW : 2 * LW],
            total[0:16, 2 * LW : 3 * LW] + total[16:32, 3 * LW :],
        ],
        axis=0,
    )


PIVOTS = [*range(0, 13), *range(16, 28), *range(32, 44)]


def solve(normal):
    sub, lane = iota((48, LW), 0), iota((48, LW), 1)
    live = (lax.rem(sub, 16) < NB) | (sub == ONE_PLANE)
    mat = jnp.where((sub == lane) & live, normal + RIDGE_WEIGHT, normal)
    at = lambda value, k: value[k : k + 1, :]
    for i in range(0, NU - 1, 2):
        j, k = PIVOTS[i], PIVOTS[i + 1]
        cj = jnp.broadcast_to(mat[:, j : j + 1], (48, LW))
        ck = jnp.broadcast_to(mat[:, k : k + 1], (48, LW))
        jj, jk, kj, kk = at(cj, j), at(ck, j), at(cj, k), at(ck, k)
        scale = 1.0 / (jj * kk - jk * kj)
        rj, rk = at(mat, j), at(mat, k)
        nj = (kk * rj - jk * rk) * scale
        nk = (jj * rk - kj * rj) * scale
        mat = jnp.where(sub == j, nj, jnp.where(sub == k, nk, mat - cj * nj - ck * nk))
    k = PIVOTS[-1]
    column = jnp.broadcast_to(mat[:, k : k + 1], (48, LW))
    row = at(mat, k) / at(column, k)
    mat = jnp.where(sub == k, row, mat - column * row)
    return mat[:, SCI_PLANE : SCI_PLANE + 1]


def coeff_row(answer):
    sub, lane = iota((48, LW), 0), iota((48, LW), 1)
    kind, base = sub // 16, lax.rem(sub, 16)
    goes = jnp.where(base < NB, kind * NB + base, jnp.where(sub == ONE_PLANE, NU - 1, -1))
    return jnp.sum(jnp.where(goes == lane, answer, 0.0), axis=0, keepdims=True)


def apply_model(answer, resp_ref, sci_ref, out_ref, first_row, rows, total_rows, cols):
    wide = jnp.broadcast_to(answer, (48, LW))
    lift = lambda i: jnp.broadcast_to(wide[i : i + 1, :], (8, LW))
    blocks = cols // LW
    const = lift(ONE_PLANE)
    for g in range(rows // 8):
        y = (2.0 / total_rows) * (first_row + 8 * g + iota((8, LW), 0)).astype(F32) - 1.0
        level = [lift(b) + y * lift(32 + b) for b in range(NB)]
        slope = [lift(16 + b) for b in range(NB)]

        def body(k, carry):
            flat = const
            tilt = jnp.zeros((8, LW), F32)
            for b in range(NB):
                r = resp_ref[b, k, 8 * g : 8 * g + 8, :]
                flat = flat + level[b] * r
                tilt = tilt + slope[b] * r
            at = pl.multiple_of(k * LW, LW)
            x = (k * LW + iota((8, LW), 1)).astype(F32) * (2.0 / cols) - 1.0
            out_ref[0, 8 * g : 8 * g + 8, pl.ds(at, LW)] = sci_ref[k, 8 * g : 8 * g + 8, :] - (flat + x * tilt)
            return carry

        lax.fori_loop(0, blocks, body, 0, unroll=4)


def kernel(
    dets, strips,
    sci_ref, tmpl_ref, row_in, col_in, srow_in, scol_in,
    out_ref, coef_ref,
    row_ref, col_ref, srow_ref, scol_ref,
    frame, pad, row_table, col_table, stamp_table, win_hi, win_lo, resp, stamp_win, stamp_resp, left, right, maps, parts, sci_buf, sky, sci,
    main_send, main_recv, up_send, up_recv, down_send, down_recv, part_send, part_recv, own_sem, sci_sem, small_sem,
):
    _, rows, cols = sci_ref.shape
    width = tmpl_ref.shape[2]
    total_rows = rows * strips
    det, strip = lax.axis_index("det"), lax.axis_index("strip")
    above, below = strip > 0, strip < strips - 1
    first_row = strip * rows

    small = [
        pltpu.make_async_copy(a, b, small_sem.at[i])
        for i, (a, b) in enumerate(((row_in, row_ref), (col_in, col_ref), (srow_in, srow_ref), (scol_in, scol_ref)))
    ]
    for copy in small:
        copy.start()

    barrier = pltpu.get_barrier_semaphore()

    def greet(target_det, target_strip):
        pl.semaphore_signal(barrier, inc=1, device_id=(target_det, target_strip), device_id_type=MESH)

    for i in range(1, dets):
        greet(lax.rem(det + i, dets), strip)

    @pl.when(above)
    def _():
        for i in range(dets):
            greet(lax.rem(det + i, dets), strip - 1)

    @pl.when(below)
    def _():
        for i in range(dets):
            greet(lax.rem(det + i, dets), strip + 1)

    for i in range(2, strips - 1):
        other = lax.rem(strip + i, strips)

        @pl.when((other != strip - 1) & (other != strip + 1))
        def _():
            greet(det, other)

    @pl.when(strip == 0)
    def _():
        greet(det, strips - 1)

    @pl.when(strip == strips - 1)
    def _():
        greet(det, 0)

    ends = jnp.where(above & below, 0, 1)
    count = (dets - 1) + dets * (2 - ends) + (strips - 3 + ends)
    pl.semaphore_wait(barrier, count)

    here = pl.ds(pl.multiple_of(det * width, width), width)

    def main_copy(i):
        target = lax.rem(det + dets - i, dets)
        return pltpu.make_async_remote_copy(
            tmpl_ref.at[target], frame.at[pl.ds(HALO, rows), here],
            main_send.at[i], main_recv.at[i], device_id=(target, strip), device_id_type=MESH,
        )

    ups = ((0, 8), (8, KH - 8))
    downs = ((rows - 8, 8), (rows - KH, KH - 8))

    def up_copy(i, p):
        target = lax.rem(det + dets - i, dets)
        at, size = ups[p]
        return pltpu.make_async_remote_copy(
            tmpl_ref.at[target, pl.ds(at, size), :], frame.at[pl.ds(HALO + rows + at, size), here],
            up_send.at[p, i], up_recv.at[p, i], device_id=(target, strip - 1), device_id_type=MESH,
        )

    def down_copy(i, p):
        target = lax.rem(det + dets - i, dets)
        at, size = downs[p]
        return pltpu.make_async_remote_copy(
            tmpl_ref.at[target, pl.ds(at, size), :], frame.at[pl.ds(HALO - rows + at, size), here],
            down_send.at[p, i], down_recv.at[p, i], device_id=(target, strip + 1), device_id_type=MESH,
        )

    own = pltpu.make_async_copy(
        tmpl_ref.at[det], frame.at[pl.ds(HALO, rows), here], own_sem
    )
    own.start()
    sci_copy = pltpu.make_async_copy(sci_ref.at[0], sci_buf, sci_sem)
    sci_copy.start()
    for i in range(dets):
        if i:
            main_copy(i).start()

        @pl.when(above)
        def _():
            up_copy(i, 0).start()
            up_copy(i, 1).start()

        @pl.when(below)
        def _():
            down_copy(i, 0).start()
            down_copy(i, 1).start()

    blocks = cols // LW
    sky[0] = jnp.zeros((2 * HALO + rows, LW), F32)
    sky[blocks + 1] = jnp.zeros((2 * HALO + rows, LW), F32)
    sci[blocks] = jnp.zeros((rows, LW), F32)
    for copy in small:
        copy.wait()
    build_row_table(row_ref, pad, row_table, rows)
    build_col_tables(col_ref, pad, col_table, stamp_table)
    build_maps(maps, first_row, rows, total_rows)
    sci_copy.wait()
    for k in range(blocks):
        sci[k] = sci_buf[:, k * LW : (k + 1) * LW]
    held = held_rows(LW, first_row, rows, total_rows)
    windows = (win_hi, win_lo)
    half = width // LW

    def received(i):
        @pl.when(above)
        def _():
            for p in range(2):
                down_copy(i, p).wait_recv()

        @pl.when(below)
        def _():
            for p in range(2):
                up_copy(i, p).wait_recv()

        first = half * lax.rem(det + i, dets)
        for t in range(half):
            sky[first + t + 1] = jnp.where(held, frame[:, pl.ds(pl.multiple_of((first + t) * LW, LW), LW)], 0.0)

    def place(n):
        return lax.rem(half * det + 1 + n, blocks + 1)

    def arrive(i, carry):
        main_copy(i).wait_recv()
        received(i)
        row_stage(sky, row_table, windows, [place(half * (i - 1) + t) for t in range(half)], rows)
        return carry

    own.wait()
    received(0)
    lax.fori_loop(1, dets - 1, arrive, 0)
    main_copy(dets - 1).wait_recv()
    received(dets - 1)
    stamp_responses(sky, row_table, stamp_table, stamp_win, stamp_resp, scol_ref, rows, cols)
    pack_stamps(stamp_resp, sci, srow_ref, scol_ref, left, right, first_row, rows, cols)
    parts[strip] = normal_part(left, right, maps, rows)

    def part_copy(i):
        return pltpu.make_async_remote_copy(
            parts.at[strip], parts.at[strip], part_send.at[i], part_recv.at[i],
            device_id=(det, lax.rem(strip + i, strips)), device_id_type=MESH,
        )

    for i in range(1, strips):
        part_copy(i).start()
    done = half * (dets - 2)
    row_stage(sky, row_table, windows, [place(done + t) for t in range(2)], rows)
    row_stage(sky, row_table, windows, [place(done + 2 + t) for t in range(2)], rows)
    row_stage(sky, row_table, windows, [place(blocks)], rows)
    col_stage(windows, col_table, resp, rows, cols)
    for i in range(1, strips):
        source = lax.rem(strip + strips - i, strips)
        part_copy(i).wait_send()
        pltpu.make_async_remote_copy(
            parts.at[source], parts.at[source], part_send.at[i], part_recv.at[i],
            device_id=(det, source), device_id_type=MESH,
        ).wait_recv()
    for i in range(dets):
        if i:
            main_copy(i).wait_send()

        @pl.when(above)
        def _():
            for p in range(2):
                up_copy(i, p).wait_send()

        @pl.when(below)
        def _():
            for p in range(2):
                down_copy(i, p).wait_send()

    normal = parts[0]
    for i in range(1, strips):
        normal = normal + parts[i]
    answer = solve(normal)
    coef_ref[...] = coeff_row(answer)[:, :NU]
    apply_model(answer, resp, sci, out_ref, first_row, rows, total_rows, cols)


def local(dets, strips, science, template, row_taps, col_taps, stamp_rows, stamp_cols):
    _, rows, cols = science.shape
    blocks = cols // LW
    stamps = stamp_rows.shape[1]
    packed = stamps // 2 * LW
    any_space = pl.BlockSpec(memory_space=pl.ANY)
    vmem = pl.BlockSpec(memory_space=pltpu.VMEM)
    hbm = pl.BlockSpec(memory_space=pltpu.HBM)
    dma = pltpu.SemaphoreType.DMA
    results = (jax.ShapeDtypeStruct(science.shape, F32), jax.ShapeDtypeStruct((1, NU), F32))
    return pl.pallas_call(
        functools.partial(kernel, dets, strips),
        out_shape=(pltpu.VMEM(science.shape, F32), pltpu.VMEM((1, NU), F32)),
        in_specs=[hbm] * 6,
        out_specs=(vmem, vmem),
        scratch_shapes=[
            pltpu.VMEM((NB, KS), F32),
            pltpu.VMEM((NB, KS), F32),
            pltpu.SMEM((1, stamps), jnp.int32),
            pltpu.SMEM((1, stamps), jnp.int32),
            pltpu.VMEM((rows + 2 * HALO, cols), F32),
            pltpu.VMEM((16, LW), F32),
            pltpu.VMEM((NB * rows, 256), BF),
            pltpu.VMEM((NB, 256, 256), BF),
            pltpu.VMEM((NB, 256, 256), BF),
            pltpu.VMEM((NB, blocks + 2, rows, 256), BF),
            pltpu.VMEM((NB, blocks + 2, rows, 256), BF),
            pltpu.VMEM((NB, blocks, rows, LW), F32),
            pltpu.VMEM((NB, stamps // 2, rows, 256), BF),
            pltpu.VMEM((NB, stamps // 2, rows, LW), F32),
            pltpu.VMEM((rows // 8, 6 * PLANES * 8, packed), BF),
            pltpu.VMEM((rows // 8, 2 * PLANES * 8, packed), BF),
            pltpu.VMEM((rows * PLANES, 4 * LW), F32),
            pltpu.VMEM((strips, 48, LW), F32),
            pltpu.VMEM((rows, cols), F32),
            pltpu.VMEM((blocks + 2, rows + 2 * HALO, LW), F32),
            pltpu.VMEM((blocks + 1, rows, LW), F32),
            dma((dets,)), dma((dets,)), dma((2, dets)), dma((2, dets)), dma((2, dets)), dma((2, dets)),
            dma((strips,)), dma((strips,)), dma, dma, dma((4,)),
        ],
        compiler_params=pltpu.CompilerParams(
            collective_id=0, has_side_effects=True, vmem_limit_bytes=53 * 1024 * 1024
        ),
    )(
        science,
        template,
        *[pltpu.with_memory_space_constraint(v, pltpu.HBM) for v in (row_taps, col_taps, stamp_rows, stamp_cols)],
    )


def solution(mesh):
    return jax.shard_map(
        functools.partial(local, mesh.shape["det"], mesh.shape["strip"]),
        mesh=mesh,
        in_specs=(
            P("det", "strip", None),
            P(None, "strip", "det"),
            P(),
            P(),
            P("det", None),
            P("det", None),
        ),
        out_specs=(P("det", "strip", None), P("det", None)),
        check_vma=False,
    )
```

```python
import functools

import jax
import jax.numpy as jnp
from jax import lax
from jax.experimental import pallas as pl
from jax.experimental.pallas import tpu as pltpu
from jax.sharding import PartitionSpec as P

NB = 12
KS = 21
HS = 17
KH = 10
NU = 37
LW = 128
HALO = 16
SLOT = 64
PLANES = 16
ONE_PLANE = 12
SCI_PLANE = 13
RIDGE_WEIGHT = 1.0
HIGHEST_MODE = lax.Precision.HIGHEST
MESH = pl.DeviceIdType.MESH
BF = jnp.bfloat16
F32 = jnp.float32


def iota(shape, dim):
    return lax.broadcasted_iota(jnp.int32, shape, dim)


def split(value):
    high = value.astype(BF)
    return high, (value - high.astype(F32)).astype(BF)


def build_row_table(taps_ref, pad_ref, table_ref, rows):
    pad_ref[...] = jnp.zeros_like(pad_ref)
    pad_ref[:NB, :KS] = taps_ref[...]
    for b in range(NB):
        wide = jnp.broadcast_to(pad_ref[b : b + 1, :], (rows, LW))
        moved = pltpu.roll(wide, HALO - KH, 1, stride=1, stride_axis=0)
        high, low = split(moved)
        high, low = high.astype(F32), low.astype(F32)
        high = high + pltpu.roll(high, 64, 1)
        low = low + pltpu.roll(low, 64, 1)
        table_ref[b * rows : (b + 1) * rows, :LW] = high.astype(BF)
        table_ref[b * rows : (b + 1) * rows, LW:] = low.astype(BF)


def build_col_tables(taps_ref, pad_ref, table_ref, stamp_table_ref):
    pad_ref[...] = jnp.zeros_like(pad_ref)
    pad_ref[:NB, :KS] = taps_ref[...]
    lane, sub = iota((LW, LW), 1), iota((LW, LW), 0)
    same_slot = lane // SLOT == sub // SLOT
    for b in range(NB):
        wide = jnp.broadcast_to(pad_ref[b : b + 1, :], (LW, LW))
        moved = pltpu.roll(wide, 0, 1, stride=1, stride_axis=0)
        near = jnp.where(lane >= sub, moved, 0.0).T
        far = jnp.where(lane < sub, moved, 0.0).T
        for part, at in ((near, 0), (far, LW)):
            high, low = split(part)
            table_ref[b, at : at + LW, :LW] = high
            table_ref[b, at : at + LW, LW:] = low
        high, low = split(jnp.where(same_slot, near, 0.0))
        for at in (0, LW):
            stamp_table_ref[b, at : at + LW, :LW] = high
            stamp_table_ref[b, at : at + LW, LW:] = low


def row_filtered(row_table_ref, moved, rows):
    high, low = split(moved)
    stacked = jnp.concatenate([high, low, high, low], axis=0)
    size = NB // 2
    for base in (0, size):
        out = jnp.dot(row_table_ref[base * rows : (base + size) * rows, :], stacked, preferred_element_type=F32)
        yield base, [v.reshape(size, rows, moved.shape[1]) for v in split(out)]


def held_rows(width, first_row, rows, total_rows):
    sub = iota((2 * HALO + rows, width), 0)
    sky = first_row - HALO + sub
    return (sub >= HALO - KH) & (sub < HALO + rows + KH) & (sky >= 0) & (sky < total_rows)


def row_stage(sky_ref, row_table_ref, windows, places, rows):
    size = NB // 2
    lane = iota((2 * HALO + rows, LW), 1)
    moved = [pltpu.roll(jnp.where(lane < LW - KH, sky_ref[m + 1], sky_ref[m]), KH, 1) for m in places]
    moved = jnp.concatenate(moved, axis=1) if len(places) > 1 else moved[0]
    for base, pair in row_filtered(row_table_ref, moved, rows):
        for ref, val in zip(windows, pair):
            for i, m in enumerate(places):
                part = val[:, :, i * LW : (i + 1) * LW]
                ref[base : base + size, m + 1, :, :LW] = part
                ref[base : base + size, m, :, LW:] = part


def col_stage(windows, col_table_ref, resp_ref, rows, cols):
    blocks = cols // LW
    per = 8

    def body(b, carry):
        table = col_table_ref[b]
        for k in range(0, blocks, per):
            hi, lo = [ref[b, k + 1 : k + 1 + per].reshape(per * rows, 2 * LW) for ref in windows]
            out = jnp.dot(hi, table, preferred_element_type=F32) + jnp.dot(lo, table, preferred_element_type=F32)
            resp_ref[b, k : k + per] = (out[:, :LW] + out[:, LW:]).reshape(per, rows, LW)
        return carry

    lax.fori_loop(0, NB, body, 0, unroll=True)


def gather(ref, starts):
    picked = []
    for t, start in enumerate(starts):
        k = start // LW
        off = start - k * LW
        near, far = ref[k], ref[k + 1]
        both = jnp.where(iota(near.shape, 1) >= off, near, far)
        picked.append(pltpu.roll(both, lax.rem(SLOT * t - off + LW, LW), 1))
    return jnp.where(iota(picked[0].shape, 1) < SLOT, *picked)


def stamp_left(cols_ref, s, cols):
    return jnp.clip(cols_ref[0, s] - HS, 0, cols - 1)


def stamp_responses(sky_ref, row_table_ref, stamp_table_ref, win_ref, resp_ref, cols_ref, rows, cols):
    pairs = resp_ref.shape[1]
    size = NB // 2

    def body(u, carry):
        lefts = [stamp_left(cols_ref, 4 * u + t, cols) + (LW - KH) for t in range(4)]
        moved = jnp.concatenate([gather(sky_ref, lefts[:2]), gather(sky_ref, lefts[2:])], axis=1)
        for base, pair in row_filtered(row_table_ref, moved, rows):
            for part, val in enumerate(pair):
                for i in range(2):
                    win_ref[base : base + size, 2 * u + i, :, part * LW : (part + 1) * LW] = val[:, :, i * LW : (i + 1) * LW]
        return carry

    lax.fori_loop(0, pairs // 2, body, 0, unroll=True)

    def filt(b, carry):
        out = jnp.dot(win_ref[b].reshape(pairs * rows, 2 * LW), stamp_table_ref[b], preferred_element_type=F32)
        resp_ref[b] = (out[:, :LW] + out[:, LW:]).reshape(pairs, rows, LW)
        return carry

    lax.fori_loop(0, NB, filt, 0, unroll=True)


def pack_stamps(resp_ref, sci_ref, rows_ref, cols_ref, left_ref, right_ref, first_row, rows, cols):
    groups = rows // 8
    lane = iota((8, LW), 1)

    def body(q, carry):
        lefts = [stamp_left(cols_ref, 2 * q + t, cols) for t in range(2)]
        second = lane >= SLOT
        inside = lane - jnp.where(second, SLOT, 0)
        rowv = jnp.where(second, rows_ref[0, 2 * q + 1], rows_ref[0, 2 * q])
        xv = (jnp.where(second, lefts[1], lefts[0]) + inside).astype(F32) * (2.0 / cols) - 1.0
        sci = gather(sci_ref, lefts)
        at = pl.multiple_of(q * LW, LW)
        ones, zeros = jnp.ones((1, 8, LW), F32), jnp.zeros((PLANES - SCI_PLANE - 1, 8, LW), F32)
        for g in range(groups):
            near = slice(8 * g, 8 * g + 8)
            yv = first_row + 8 * g + iota((8, LW), 0)
            hit = ((jnp.abs(yv - rowv) <= HS) & (inside < 2 * HS + 1)).astype(F32)
            planes = jnp.concatenate([resp_ref[:, q, near, :], ones, sci[None, near, :], zeros], axis=0)
            high, low = split(planes.reshape(PLANES * 8, LW))
            right_ref[g, : PLANES * 8, pl.ds(at, LW)] = high
            right_ref[g, PLANES * 8 :, pl.ds(at, LW)] = low
            moment = planes * hit[None]
            for m in range(3):
                if m:
                    moment = moment * xv[None]
                high, low = split(moment.reshape(PLANES * 8, LW))
                left_ref[g, m * PLANES * 8 : (m + 1) * PLANES * 8, pl.ds(at, LW)] = high
                left_ref[g, (m + 3) * PLANES * 8 : (m + 4) * PLANES * 8, pl.ds(at, LW)] = low
        return carry

    lax.fori_loop(0, resp_ref.shape[1], body, 0, unroll=4)


def build_maps(maps_ref, first_row, rows, total_rows):
    span = PLANES * 8
    plane, col = iota((span, LW), 0) // 8, iota((span, LW), 1)
    kind, base = col // 16, lax.rem(col, 16)
    match = plane == base
    real = match & (plane < NB)
    zero = jnp.zeros((span, LW), F32)
    plain = jnp.where(match & (kind == 0), 1.0, zero)
    in_x = jnp.where(real & (kind == 1), 1.0, zero)
    for g in range(rows // 8):
        y = (2.0 / total_rows) * (first_row + 8 * g + lax.rem(iota((span, LW), 0), 8)).astype(F32) - 1.0
        level = plain + jnp.where(real & (kind == 2), y, zero)
        for i, part in enumerate((level, in_x, level * y, in_x * y)):
            high, low = split(part)
            maps_ref[g * span : (g + 1) * span, i * LW : (i + 1) * LW] = high
            if i == 2:
                maps_ref[g * span : (g + 1) * span, 4 * LW :] = low


def normal_part(left_ref, right_ref, maps_ref, rows):
    span = PLANES * 8
    same_y = (lax.rem(iota((8, span), 1), 8) == iota((8, span), 0)).astype(F32)
    picked = []
    for g in range(rows // 8):
        out = lax.dot_general(left_ref[g], right_ref[g], (((1,), (1,)), ((), ())), preferred_element_type=F32)
        folded = out[: 3 * span, :span] + out[: 3 * span, span:] + out[3 * span :, :span]
        picked.append(jnp.sum(folded.reshape(3 * PLANES, 8, span) * same_y[None], axis=1))
    sums = jnp.concatenate(picked, axis=1)
    high, low = split(sums)
    lower = (sums - high.astype(F32) - low.astype(F32)).astype(BF)
    total = jnp.dot(jnp.concatenate([high, low, lower], axis=0), maps_ref[...], preferred_element_type=F32)
    total = total[:48] + total[48:96] + total[96:]
    squared = total[:, 2 * LW : 3 * LW] + total[:, 4 * LW :]
    whole = jnp.concatenate(
        [
            total[0:16, 0:LW] + total[16:32, LW : 2 * LW],
            total[16:32, 0:LW] + total[32:48, LW : 2 * LW],
            squared[0:16] + total[16:32, 3 * LW : 4 * LW],
        ],
        axis=0,
    )
    return jnp.where(iota((24, LW), 1) < LW // 2, whole[:24], pltpu.roll(whole[24:], LW // 2, 1))


def unfolded(halves):
    return jnp.concatenate([halves, pltpu.roll(halves, LW // 2, 1)], axis=0)


PIVOTS = [*range(0, 13), *range(16, 28), *range(32, 44)]


def solve(normal):
    sub, lane = iota((48, LW), 0), iota((48, LW), 1)
    live = (lax.rem(sub, 16) < NB) | (sub == ONE_PLANE)
    mat = jnp.where((sub == lane) & live, normal + RIDGE_WEIGHT, normal)
    at = lambda value, k: value[k : k + 1, :]
    for i in range(0, NU - 1, 2):
        j, k = PIVOTS[i], PIVOTS[i + 1]
        cj = jnp.broadcast_to(mat[:, j : j + 1], (48, LW))
        ck = jnp.broadcast_to(mat[:, k : k + 1], (48, LW))
        jj, jk, kj, kk = at(cj, j), at(ck, j), at(cj, k), at(ck, k)
        scale = 1.0 / (jj * kk - jk * kj)
        rj, rk = at(mat, j), at(mat, k)
        nj = (kk * rj - jk * rk) * scale
        nk = (jj * rk - kj * rj) * scale
        mat = jnp.where(sub == j, nj, jnp.where(sub == k, nk, mat - cj * nj - ck * nk))
    k = PIVOTS[-1]
    column = jnp.broadcast_to(mat[:, k : k + 1], (48, LW))
    row = at(mat, k) / at(column, k)
    mat = jnp.where(sub == k, row, mat - column * row)
    return mat[:, SCI_PLANE : SCI_PLANE + 1]


def coeff_row(answer):
    sub, lane = iota((48, LW), 0), iota((48, LW), 1)
    kind, base = sub // 16, lax.rem(sub, 16)
    goes = jnp.where(base < NB, kind * NB + base, jnp.where(sub == ONE_PLANE, NU - 1, -1))
    return jnp.sum(jnp.where(goes == lane, answer, 0.0), axis=0, keepdims=True)


def apply_model(answer, resp_ref, sci_ref, out_ref, first_row, rows, total_rows, cols):
    wide = jnp.broadcast_to(answer, (48, LW))
    lift = lambda i: jnp.broadcast_to(wide[i : i + 1, :], (8, LW))
    blocks = cols // LW
    const = lift(ONE_PLANE)
    for g in range(rows // 8):
        y = (2.0 / total_rows) * (first_row + 8 * g + iota((8, LW), 0)).astype(F32) - 1.0
        level = [lift(b) + y * lift(32 + b) for b in range(NB)]
        slope = [lift(16 + b) for b in range(NB)]

        def body(k, carry):
            flat = const
            tilt = jnp.zeros((8, LW), F32)
            for b in range(NB):
                r = resp_ref[b, k, 8 * g : 8 * g + 8, :]
                flat = flat + level[b] * r
                tilt = tilt + slope[b] * r
            at = pl.multiple_of(k * LW, LW)
            x = (k * LW + iota((8, LW), 1)).astype(F32) * (2.0 / cols) - 1.0
            out_ref[0, 8 * g : 8 * g + 8, pl.ds(at, LW)] = sci_ref[k, 8 * g : 8 * g + 8, :] - (flat + x * tilt)
            return carry

        lax.fori_loop(0, blocks, body, 0, unroll=4)


def kernel(
    dets, strips,
    sci_ref, tmpl_ref, row_in, col_in, srow_in, scol_in,
    out_ref, coef_ref,
    row_ref, col_ref, srow_ref, scol_ref,
    frame, pad, row_table, col_table, stamp_table, win_hi, win_lo, resp, stamp_win, stamp_resp, left, right, maps, parts, sci_buf, sky, sci,
    main_send, main_recv, up_send, up_recv, down_send, down_recv, part_send, part_recv, own_sem, sci_sem, small_sem,
):
    _, rows, cols = sci_ref.shape
    width = tmpl_ref.shape[2]
    total_rows = rows * strips
    det, strip = lax.axis_index("det"), lax.axis_index("strip")
    above, below = strip > 0, strip < strips - 1
    first_row = strip * rows

    small = [
        pltpu.make_async_copy(a, b, small_sem.at[i])
        for i, (a, b) in enumerate(((row_in, row_ref), (col_in, col_ref), (srow_in, srow_ref), (scol_in, scol_ref)))
    ]
    for copy in small:
        copy.start()

    barrier = pltpu.get_barrier_semaphore()

    def greet(target_det, target_strip):
        pl.semaphore_signal(barrier, inc=1, device_id=(target_det, target_strip), device_id_type=MESH)

    for i in range(1, dets):
        greet(lax.rem(det + i, dets), strip)

    @pl.when(above)
    def _():
        for i in range(dets):
            greet(lax.rem(det + i, dets), strip - 1)

    @pl.when(below)
    def _():
        for i in range(dets):
            greet(lax.rem(det + i, dets), strip + 1)

    for i in range(2, strips - 1):
        other = lax.rem(strip + i, strips)

        @pl.when((other != strip - 1) & (other != strip + 1))
        def _():
            greet(det, other)

    @pl.when(strip == 0)
    def _():
        greet(det, strips - 1)

    @pl.when(strip == strips - 1)
    def _():
        greet(det, 0)

    ends = jnp.where(above & below, 0, 1)
    count = (dets - 1) + dets * (2 - ends) + (strips - 3 + ends)
    pl.semaphore_wait(barrier, count)

    here = pl.ds(pl.multiple_of(det * width, width), width)

    def main_copy(i):
        target = lax.rem(det + dets - i, dets)
        return pltpu.make_async_remote_copy(
            tmpl_ref.at[target], frame.at[pl.ds(HALO, rows), here],
            main_send.at[i], main_recv.at[i], device_id=(target, strip), device_id_type=MESH,
        )

    ups = ((0, 8), (8, KH - 8))
    downs = ((rows - 8, 8), (rows - KH, KH - 8))

    def up_copy(i, p):
        target = lax.rem(det + dets - i, dets)
        at, size = ups[p]
        return pltpu.make_async_remote_copy(
            tmpl_ref.at[target, pl.ds(at, size), :], frame.at[pl.ds(HALO + rows + at, size), here],
            up_send.at[p, i], up_recv.at[p, i], device_id=(target, strip - 1), device_id_type=MESH,
        )

    def down_copy(i, p):
        target = lax.rem(det + dets - i, dets)
        at, size = downs[p]
        return pltpu.make_async_remote_copy(
            tmpl_ref.at[target, pl.ds(at, size), :], frame.at[pl.ds(HALO - rows + at, size), here],
            down_send.at[p, i], down_recv.at[p, i], device_id=(target, strip + 1), device_id_type=MESH,
        )

    own = pltpu.make_async_copy(
        tmpl_ref.at[det], frame.at[pl.ds(HALO, rows), here], own_sem
    )
    own.start()
    sci_copy = pltpu.make_async_copy(sci_ref.at[0], sci_buf, sci_sem)
    sci_copy.start()
    for i in range(dets):
        if i:
            main_copy(i).start()

        @pl.when(above)
        def _():
            up_copy(i, 0).start()
            up_copy(i, 1).start()

        @pl.when(below)
        def _():
            down_copy(i, 0).start()
            down_copy(i, 1).start()

    blocks = cols // LW
    sky[0] = jnp.zeros((2 * HALO + rows, LW), F32)
    sky[blocks + 1] = jnp.zeros((2 * HALO + rows, LW), F32)
    sci[blocks] = jnp.zeros((rows, LW), F32)
    for copy in small:
        copy.wait()
    build_row_table(row_ref, pad, row_table, rows)
    build_col_tables(col_ref, pad, col_table, stamp_table)
    build_maps(maps, first_row, rows, total_rows)
    sci_copy.wait()
    for k in range(blocks):
        sci[k] = sci_buf[:, k * LW : (k + 1) * LW]
    held = held_rows(LW, first_row, rows, total_rows)
    windows = (win_hi, win_lo)
    half = width // LW

    def received(i):
        @pl.when(above)
        def _():
            for p in range(2):
                down_copy(i, p).wait_recv()

        @pl.when(below)
        def _():
            for p in range(2):
                up_copy(i, p).wait_recv()

        first = half * lax.rem(det + i, dets)
        for t in range(half):
            sky[first + t + 1] = jnp.where(held, frame[:, pl.ds(pl.multiple_of((first + t) * LW, LW), LW)], 0.0)

    def place(n):
        return lax.rem(half * det + 1 + n, blocks + 1)

    def arrive(i, carry):
        main_copy(i).wait_recv()
        received(i)
        row_stage(sky, row_table, windows, [place(half * (i - 1) + t) for t in range(half)], rows)
        return carry

    own.wait()
    received(0)
    lax.fori_loop(1, dets - 1, arrive, 0)
    main_copy(dets - 1).wait_recv()
    received(dets - 1)
    stamp_responses(sky, row_table, stamp_table, stamp_win, stamp_resp, scol_ref, rows, cols)
    pack_stamps(stamp_resp, sci, srow_ref, scol_ref, left, right, first_row, rows, cols)
    parts[strip] = normal_part(left, right, maps, rows)

    def part_copy(i):
        return pltpu.make_async_remote_copy(
            parts.at[strip], parts.at[strip], part_send.at[i], part_recv.at[i],
            device_id=(det, lax.rem(strip + i, strips)), device_id_type=MESH,
        )

    for i in range(1, strips):
        part_copy(i).start()
    done = half * (dets - 2)
    row_stage(sky, row_table, windows, [place(done + t) for t in range(2)], rows)
    row_stage(sky, row_table, windows, [place(done + 2 + t) for t in range(2)], rows)
    row_stage(sky, row_table, windows, [place(blocks)], rows)
    col_stage(windows, col_table, resp, rows, cols)
    for i in range(1, strips):
        source = lax.rem(strip + strips - i, strips)
        part_copy(i).wait_send()
        pltpu.make_async_remote_copy(
            parts.at[source], parts.at[source], part_send.at[i], part_recv.at[i],
            device_id=(det, source), device_id_type=MESH,
        ).wait_recv()
    for i in range(dets):
        if i:
            main_copy(i).wait_send()

        @pl.when(above)
        def _():
            for p in range(2):
                up_copy(i, p).wait_send()

        @pl.when(below)
        def _():
            for p in range(2):
                down_copy(i, p).wait_send()

    normal = parts[0]
    for i in range(1, strips):
        normal = normal + parts[i]
    answer = solve(unfolded(normal))
    coef_ref[...] = coeff_row(answer)[:, :NU]
    apply_model(answer, resp, sci, out_ref, first_row, rows, total_rows, cols)


def local(dets, strips, science, template, row_taps, col_taps, stamp_rows, stamp_cols):
    _, rows, cols = science.shape
    blocks = cols // LW
    stamps = stamp_rows.shape[1]
    packed = stamps // 2 * LW
    any_space = pl.BlockSpec(memory_space=pl.ANY)
    vmem = pl.BlockSpec(memory_space=pltpu.VMEM)
    hbm = pl.BlockSpec(memory_space=pltpu.HBM)
    dma = pltpu.SemaphoreType.DMA
    results = (jax.ShapeDtypeStruct(science.shape, F32), jax.ShapeDtypeStruct((1, NU), F32))
    return pl.pallas_call(
        functools.partial(kernel, dets, strips),
        out_shape=(pltpu.VMEM(science.shape, F32), pltpu.VMEM((1, NU), F32)),
        in_specs=[hbm] * 6,
        out_specs=(vmem, vmem),
        scratch_shapes=[
            pltpu.VMEM((NB, KS), F32),
            pltpu.VMEM((NB, KS), F32),
            pltpu.SMEM((1, stamps), jnp.int32),
            pltpu.SMEM((1, stamps), jnp.int32),
            pltpu.VMEM((rows + 2 * HALO, cols), F32),
            pltpu.VMEM((16, LW), F32),
            pltpu.VMEM((NB * rows, 256), BF),
            pltpu.VMEM((NB, 256, 256), BF),
            pltpu.VMEM((NB, 256, 256), BF),
            pltpu.VMEM((NB, blocks + 2, rows, 256), BF),
            pltpu.VMEM((NB, blocks + 2, rows, 256), BF),
            pltpu.VMEM((NB, blocks, rows, LW), F32),
            pltpu.VMEM((NB, stamps // 2, rows, 256), BF),
            pltpu.VMEM((NB, stamps // 2, rows, LW), F32),
            pltpu.VMEM((rows // 8, 6 * PLANES * 8, packed), BF),
            pltpu.VMEM((rows // 8, 2 * PLANES * 8, packed), BF),
            pltpu.VMEM((rows * PLANES, 5 * LW), BF),
            pltpu.VMEM((strips, 24, LW), F32),
            pltpu.VMEM((rows, cols), F32),
            pltpu.VMEM((blocks + 2, rows + 2 * HALO, LW), F32),
            pltpu.VMEM((blocks + 1, rows, LW), F32),
            dma((dets,)), dma((dets,)), dma((2, dets)), dma((2, dets)), dma((2, dets)), dma((2, dets)),
            dma((strips,)), dma((strips,)), dma, dma, dma((4,)),
        ],
        compiler_params=pltpu.CompilerParams(
            collective_id=0, has_side_effects=True, vmem_limit_bytes=53 * 1024 * 1024
        ),
    )(
        science,
        template,
        *[pltpu.with_memory_space_constraint(v, pltpu.HBM) for v in (row_taps, col_taps, stamp_rows, stamp_cols)],
    )


def solution(mesh):
    return jax.shard_map(
        functools.partial(local, mesh.shape["det"], mesh.shape["strip"]),
        mesh=mesh,
        in_specs=(
            P("det", "strip", None),
            P(None, "strip", "det"),
            P(),
            P(),
            P("det", None),
            P("det", None),
        ),
        out_specs=(P("det", "strip", None), P("det", None)),
        check_vma=False,
    )
```

```python
import functools

import jax
import jax.numpy as jnp
from jax import lax
from jax.experimental import pallas as pl
from jax.experimental.pallas import tpu as pltpu
from jax.sharding import PartitionSpec as P

NB = 12
KS = 21
HS = 17
KH = 10
NU = 37
LW = 128
HALO = 16
SLOT = 64
PLANES = 16
ONE_PLANE = 12
SCI_PLANE = 13
RIDGE_WEIGHT = 1.0
HIGHEST_MODE = lax.Precision.HIGHEST
MESH = pl.DeviceIdType.MESH
BF = jnp.bfloat16
F32 = jnp.float32


def iota(shape, dim):
    return lax.broadcasted_iota(jnp.int32, shape, dim)


def split(value):
    high = value.astype(BF)
    return high, (value - high.astype(F32)).astype(BF)


def build_row_table(taps_ref, pad_ref, table_ref, rows):
    pad_ref[...] = jnp.zeros_like(pad_ref)
    pad_ref[:NB, :KS] = taps_ref[...]
    for b in range(NB):
        wide = jnp.broadcast_to(pad_ref[b : b + 1, :], (rows, LW))
        moved = pltpu.roll(wide, HALO - KH, 1, stride=1, stride_axis=0)
        high, low = split(moved)
        high, low = high.astype(F32), low.astype(F32)
        high = high + pltpu.roll(high, 64, 1)
        low = low + pltpu.roll(low, 64, 1)
        table_ref[b * rows : (b + 1) * rows, :LW] = high.astype(BF)
        table_ref[b * rows : (b + 1) * rows, LW:] = low.astype(BF)


def build_col_tables(taps_ref, pad_ref, table_ref, stamp_table_ref):
    pad_ref[...] = jnp.zeros_like(pad_ref)
    pad_ref[:NB, :KS] = taps_ref[...]
    lane, sub = iota((LW, LW), 1), iota((LW, LW), 0)
    same_slot = lane // SLOT == sub // SLOT
    for b in range(NB):
        wide = jnp.broadcast_to(pad_ref[b : b + 1, :], (LW, LW))
        moved = pltpu.roll(wide, 0, 1, stride=1, stride_axis=0)
        near = jnp.where(lane >= sub, moved, 0.0).T
        far = jnp.where(lane < sub, moved, 0.0).T
        for part, at in ((near, 0), (far, LW)):
            high, low = split(part)
            table_ref[b, at : at + LW, :LW] = high
            table_ref[b, at : at + LW, LW:] = low
        high, low = split(jnp.where(same_slot, near, 0.0))
        for at in (0, LW):
            stamp_table_ref[b, at : at + LW, :LW] = high
            stamp_table_ref[b, at : at + LW, LW:] = low


def row_filtered(row_table_ref, moved, rows):
    high, low = split(moved)
    stacked = jnp.concatenate([high, low, high, low], axis=0)
    size = NB // 2
    for base in (0, size):
        out = jnp.dot(row_table_ref[base * rows : (base + size) * rows, :], stacked, preferred_element_type=F32)
        yield base, [v.reshape(size, rows, moved.shape[1]) for v in split(out)]


def held_rows(width, first_row, rows, total_rows):
    sub = iota((2 * HALO + rows, width), 0)
    sky = first_row - HALO + sub
    return (sub >= HALO - KH) & (sub < HALO + rows + KH) & (sky >= 0) & (sky < total_rows)


def row_stage(sky_ref, row_table_ref, windows, places, rows):
    size = NB // 2
    lane = iota((2 * HALO + rows, LW), 1)
    moved = [pltpu.roll(jnp.where(lane < LW - KH, sky_ref[m + 1], sky_ref[m]), KH, 1) for m in places]
    moved = jnp.concatenate(moved, axis=1) if len(places) > 1 else moved[0]
    for base, pair in row_filtered(row_table_ref, moved, rows):
        for ref, val in zip(windows, pair):
            for i, m in enumerate(places):
                part = val[:, :, i * LW : (i + 1) * LW]
                ref[base : base + size, m + 1, :, :LW] = part
                ref[base : base + size, m, :, LW:] = part


def col_stage(windows, col_table_ref, resp_ref, rows, cols):
    blocks = cols // LW
    per = 8

    def body(b, carry):
        table = col_table_ref[b]
        for k in range(0, blocks, per):
            hi, lo = [ref[b, k + 1 : k + 1 + per].reshape(per * rows, 2 * LW) for ref in windows]
            out = jnp.dot(hi, table, preferred_element_type=F32) + jnp.dot(lo, table, preferred_element_type=F32)
            resp_ref[b, k : k + per] = (out[:, :LW] + out[:, LW:]).reshape(per, rows, LW)
        return carry

    lax.fori_loop(0, NB, body, 0, unroll=True)


def gather(ref, starts):
    picked = []
    for t, start in enumerate(starts):
        k = start // LW
        off = start - k * LW
        near, far = ref[k], ref[k + 1]
        both = jnp.where(iota(near.shape, 1) >= off, near, far)
        picked.append(pltpu.roll(both, lax.rem(SLOT * t - off + LW, LW), 1))
    return jnp.where(iota(picked[0].shape, 1) < SLOT, *picked)


def stamp_left(cols_ref, s, cols):
    return jnp.clip(cols_ref[0, s] - HS, 0, cols - 1)


def stamp_responses(sky_ref, row_table_ref, stamp_table_ref, win_ref, resp_ref, cols_ref, rows, cols):
    pairs = resp_ref.shape[1]
    size = NB // 2

    def body(u, carry):
        lefts = [stamp_left(cols_ref, 4 * u + t, cols) + (LW - KH) for t in range(4)]
        moved = jnp.concatenate([gather(sky_ref, lefts[:2]), gather(sky_ref, lefts[2:])], axis=1)
        for base, pair in row_filtered(row_table_ref, moved, rows):
            for part, val in enumerate(pair):
                for i in range(2):
                    win_ref[base : base + size, 2 * u + i, :, part * LW : (part + 1) * LW] = val[:, :, i * LW : (i + 1) * LW]
        return carry

    lax.fori_loop(0, pairs // 2, body, 0, unroll=True)

    def filt(b, carry):
        out = jnp.dot(win_ref[b].reshape(pairs * rows, 2 * LW), stamp_table_ref[b], preferred_element_type=F32)
        resp_ref[b] = (out[:, :LW] + out[:, LW:]).reshape(pairs, rows, LW)
        return carry

    lax.fori_loop(0, NB, filt, 0, unroll=True)


def pack_stamps(resp_ref, sci_ref, rows_ref, cols_ref, left_ref, right_ref, first_row, rows, cols):
    groups = rows // 8
    lane = iota((8, LW), 1)

    def body(q, carry):
        lefts = [stamp_left(cols_ref, 2 * q + t, cols) for t in range(2)]
        second = lane >= SLOT
        inside = lane - jnp.where(second, SLOT, 0)
        rowv = jnp.where(second, rows_ref[0, 2 * q + 1], rows_ref[0, 2 * q])
        xv = (jnp.where(second, lefts[1], lefts[0]) + inside).astype(F32) * (2.0 / cols) - 1.0
        sci = gather(sci_ref, lefts)
        at = pl.multiple_of(q * LW, LW)
        ones, zeros = jnp.ones((1, 8, LW), F32), jnp.zeros((PLANES - SCI_PLANE - 1, 8, LW), F32)
        for g in range(groups):
            near = slice(8 * g, 8 * g + 8)
            yv = first_row + 8 * g + iota((8, LW), 0)
            hit = ((jnp.abs(yv - rowv) <= HS) & (inside < 2 * HS + 1)).astype(F32)
            planes = jnp.concatenate([resp_ref[:, q, near, :], ones, sci[None, near, :], zeros], axis=0)
            high, low = split(planes.reshape(PLANES * 8, LW))
            right_ref[g, : PLANES * 8, pl.ds(at, LW)] = high
            right_ref[g, PLANES * 8 :, pl.ds(at, LW)] = low
            moment = planes * hit[None]
            for m in range(3):
                if m:
                    moment = moment * xv[None]
                high, low = split(moment.reshape(PLANES * 8, LW))
                left_ref[g, m * PLANES * 8 : (m + 1) * PLANES * 8, pl.ds(at, LW)] = high
                left_ref[g, (m + 3) * PLANES * 8 : (m + 4) * PLANES * 8, pl.ds(at, LW)] = low
        return carry

    lax.fori_loop(0, resp_ref.shape[1], body, 0, unroll=4)


def build_maps(maps_ref, first_row, rows, total_rows):
    span = PLANES * 8
    plane, col = iota((span, LW), 0) // 8, iota((span, LW), 1)
    kind, base = col // 16, lax.rem(col, 16)
    match = plane == base
    real = match & (plane < NB)
    zero = jnp.zeros((span, LW), F32)
    plain = jnp.where(match & (kind == 0), 1.0, zero)
    in_x = jnp.where(real & (kind == 1), 1.0, zero)
    for g in range(rows // 8):
        y = (2.0 / total_rows) * (first_row + 8 * g + lax.rem(iota((span, LW), 0), 8)).astype(F32) - 1.0
        level = plain + jnp.where(real & (kind == 2), y, zero)
        for i, part in enumerate((level, in_x, level * y, in_x * y)):
            high, low = split(part)
            maps_ref[g * span : (g + 1) * span, i * LW : (i + 1) * LW] = high
            if i == 2:
                maps_ref[g * span : (g + 1) * span, 4 * LW :] = low


def normal_part(left_ref, right_ref, maps_ref, rows):
    span = PLANES * 8
    same_y = (lax.rem(iota((8, span), 1), 8) == iota((8, span), 0)).astype(F32)
    picked = []
    for g in range(rows // 8):
        out = lax.dot_general(left_ref[g], right_ref[g], (((1,), (1,)), ((), ())), preferred_element_type=F32)
        folded = out[: 3 * span, :span] + out[: 3 * span, span:] + out[3 * span :, :span]
        picked.append(jnp.sum(folded.reshape(3 * PLANES, 8, span) * same_y[None], axis=1))
    sums = jnp.concatenate(picked, axis=1)
    high, low = split(sums)
    lower = (sums - high.astype(F32) - low.astype(F32)).astype(BF)
    total = jnp.dot(jnp.concatenate([high, low, lower], axis=0), maps_ref[...], preferred_element_type=F32)
    total = total[:48] + total[48:96] + total[96:]
    squared = total[:, 2 * LW : 3 * LW] + total[:, 4 * LW :]
    whole = jnp.concatenate(
        [
            total[0:16, 0:LW] + total[16:32, LW : 2 * LW],
            total[16:32, 0:LW] + total[32:48, LW : 2 * LW],
            squared[0:16] + total[16:32, 3 * LW : 4 * LW],
        ],
        axis=0,
    )
    return jnp.where(iota((24, LW), 1) < LW // 2, whole[:24], pltpu.roll(whole[24:], LW // 2, 1))


def unfolded(halves):
    return jnp.concatenate([halves, pltpu.roll(halves, LW // 2, 1)], axis=0)


PIVOTS = [*range(0, 13), *range(16, 28), *range(32, 44)]


def solve(normal):
    sub, lane = iota((48, LW), 0), iota((48, LW), 1)
    live = (lax.rem(sub, 16) < NB) | (sub == ONE_PLANE)
    mat = jnp.where((sub == lane) & live, normal + RIDGE_WEIGHT, normal)
    at = lambda value, k: value[k : k + 1, :]

    def pair(first, second, tops, lows):
        scale = 1.0 / (first[0] * second[1] - first[1] * second[0])
        return [
            ((second[1] * t - first[1] * w) * scale, (first[0] * w - second[0] * t) * scale) for t, w in zip(tops, lows)
        ]

    for i in range(0, NU - 1, 4):
        picks = PIVOTS[i : i + 4]
        columns = [jnp.broadcast_to(mat[:, k : k + 1], (48, LW)) for k in picks]
        rows = [[at(c, k) for c in columns] + [at(mat, k)] for k in picks]
        upper = pair(rows[0], rows[1], rows[0][2:], rows[1][2:])
        rest = [[r[2 + j] - r[0] * t - r[1] * w for j, (t, w) in enumerate(upper)] for r in rows[2:]]
        ((third, fourth),) = pair(rest[0], rest[1], rest[0][2:], rest[1][2:])
        first = upper[2][0] - upper[0][0] * third - upper[1][0] * fourth
        second = upper[2][1] - upper[0][1] * third - upper[1][1] * fourth
        solved = [first, second, third, fourth]
        left = mat
        for c, r in zip(columns, solved):
            left = left - c * r
        for k, r in zip(picks, solved):
            left = jnp.where(sub == k, r, left)
        mat = left
    k = PIVOTS[-1]
    column = jnp.broadcast_to(mat[:, k : k + 1], (48, LW))
    row = at(mat, k) / at(column, k)
    mat = jnp.where(sub == k, row, mat - column * row)
    return mat[:, SCI_PLANE : SCI_PLANE + 1]


def coeff_row(answer):
    sub, lane = iota((48, LW), 0), iota((48, LW), 1)
    kind, base = sub // 16, lax.rem(sub, 16)
    goes = jnp.where(base < NB, kind * NB + base, jnp.where(sub == ONE_PLANE, NU - 1, -1))
    return jnp.sum(jnp.where(goes == lane, answer, 0.0), axis=0, keepdims=True)


def apply_model(answer, resp_ref, sci_ref, out_ref, first_row, rows, total_rows, cols):
    wide = jnp.broadcast_to(answer, (48, LW))
    lift = lambda i: jnp.broadcast_to(wide[i : i + 1, :], (8, LW))
    blocks = cols // LW
    const = lift(ONE_PLANE)
    for g in range(rows // 8):
        y = (2.0 / total_rows) * (first_row + 8 * g + iota((8, LW), 0)).astype(F32) - 1.0
        level = [lift(b) + y * lift(32 + b) for b in range(NB)]
        slope = [lift(16 + b) for b in range(NB)]

        def body(k, carry):
            flat = const
            tilt = jnp.zeros((8, LW), F32)
            for b in range(NB):
                r = resp_ref[b, k, 8 * g : 8 * g + 8, :]
                flat = flat + level[b] * r
                tilt = tilt + slope[b] * r
            at = pl.multiple_of(k * LW, LW)
            x = (k * LW + iota((8, LW), 1)).astype(F32) * (2.0 / cols) - 1.0
            out_ref[0, 8 * g : 8 * g + 8, pl.ds(at, LW)] = sci_ref[k, 8 * g : 8 * g + 8, :] - (flat + x * tilt)
            return carry

        lax.fori_loop(0, blocks, body, 0, unroll=4)


def kernel(
    dets, strips,
    sci_ref, tmpl_ref, row_in, col_in, srow_in, scol_in,
    out_ref, coef_ref,
    row_ref, col_ref, srow_ref, scol_ref,
    frame, pad, row_table, col_table, stamp_table, win_hi, win_lo, resp, stamp_win, stamp_resp, left, right, maps, parts, sci_buf, sky, sci,
    main_send, main_recv, up_send, up_recv, down_send, down_recv, part_send, part_recv, own_sem, sci_sem, small_sem,
):
    _, rows, cols = sci_ref.shape
    width = tmpl_ref.shape[2]
    total_rows = rows * strips
    det, strip = lax.axis_index("det"), lax.axis_index("strip")
    above, below = strip > 0, strip < strips - 1
    first_row = strip * rows

    small = [
        pltpu.make_async_copy(a, b, small_sem.at[i])
        for i, (a, b) in enumerate(((row_in, row_ref), (col_in, col_ref), (srow_in, srow_ref), (scol_in, scol_ref)))
    ]
    for copy in small:
        copy.start()

    barrier = pltpu.get_barrier_semaphore()

    def greet(target_det, target_strip):
        pl.semaphore_signal(barrier, inc=1, device_id=(target_det, target_strip), device_id_type=MESH)

    for i in range(1, dets):
        greet(lax.rem(det + i, dets), strip)

    @pl.when(above)
    def _():
        for i in range(dets):
            greet(lax.rem(det + i, dets), strip - 1)

    @pl.when(below)
    def _():
        for i in range(dets):
            greet(lax.rem(det + i, dets), strip + 1)

    for i in range(2, strips - 1):
        other = lax.rem(strip + i, strips)

        @pl.when((other != strip - 1) & (other != strip + 1))
        def _():
            greet(det, other)

    @pl.when(strip == 0)
    def _():
        greet(det, strips - 1)

    @pl.when(strip == strips - 1)
    def _():
        greet(det, 0)

    ends = jnp.where(above & below, 0, 1)
    count = (dets - 1) + dets * (2 - ends) + (strips - 3 + ends)
    pl.semaphore_wait(barrier, count)

    here = pl.ds(pl.multiple_of(det * width, width), width)

    def main_copy(i):
        target = lax.rem(det + dets - i, dets)
        return pltpu.make_async_remote_copy(
            tmpl_ref.at[target], frame.at[pl.ds(HALO, rows), here],
            main_send.at[i], main_recv.at[i], device_id=(target, strip), device_id_type=MESH,
        )

    ups = ((0, 8), (8, KH - 8))
    downs = ((rows - 8, 8), (rows - KH, KH - 8))

    def up_copy(i, p):
        target = lax.rem(det + dets - i, dets)
        at, size = ups[p]
        return pltpu.make_async_remote_copy(
            tmpl_ref.at[target, pl.ds(at, size), :], frame.at[pl.ds(HALO + rows + at, size), here],
            up_send.at[p, i], up_recv.at[p, i], device_id=(target, strip - 1), device_id_type=MESH,
        )

    def down_copy(i, p):
        target = lax.rem(det + dets - i, dets)
        at, size = downs[p]
        return pltpu.make_async_remote_copy(
            tmpl_ref.at[target, pl.ds(at, size), :], frame.at[pl.ds(HALO - rows + at, size), here],
            down_send.at[p, i], down_recv.at[p, i], device_id=(target, strip + 1), device_id_type=MESH,
        )

    own = pltpu.make_async_copy(
        tmpl_ref.at[det], frame.at[pl.ds(HALO, rows), here], own_sem
    )
    own.start()
    sci_copy = pltpu.make_async_copy(sci_ref.at[0], sci_buf, sci_sem)
    sci_copy.start()
    for i in range(dets):
        if i:
            main_copy(i).start()

        @pl.when(above)
        def _():
            up_copy(i, 0).start()
            up_copy(i, 1).start()

        @pl.when(below)
        def _():
            down_copy(i, 0).start()
            down_copy(i, 1).start()

    blocks = cols // LW
    sky[0] = jnp.zeros((2 * HALO + rows, LW), F32)
    sky[blocks + 1] = jnp.zeros((2 * HALO + rows, LW), F32)
    sci[blocks] = jnp.zeros((rows, LW), F32)
    for copy in small:
        copy.wait()
    build_row_table(row_ref, pad, row_table, rows)
    build_col_tables(col_ref, pad, col_table, stamp_table)
    build_maps(maps, first_row, rows, total_rows)
    sci_copy.wait()
    for k in range(blocks):
        sci[k] = sci_buf[:, k * LW : (k + 1) * LW]
    held = held_rows(LW, first_row, rows, total_rows)
    windows = (win_hi, win_lo)
    half = width // LW

    def received(i):
        @pl.when(above)
        def _():
            for p in range(2):
                down_copy(i, p).wait_recv()

        @pl.when(below)
        def _():
            for p in range(2):
                up_copy(i, p).wait_recv()

        first = half * lax.rem(det + i, dets)
        for t in range(half):
            sky[first + t + 1] = jnp.where(held, frame[:, pl.ds(pl.multiple_of((first + t) * LW, LW), LW)], 0.0)

    def place(n):
        return lax.rem(half * det + 1 + n, blocks + 1)

    def arrive(i, carry):
        main_copy(i).wait_recv()
        received(i)
        row_stage(sky, row_table, windows, [place(half * (i - 1) + t) for t in range(half)], rows)
        return carry

    own.wait()
    received(0)
    lax.fori_loop(1, dets - 1, arrive, 0)
    main_copy(dets - 1).wait_recv()
    received(dets - 1)
    stamp_responses(sky, row_table, stamp_table, stamp_win, stamp_resp, scol_ref, rows, cols)
    pack_stamps(stamp_resp, sci, srow_ref, scol_ref, left, right, first_row, rows, cols)
    parts[strip] = normal_part(left, right, maps, rows)

    def part_copy(i):
        return pltpu.make_async_remote_copy(
            parts.at[strip], parts.at[strip], part_send.at[i], part_recv.at[i],
            device_id=(det, lax.rem(strip + i, strips)), device_id_type=MESH,
        )

    for i in range(1, strips):
        part_copy(i).start()
    done = half * (dets - 2)
    row_stage(sky, row_table, windows, [place(done + t) for t in range(2)], rows)
    row_stage(sky, row_table, windows, [place(done + 2 + t) for t in range(2)], rows)
    row_stage(sky, row_table, windows, [place(blocks)], rows)
    col_stage(windows, col_table, resp, rows, cols)
    for i in range(1, strips):
        source = lax.rem(strip + strips - i, strips)
        part_copy(i).wait_send()
        pltpu.make_async_remote_copy(
            parts.at[source], parts.at[source], part_send.at[i], part_recv.at[i],
            device_id=(det, source), device_id_type=MESH,
        ).wait_recv()
    for i in range(dets):
        if i:
            main_copy(i).wait_send()

        @pl.when(above)
        def _():
            for p in range(2):
                up_copy(i, p).wait_send()

        @pl.when(below)
        def _():
            for p in range(2):
                down_copy(i, p).wait_send()

    normal = parts[0]
    for i in range(1, strips):
        normal = normal + parts[i]
    answer = solve(unfolded(normal))
    coef_ref[...] = coeff_row(answer)[:, :NU]
    apply_model(answer, resp, sci, out_ref, first_row, rows, total_rows, cols)


def local(dets, strips, science, template, row_taps, col_taps, stamp_rows, stamp_cols):
    _, rows, cols = science.shape
    blocks = cols // LW
    stamps = stamp_rows.shape[1]
    packed = stamps // 2 * LW
    any_space = pl.BlockSpec(memory_space=pl.ANY)
    vmem = pl.BlockSpec(memory_space=pltpu.VMEM)
    hbm = pl.BlockSpec(memory_space=pltpu.HBM)
    dma = pltpu.SemaphoreType.DMA
    results = (jax.ShapeDtypeStruct(science.shape, F32), jax.ShapeDtypeStruct((1, NU), F32))
    return pl.pallas_call(
        functools.partial(kernel, dets, strips),
        out_shape=(pltpu.VMEM(science.shape, F32), pltpu.VMEM((1, NU), F32)),
        in_specs=[hbm] * 6,
        out_specs=(vmem, vmem),
        scratch_shapes=[
            pltpu.VMEM((NB, KS), F32),
            pltpu.VMEM((NB, KS), F32),
            pltpu.SMEM((1, stamps), jnp.int32),
            pltpu.SMEM((1, stamps), jnp.int32),
            pltpu.VMEM((rows + 2 * HALO, cols), F32),
            pltpu.VMEM((16, LW), F32),
            pltpu.VMEM((NB * rows, 256), BF),
            pltpu.VMEM((NB, 256, 256), BF),
            pltpu.VMEM((NB, 256, 256), BF),
            pltpu.VMEM((NB, blocks + 2, rows, 256), BF),
            pltpu.VMEM((NB, blocks + 2, rows, 256), BF),
            pltpu.VMEM((NB, blocks, rows, LW), F32),
            pltpu.VMEM((NB, stamps // 2, rows, 256), BF),
            pltpu.VMEM((NB, stamps // 2, rows, LW), F32),
            pltpu.VMEM((rows // 8, 6 * PLANES * 8, packed), BF),
            pltpu.VMEM((rows // 8, 2 * PLANES * 8, packed), BF),
            pltpu.VMEM((rows * PLANES, 5 * LW), BF),
            pltpu.VMEM((strips, 24, LW), F32),
            pltpu.VMEM((rows, cols), F32),
            pltpu.VMEM((blocks + 2, rows + 2 * HALO, LW), F32),
            pltpu.VMEM((blocks + 1, rows, LW), F32),
            dma((dets,)), dma((dets,)), dma((2, dets)), dma((2, dets)), dma((2, dets)), dma((2, dets)),
            dma((strips,)), dma((strips,)), dma, dma, dma((4,)),
        ],
        compiler_params=pltpu.CompilerParams(
            collective_id=0, has_side_effects=True, vmem_limit_bytes=53 * 1024 * 1024
        ),
    )(
        science,
        template,
        *[pltpu.with_memory_space_constraint(v, pltpu.HBM) for v in (row_taps, col_taps, stamp_rows, stamp_cols)],
    )


def solution(mesh):
    return jax.shard_map(
        functools.partial(local, mesh.shape["det"], mesh.shape["strip"]),
        mesh=mesh,
        in_specs=(
            P("det", "strip", None),
            P(None, "strip", "det"),
            P(),
            P(),
            P("det", None),
            P("det", None),
        ),
        out_specs=(P("det", "strip", None), P("det", None)),
        check_vma=False,
    )
```

```python
import functools

import jax
import jax.numpy as jnp
from jax import lax
from jax.experimental import pallas as pl
from jax.experimental.pallas import tpu as pltpu
from jax.sharding import PartitionSpec as P

NB = 12
KS = 21
HS = 17
KH = 10
NU = 37
LW = 128
HALO = 16
SLOT = 64
PLANES = 16
FITTED = 14
ONE_PLANE = 12
SCI_PLANE = 13
RIDGE_WEIGHT = 1.0
HIGHEST_MODE = lax.Precision.HIGHEST
MESH = pl.DeviceIdType.MESH
BF = jnp.bfloat16
F32 = jnp.float32


def iota(shape, dim):
    return lax.broadcasted_iota(jnp.int32, shape, dim)


def split(value):
    high = value.astype(BF)
    return high, (value - high.astype(F32)).astype(BF)


def build_row_table(taps_ref, pad_ref, table_ref, rows):
    pad_ref[...] = jnp.zeros_like(pad_ref)
    pad_ref[:NB, :KS] = taps_ref[...]
    for b in range(NB):
        wide = jnp.broadcast_to(pad_ref[b : b + 1, :], (rows, LW))
        moved = pltpu.roll(wide, HALO - KH, 1, stride=1, stride_axis=0)
        high, low = split(moved)
        high, low = high.astype(F32), low.astype(F32)
        high = high + pltpu.roll(high, 64, 1)
        low = low + pltpu.roll(low, 64, 1)
        table_ref[b * rows : (b + 1) * rows, :LW] = high.astype(BF)
        table_ref[b * rows : (b + 1) * rows, LW:] = low.astype(BF)


def build_col_tables(taps_ref, pad_ref, table_ref, stamp_table_ref):
    pad_ref[...] = jnp.zeros_like(pad_ref)
    pad_ref[:NB, :KS] = taps_ref[...]
    lane, sub = iota((LW, LW), 1), iota((LW, LW), 0)
    same_slot = lane // SLOT == sub // SLOT
    for b in range(NB):
        wide = jnp.broadcast_to(pad_ref[b : b + 1, :], (LW, LW))
        moved = pltpu.roll(wide, 0, 1, stride=1, stride_axis=0)
        near = jnp.where(lane >= sub, moved, 0.0).T
        far = jnp.where(lane < sub, moved, 0.0).T
        for part, at in ((near, 0), (far, LW)):
            high, low = split(part)
            table_ref[b, at : at + LW, :LW] = high
            table_ref[b, at : at + LW, LW:] = low
        high, low = split(jnp.where(same_slot, near, 0.0))
        for at in (0, LW):
            stamp_table_ref[b, at : at + LW, :LW] = high
            stamp_table_ref[b, at : at + LW, LW:] = low


def row_filtered(row_table_ref, moved, rows):
    high, low = split(moved)
    stacked = jnp.concatenate([high, low, high, low], axis=0)
    size = NB // 2
    for base in (0, size):
        out = jnp.dot(row_table_ref[base * rows : (base + size) * rows, :], stacked, preferred_element_type=F32)
        yield base, [v.reshape(size, rows, moved.shape[1]) for v in split(out)]


def held_rows(width, first_row, rows, total_rows):
    sub = iota((2 * HALO + rows, width), 0)
    sky = first_row - HALO + sub
    return (sub >= HALO - KH) & (sub < HALO + rows + KH) & (sky >= 0) & (sky < total_rows)


def row_stage(sky_ref, row_table_ref, windows, places, rows):
    size = NB // 2
    lane = iota((2 * HALO + rows, LW), 1)
    moved = [pltpu.roll(jnp.where(lane < LW - KH, sky_ref[m + 1], sky_ref[m]), KH, 1) for m in places]
    moved = jnp.concatenate(moved, axis=1) if len(places) > 1 else moved[0]
    for base, pair in row_filtered(row_table_ref, moved, rows):
        for ref, val in zip(windows, pair):
            for i, m in enumerate(places):
                part = val[:, :, i * LW : (i + 1) * LW]
                ref[base : base + size, m + 1, :, :LW] = part
                ref[base : base + size, m, :, LW:] = part


def col_stage(windows, col_table_ref, resp_ref, rows, cols):
    blocks = cols // LW
    per = 8

    def body(b, carry):
        table = col_table_ref[b]
        for k in range(0, blocks, per):
            hi, lo = [ref[b, k + 1 : k + 1 + per].reshape(per * rows, 2 * LW) for ref in windows]
            out = jnp.dot(hi, table, preferred_element_type=F32) + jnp.dot(lo, table, preferred_element_type=F32)
            resp_ref[b, k : k + per] = (out[:, :LW] + out[:, LW:]).reshape(per, rows, LW)
        return carry

    lax.fori_loop(0, NB, body, 0, unroll=True)


def gather(ref, starts):
    tall = 3 * FITTED * 8
    picked = []
    for t, start in enumerate(starts):
        k = start // LW
        off = start - k * LW
        near, far = ref[k], ref[k + 1]
        both = jnp.where(iota(near.shape, 1) >= off, near, far)
        picked.append(pltpu.roll(both, lax.rem(SLOT * t - off + LW, LW), 1))
    return jnp.where(iota(picked[0].shape, 1) < SLOT, *picked)


def stamp_left(cols_ref, s, cols):
    return jnp.clip(cols_ref[0, s] - HS, 0, cols - 1)


def stamp_responses(sky_ref, row_table_ref, stamp_table_ref, win_ref, resp_ref, cols_ref, rows, cols):
    pairs = resp_ref.shape[1]
    size = NB // 2

    def body(u, carry):
        lefts = [stamp_left(cols_ref, 4 * u + t, cols) + (LW - KH) for t in range(4)]
        moved = jnp.concatenate([gather(sky_ref, lefts[:2]), gather(sky_ref, lefts[2:])], axis=1)
        for base, pair in row_filtered(row_table_ref, moved, rows):
            for part, val in enumerate(pair):
                for i in range(2):
                    win_ref[base : base + size, 2 * u + i, :, part * LW : (part + 1) * LW] = val[:, :, i * LW : (i + 1) * LW]
        return carry

    lax.fori_loop(0, pairs // 2, body, 0, unroll=True)

    def filt(b, carry):
        out = jnp.dot(win_ref[b].reshape(pairs * rows, 2 * LW), stamp_table_ref[b], preferred_element_type=F32)
        resp_ref[b] = (out[:, :LW] + out[:, LW:]).reshape(pairs, rows, LW)
        return carry

    lax.fori_loop(0, NB, filt, 0, unroll=True)


def pack_stamps(resp_ref, sci_ref, rows_ref, cols_ref, left_ref, right_ref, first_row, rows, cols):
    groups = rows // 8
    lane = iota((8, LW), 1)

    def body(q, carry):
        lefts = [stamp_left(cols_ref, 2 * q + t, cols) for t in range(2)]
        second = lane >= SLOT
        inside = lane - jnp.where(second, SLOT, 0)
        rowv = jnp.where(second, rows_ref[0, 2 * q + 1], rows_ref[0, 2 * q])
        xv = (jnp.where(second, lefts[1], lefts[0]) + inside).astype(F32) * (2.0 / cols) - 1.0
        sci = gather(sci_ref, lefts)
        at = pl.multiple_of(q * LW, LW)
        ones, zeros = jnp.ones((1, 8, LW), F32), jnp.zeros((PLANES - SCI_PLANE - 1, 8, LW), F32)
        for g in range(groups):
            near = slice(8 * g, 8 * g + 8)
            yv = first_row + 8 * g + iota((8, LW), 0)
            hit = ((jnp.abs(yv - rowv) <= HS) & (inside < 2 * HS + 1)).astype(F32)
            planes = jnp.concatenate([resp_ref[:, q, near, :], ones, sci[None, near, :], zeros], axis=0)
            high, low = split(planes.reshape(PLANES * 8, LW))
            right_ref[g, : PLANES * 8, pl.ds(at, LW)] = high
            right_ref[g, PLANES * 8 :, pl.ds(at, LW)] = low
            moment = planes[:FITTED] * hit[None]
            for m in range(3):
                if m:
                    moment = moment * xv[None]
                high, low = split(moment.reshape(FITTED * 8, LW))
                left_ref[g, m * FITTED * 8 : (m + 1) * FITTED * 8, pl.ds(at, LW)] = high
                left_ref[g, (m + 3) * FITTED * 8 : (m + 4) * FITTED * 8, pl.ds(at, LW)] = low
        return carry

    lax.fori_loop(0, resp_ref.shape[1], body, 0, unroll=4)


def build_maps(maps_ref, first_row, rows, total_rows):
    span = PLANES * 8
    plane, col = iota((span, LW), 0) // 8, iota((span, LW), 1)
    kind, base = col // 16, lax.rem(col, 16)
    match = plane == base
    real = match & (plane < NB)
    zero = jnp.zeros((span, LW), F32)
    plain = jnp.where(match & (kind == 0), 1.0, zero)
    in_x = jnp.where(real & (kind == 1), 1.0, zero)
    for g in range(rows // 8):
        y = (2.0 / total_rows) * (first_row + 8 * g + lax.rem(iota((span, LW), 0), 8)).astype(F32) - 1.0
        level = plain + jnp.where(real & (kind == 2), y, zero)
        for i, part in enumerate((level, in_x, level * y, in_x * y)):
            high, low = split(part)
            maps_ref[g * span : (g + 1) * span, i * LW : (i + 1) * LW] = high
            if i == 2:
                maps_ref[g * span : (g + 1) * span, 4 * LW :] = low


def normal_part(left_ref, right_ref, maps_ref, rows):
    span = PLANES * 8
    same_y = (lax.rem(iota((8, span), 1), 8) == iota((8, span), 0)).astype(F32)
    tall = 3 * FITTED * 8
    picked = []
    for g in range(rows // 8):
        out = lax.dot_general(left_ref[g], right_ref[g], (((1,), (1,)), ((), ())), preferred_element_type=F32)
        folded = out[:tall, :span] + out[:tall, span:] + out[tall:, :span]
        picked.append(jnp.sum(folded.reshape(3 * FITTED, 8, span) * same_y[None], axis=1))
    sums = jnp.concatenate(picked, axis=1)
    gap = jnp.zeros((PLANES - FITTED, sums.shape[1]), F32)
    sums = jnp.concatenate([v for m in range(3) for v in (sums[m * FITTED : (m + 1) * FITTED], gap)], axis=0)
    high, low = split(sums)
    lower = (sums - high.astype(F32) - low.astype(F32)).astype(BF)
    total = jnp.dot(jnp.concatenate([high, low, lower], axis=0), maps_ref[...], preferred_element_type=F32)
    total = total[:48] + total[48:96] + total[96:]
    squared = total[:, 2 * LW : 3 * LW] + total[:, 4 * LW :]
    whole = jnp.concatenate(
        [
            total[0:16, 0:LW] + total[16:32, LW : 2 * LW],
            total[16:32, 0:LW] + total[32:48, LW : 2 * LW],
            squared[0:16] + total[16:32, 3 * LW : 4 * LW],
        ],
        axis=0,
    )
    return jnp.where(iota((24, LW), 1) < LW // 2, whole[:24], pltpu.roll(whole[24:], LW // 2, 1))


def unfolded(halves):
    return jnp.concatenate([halves, pltpu.roll(halves, LW // 2, 1)], axis=0)


PIVOTS = [*range(0, 13), *range(16, 28), *range(32, 44)]


def solve(normal):
    sub, lane = iota((48, LW), 0), iota((48, LW), 1)
    live = (lax.rem(sub, 16) < NB) | (sub == ONE_PLANE)
    mat = jnp.where((sub == lane) & live, normal + RIDGE_WEIGHT, normal)
    at = lambda value, k: value[k : k + 1, :]

    def pair(first, second, tops, lows):
        scale = 1.0 / (first[0] * second[1] - first[1] * second[0])
        return [
            ((second[1] * t - first[1] * w) * scale, (first[0] * w - second[0] * t) * scale) for t, w in zip(tops, lows)
        ]

    for i in range(0, NU - 1, 4):
        picks = PIVOTS[i : i + 4]
        columns = [jnp.broadcast_to(mat[:, k : k + 1], (48, LW)) for k in picks]
        rows = [[at(c, k) for c in columns] + [at(mat, k)] for k in picks]
        upper = pair(rows[0], rows[1], rows[0][2:], rows[1][2:])
        rest = [[r[2 + j] - r[0] * t - r[1] * w for j, (t, w) in enumerate(upper)] for r in rows[2:]]
        ((third, fourth),) = pair(rest[0], rest[1], rest[0][2:], rest[1][2:])
        first = upper[2][0] - upper[0][0] * third - upper[1][0] * fourth
        second = upper[2][1] - upper[0][1] * third - upper[1][1] * fourth
        solved = [first, second, third, fourth]
        left = mat
        for c, r in zip(columns, solved):
            left = left - c * r
        for k, r in zip(picks, solved):
            left = jnp.where(sub == k, r, left)
        mat = left
    k = PIVOTS[-1]
    column = jnp.broadcast_to(mat[:, k : k + 1], (48, LW))
    row = at(mat, k) / at(column, k)
    mat = jnp.where(sub == k, row, mat - column * row)
    return mat[:, SCI_PLANE : SCI_PLANE + 1]


def coeff_row(answer):
    sub, lane = iota((48, LW), 0), iota((48, LW), 1)
    kind, base = sub // 16, lax.rem(sub, 16)
    goes = jnp.where(base < NB, kind * NB + base, jnp.where(sub == ONE_PLANE, NU - 1, -1))
    return jnp.sum(jnp.where(goes == lane, answer, 0.0), axis=0, keepdims=True)


def apply_model(answer, resp_ref, sci_ref, out_ref, first_row, rows, total_rows, cols):
    wide = jnp.broadcast_to(answer, (48, LW))
    lift = lambda i: jnp.broadcast_to(wide[i : i + 1, :], (8, LW))
    blocks = cols // LW
    const = lift(ONE_PLANE)
    for g in range(rows // 8):
        y = (2.0 / total_rows) * (first_row + 8 * g + iota((8, LW), 0)).astype(F32) - 1.0
        level = [lift(b) + y * lift(32 + b) for b in range(NB)]
        slope = [lift(16 + b) for b in range(NB)]

        def body(k, carry):
            flat = const
            tilt = jnp.zeros((8, LW), F32)
            for b in range(NB):
                r = resp_ref[b, k, 8 * g : 8 * g + 8, :]
                flat = flat + level[b] * r
                tilt = tilt + slope[b] * r
            at = pl.multiple_of(k * LW, LW)
            x = (k * LW + iota((8, LW), 1)).astype(F32) * (2.0 / cols) - 1.0
            out_ref[0, 8 * g : 8 * g + 8, pl.ds(at, LW)] = sci_ref[k, 8 * g : 8 * g + 8, :] - (flat + x * tilt)
            return carry

        lax.fori_loop(0, blocks, body, 0, unroll=4)


def kernel(
    dets, strips,
    sci_ref, tmpl_ref, row_in, col_in, srow_in, scol_in,
    out_ref, coef_ref,
    row_ref, col_ref, srow_ref, scol_ref,
    frame, pad, row_table, col_table, stamp_table, win_hi, win_lo, resp, stamp_win, stamp_resp, left, right, maps, parts, sci_buf, sky, sci,
    main_send, main_recv, up_send, up_recv, down_send, down_recv, part_send, part_recv, own_sem, sci_sem, small_sem,
):
    _, rows, cols = sci_ref.shape
    width = tmpl_ref.shape[2]
    total_rows = rows * strips
    det, strip = lax.axis_index("det"), lax.axis_index("strip")
    above, below = strip > 0, strip < strips - 1
    first_row = strip * rows

    small = [
        pltpu.make_async_copy(a, b, small_sem.at[i])
        for i, (a, b) in enumerate(((row_in, row_ref), (col_in, col_ref), (srow_in, srow_ref), (scol_in, scol_ref)))
    ]
    for copy in small:
        copy.start()

    barrier = pltpu.get_barrier_semaphore()

    def greet(target_det, target_strip):
        pl.semaphore_signal(barrier, inc=1, device_id=(target_det, target_strip), device_id_type=MESH)

    for i in range(1, dets):
        greet(lax.rem(det + i, dets), strip)

    @pl.when(above)
    def _():
        for i in range(dets):
            greet(lax.rem(det + i, dets), strip - 1)

    @pl.when(below)
    def _():
        for i in range(dets):
            greet(lax.rem(det + i, dets), strip + 1)

    for i in range(2, strips - 1):
        other = lax.rem(strip + i, strips)

        @pl.when((other != strip - 1) & (other != strip + 1))
        def _():
            greet(det, other)

    @pl.when(strip == 0)
    def _():
        greet(det, strips - 1)

    @pl.when(strip == strips - 1)
    def _():
        greet(det, 0)

    ends = jnp.where(above & below, 0, 1)
    count = (dets - 1) + dets * (2 - ends) + (strips - 3 + ends)
    pl.semaphore_wait(barrier, count)

    here = pl.ds(pl.multiple_of(det * width, width), width)

    def main_copy(i):
        target = lax.rem(det + dets - i, dets)
        return pltpu.make_async_remote_copy(
            tmpl_ref.at[target], frame.at[pl.ds(HALO, rows), here],
            main_send.at[i], main_recv.at[i], device_id=(target, strip), device_id_type=MESH,
        )

    ups = ((0, 8), (8, KH - 8))
    downs = ((rows - 8, 8), (rows - KH, KH - 8))

    def up_copy(i, p):
        target = lax.rem(det + dets - i, dets)
        at, size = ups[p]
        return pltpu.make_async_remote_copy(
            tmpl_ref.at[target, pl.ds(at, size), :], frame.at[pl.ds(HALO + rows + at, size), here],
            up_send.at[p, i], up_recv.at[p, i], device_id=(target, strip - 1), device_id_type=MESH,
        )

    def down_copy(i, p):
        target = lax.rem(det + dets - i, dets)
        at, size = downs[p]
        return pltpu.make_async_remote_copy(
            tmpl_ref.at[target, pl.ds(at, size), :], frame.at[pl.ds(HALO - rows + at, size), here],
            down_send.at[p, i], down_recv.at[p, i], device_id=(target, strip + 1), device_id_type=MESH,
        )

    own = pltpu.make_async_copy(
        tmpl_ref.at[det], frame.at[pl.ds(HALO, rows), here], own_sem
    )
    own.start()
    sci_copy = pltpu.make_async_copy(sci_ref.at[0], sci_buf, sci_sem)
    sci_copy.start()
    for i in range(dets):
        if i:
            main_copy(i).start()

        @pl.when(above)
        def _():
            up_copy(i, 0).start()
            up_copy(i, 1).start()

        @pl.when(below)
        def _():
            down_copy(i, 0).start()
            down_copy(i, 1).start()

    blocks = cols // LW
    sky[0] = jnp.zeros((2 * HALO + rows, LW), F32)
    sky[blocks + 1] = jnp.zeros((2 * HALO + rows, LW), F32)
    sci[blocks] = jnp.zeros((rows, LW), F32)
    for copy in small:
        copy.wait()
    build_row_table(row_ref, pad, row_table, rows)
    build_col_tables(col_ref, pad, col_table, stamp_table)
    build_maps(maps, first_row, rows, total_rows)
    sci_copy.wait()
    for k in range(blocks):
        sci[k] = sci_buf[:, k * LW : (k + 1) * LW]
    held = held_rows(LW, first_row, rows, total_rows)
    windows = (win_hi, win_lo)
    half = width // LW

    def received(i):
        @pl.when(above)
        def _():
            for p in range(2):
                down_copy(i, p).wait_recv()

        @pl.when(below)
        def _():
            for p in range(2):
                up_copy(i, p).wait_recv()

        first = half * lax.rem(det + i, dets)
        for t in range(half):
            sky[first + t + 1] = jnp.where(held, frame[:, pl.ds(pl.multiple_of((first + t) * LW, LW), LW)], 0.0)

    def place(n):
        return lax.rem(half * det + 1 + n, blocks + 1)

    def arrive(i, carry):
        main_copy(i).wait_recv()
        received(i)
        row_stage(sky, row_table, windows, [place(half * (i - 1) + t) for t in range(half)], rows)
        return carry

    own.wait()
    received(0)
    lax.fori_loop(1, dets - 1, arrive, 0)
    main_copy(dets - 1).wait_recv()
    received(dets - 1)
    stamp_responses(sky, row_table, stamp_table, stamp_win, stamp_resp, scol_ref, rows, cols)
    pack_stamps(stamp_resp, sci, srow_ref, scol_ref, left, right, first_row, rows, cols)
    parts[strip] = normal_part(left, right, maps, rows)

    def part_copy(i):
        return pltpu.make_async_remote_copy(
            parts.at[strip], parts.at[strip], part_send.at[i], part_recv.at[i],
            device_id=(det, lax.rem(strip + i, strips)), device_id_type=MESH,
        )

    for i in range(1, strips):
        part_copy(i).start()
    done = half * (dets - 2)
    row_stage(sky, row_table, windows, [place(done + t) for t in range(2)], rows)
    row_stage(sky, row_table, windows, [place(done + 2 + t) for t in range(2)], rows)
    row_stage(sky, row_table, windows, [place(blocks)], rows)
    col_stage(windows, col_table, resp, rows, cols)
    for i in range(1, strips):
        source = lax.rem(strip + strips - i, strips)
        part_copy(i).wait_send()
        pltpu.make_async_remote_copy(
            parts.at[source], parts.at[source], part_send.at[i], part_recv.at[i],
            device_id=(det, source), device_id_type=MESH,
        ).wait_recv()
    for i in range(dets):
        if i:
            main_copy(i).wait_send()

        @pl.when(above)
        def _():
            for p in range(2):
                up_copy(i, p).wait_send()

        @pl.when(below)
        def _():
            for p in range(2):
                down_copy(i, p).wait_send()

    normal = parts[0]
    for i in range(1, strips):
        normal = normal + parts[i]
    answer = solve(unfolded(normal))
    coef_ref[...] = coeff_row(answer)[:, :NU]
    apply_model(answer, resp, sci, out_ref, first_row, rows, total_rows, cols)


def local(dets, strips, science, template, row_taps, col_taps, stamp_rows, stamp_cols):
    _, rows, cols = science.shape
    blocks = cols // LW
    stamps = stamp_rows.shape[1]
    packed = stamps // 2 * LW
    any_space = pl.BlockSpec(memory_space=pl.ANY)
    vmem = pl.BlockSpec(memory_space=pltpu.VMEM)
    hbm = pl.BlockSpec(memory_space=pltpu.HBM)
    dma = pltpu.SemaphoreType.DMA
    results = (jax.ShapeDtypeStruct(science.shape, F32), jax.ShapeDtypeStruct((1, NU), F32))
    return pl.pallas_call(
        functools.partial(kernel, dets, strips),
        out_shape=(pltpu.VMEM(science.shape, F32), pltpu.VMEM((1, NU), F32)),
        in_specs=[hbm] * 6,
        out_specs=(vmem, vmem),
        scratch_shapes=[
            pltpu.VMEM((NB, KS), F32),
            pltpu.VMEM((NB, KS), F32),
            pltpu.SMEM((1, stamps), jnp.int32),
            pltpu.SMEM((1, stamps), jnp.int32),
            pltpu.VMEM((rows + 2 * HALO, cols), F32),
            pltpu.VMEM((16, LW), F32),
            pltpu.VMEM((NB * rows, 256), BF),
            pltpu.VMEM((NB, 256, 256), BF),
            pltpu.VMEM((NB, 256, 256), BF),
            pltpu.VMEM((NB, blocks + 2, rows, 256), BF),
            pltpu.VMEM((NB, blocks + 2, rows, 256), BF),
            pltpu.VMEM((NB, blocks, rows, LW), F32),
            pltpu.VMEM((NB, stamps // 2, rows, 256), BF),
            pltpu.VMEM((NB, stamps // 2, rows, LW), F32),
            pltpu.VMEM((rows // 8, 6 * FITTED * 8, packed), BF),
            pltpu.VMEM((rows // 8, 2 * PLANES * 8, packed), BF),
            pltpu.VMEM((rows * PLANES, 5 * LW), BF),
            pltpu.VMEM((strips, 24, LW), F32),
            pltpu.VMEM((rows, cols), F32),
            pltpu.VMEM((blocks + 2, rows + 2 * HALO, LW), F32),
            pltpu.VMEM((blocks + 1, rows, LW), F32),
            dma((dets,)), dma((dets,)), dma((2, dets)), dma((2, dets)), dma((2, dets)), dma((2, dets)),
            dma((strips,)), dma((strips,)), dma, dma, dma((4,)),
        ],
        compiler_params=pltpu.CompilerParams(
            collective_id=0, has_side_effects=True, vmem_limit_bytes=53 * 1024 * 1024
        ),
    )(
        science,
        template,
        *[pltpu.with_memory_space_constraint(v, pltpu.HBM) for v in (row_taps, col_taps, stamp_rows, stamp_cols)],
    )


def solution(mesh):
    return jax.shard_map(
        functools.partial(local, mesh.shape["det"], mesh.shape["strip"]),
        mesh=mesh,
        in_specs=(
            P("det", "strip", None),
            P(None, "strip", "det"),
            P(),
            P(),
            P("det", None),
            P("det", None),
        ),
        out_specs=(P("det", "strip", None), P("det", None)),
        check_vma=False,
    )
```

```python
import functools

import jax
import jax.numpy as jnp
from jax import lax
from jax.experimental import pallas as pl
from jax.experimental.pallas import tpu as pltpu
from jax.sharding import PartitionSpec as P

NB = 12
KS = 21
HS = 17
KH = 10
NU = 37
LW = 128
HALO = 16
SLOT = 64
PLANES = 16
FITTED = 14
ONE_PLANE = 12
SCI_PLANE = 13
RIDGE_WEIGHT = 1.0
HIGHEST_MODE = lax.Precision.HIGHEST
MESH = pl.DeviceIdType.MESH
BF = jnp.bfloat16
F32 = jnp.float32


def iota(shape, dim):
    return lax.broadcasted_iota(jnp.int32, shape, dim)


def split(value):
    high = value.astype(BF)
    return high, (value - high.astype(F32)).astype(BF)


def build_row_table(taps_ref, pad_ref, table_ref, rows):
    pad_ref[...] = jnp.zeros_like(pad_ref)
    pad_ref[:NB, :KS] = taps_ref[...]
    for b in range(NB):
        wide = jnp.broadcast_to(pad_ref[b : b + 1, :], (rows, LW))
        moved = pltpu.roll(wide, HALO - KH, 1, stride=1, stride_axis=0)
        high, low = split(moved)
        high, low = high.astype(F32), low.astype(F32)
        high = high + pltpu.roll(high, 64, 1)
        low = low + pltpu.roll(low, 64, 1)
        table_ref[b * rows : (b + 1) * rows, :LW] = high.astype(BF)
        table_ref[b * rows : (b + 1) * rows, LW:] = low.astype(BF)


def build_col_tables(taps_ref, pad_ref, table_ref, stamp_table_ref):
    pad_ref[...] = jnp.zeros_like(pad_ref)
    pad_ref[:NB, :KS] = taps_ref[...]
    lane, sub = iota((LW, LW), 1), iota((LW, LW), 0)
    same_slot = lane // SLOT == sub // SLOT
    for b in range(NB):
        wide = jnp.broadcast_to(pad_ref[b : b + 1, :], (LW, LW))
        moved = pltpu.roll(wide, 0, 1, stride=1, stride_axis=0)
        near = jnp.where(lane >= sub, moved, 0.0).T
        far = jnp.where(lane < sub, moved, 0.0).T
        for part, at in ((near, 0), (far, LW)):
            high, low = split(part)
            table_ref[b, at : at + LW, :LW] = high
            table_ref[b, at : at + LW, LW:] = low
        high, low = split(jnp.where(same_slot, near, 0.0))
        for at in (0, LW):
            stamp_table_ref[b, at : at + LW, :LW] = high
            stamp_table_ref[b, at : at + LW, LW:] = low


def row_filtered(row_table_ref, moved, rows):
    high, low = split(moved)
    stacked = jnp.concatenate([high, low, high, low], axis=0)
    size = NB // 2
    for base in (0, size):
        out = jnp.dot(row_table_ref[base * rows : (base + size) * rows, :], stacked, preferred_element_type=F32)
        yield base, [v.reshape(size, rows, moved.shape[1]) for v in split(out)]


def held_rows(width, first_row, rows, total_rows):
    sub = iota((2 * HALO + rows, width), 0)
    sky = first_row - HALO + sub
    return (sub >= HALO - KH) & (sub < HALO + rows + KH) & (sky >= 0) & (sky < total_rows)


def row_stage(sky_ref, row_table_ref, windows, places, rows):
    size = NB // 2
    lane = iota((2 * HALO + rows, LW), 1)
    moved = [pltpu.roll(jnp.where(lane < LW - KH, sky_ref[m + 1], sky_ref[m]), KH, 1) for m in places]
    moved = jnp.concatenate(moved, axis=1) if len(places) > 1 else moved[0]
    for base, pair in row_filtered(row_table_ref, moved, rows):
        for ref, val in zip(windows, pair):
            for i, m in enumerate(places):
                part = val[:, :, i * LW : (i + 1) * LW]
                ref[base : base + size, m + 1, :, :LW] = part
                ref[base : base + size, m, :, LW:] = part


def col_stage(windows, col_table_ref, resp_ref, rows, cols):
    blocks = cols // LW
    per = 8

    def body(b, carry):
        table = col_table_ref[b]
        for k in range(0, blocks, per):
            hi, lo = [ref[b, k + 1 : k + 1 + per].reshape(per * rows, 2 * LW) for ref in windows]
            out = jnp.dot(hi, table, preferred_element_type=F32) + jnp.dot(lo, table, preferred_element_type=F32)
            resp_ref[b, k : k + per] = (out[:, :LW] + out[:, LW:]).reshape(per, rows, LW)
        return carry

    lax.fori_loop(0, NB, body, 0, unroll=True)


def gather(ref, starts):
    tall = 3 * FITTED * 8
    picked = []
    for t, start in enumerate(starts):
        k = start // LW
        off = start - k * LW
        near, far = ref[k], ref[k + 1]
        both = jnp.where(iota(near.shape, 1) >= off, near, far)
        picked.append(pltpu.roll(both, lax.rem(SLOT * t - off + LW, LW), 1))
    return jnp.where(iota(picked[0].shape, 1) < SLOT, *picked)


def stamp_left(cols_ref, s, cols):
    return jnp.clip(cols_ref[0, s] - HS, 0, cols - 1)


def stamp_responses(sky_ref, row_table_ref, stamp_table_ref, win_ref, resp_ref, cols_ref, rows, cols):
    pairs = resp_ref.shape[1]
    size = NB // 2

    def body(u, carry):
        lefts = [stamp_left(cols_ref, 4 * u + t, cols) + (LW - KH) for t in range(4)]
        moved = jnp.concatenate([gather(sky_ref, lefts[:2]), gather(sky_ref, lefts[2:])], axis=1)
        for base, pair in row_filtered(row_table_ref, moved, rows):
            for part, val in enumerate(pair):
                for i in range(2):
                    win_ref[base : base + size, 2 * u + i, :, part * LW : (part + 1) * LW] = val[:, :, i * LW : (i + 1) * LW]
        return carry

    lax.fori_loop(0, pairs // 2, body, 0, unroll=True)

    def filt(b, carry):
        out = jnp.dot(win_ref[b].reshape(pairs * rows, 2 * LW), stamp_table_ref[b], preferred_element_type=F32)
        resp_ref[b] = (out[:, :LW] + out[:, LW:]).reshape(pairs, rows, LW)
        return carry

    lax.fori_loop(0, NB, filt, 0, unroll=True)


def pack_stamps(resp_ref, sci_ref, rows_ref, cols_ref, left_ref, right_ref, first_row, rows, cols):
    groups = rows // 8
    lane = iota((8, LW), 1)

    def body(q, carry):
        lefts = [stamp_left(cols_ref, 2 * q + t, cols) for t in range(2)]
        second = lane >= SLOT
        inside = lane - jnp.where(second, SLOT, 0)
        rowv = jnp.where(second, rows_ref[0, 2 * q + 1], rows_ref[0, 2 * q])
        xv = (jnp.where(second, lefts[1], lefts[0]) + inside).astype(F32) * (2.0 / cols) - 1.0
        sci = gather(sci_ref, lefts)
        at = pl.multiple_of(q * LW, LW)
        ones, zeros = jnp.ones((1, 8, LW), F32), jnp.zeros((PLANES - SCI_PLANE - 1, 8, LW), F32)
        for g in range(groups):
            near = slice(8 * g, 8 * g + 8)
            yv = first_row + 8 * g + iota((8, LW), 0)
            hit = ((jnp.abs(yv - rowv) <= HS) & (inside < 2 * HS + 1)).astype(F32)
            planes = jnp.concatenate([resp_ref[:, q, near, :], ones, sci[None, near, :], zeros], axis=0)
            high, low = split(planes.reshape(PLANES * 8, LW))
            right_ref[g, : PLANES * 8, pl.ds(at, LW)] = high
            right_ref[g, PLANES * 8 :, pl.ds(at, LW)] = low
            moment = planes[:FITTED] * hit[None]
            for m in range(3):
                if m:
                    moment = moment * xv[None]
                high, low = split(moment.reshape(FITTED * 8, LW))
                left_ref[g, m * FITTED * 8 : (m + 1) * FITTED * 8, pl.ds(at, LW)] = high
                left_ref[g, (m + 3) * FITTED * 8 : (m + 4) * FITTED * 8, pl.ds(at, LW)] = low
        return carry

    lax.fori_loop(0, resp_ref.shape[1], body, 0, unroll=4)


def build_maps(maps_ref, first_row, rows, total_rows):
    span = PLANES * 8
    plane, col = iota((span, LW), 0) // 8, iota((span, LW), 1)
    kind, base = col // 16, lax.rem(col, 16)
    match = plane == base
    real = match & (plane < NB)
    zero = jnp.zeros((span, LW), F32)
    plain = jnp.where(match & (kind == 0), 1.0, zero)
    in_x = jnp.where(real & (kind == 1), 1.0, zero)
    for g in range(rows // 8):
        y = (2.0 / total_rows) * (first_row + 8 * g + lax.rem(iota((span, LW), 0), 8)).astype(F32) - 1.0
        level = plain + jnp.where(real & (kind == 2), y, zero)
        for i, part in enumerate((level, in_x, level * y, in_x * y)):
            high, low = split(part)
            maps_ref[g * span : (g + 1) * span, i * LW : (i + 1) * LW] = high
            if i == 2:
                maps_ref[g * span : (g + 1) * span, 4 * LW :] = low


def normal_part(left_ref, right_ref, maps_ref, rows):
    span = PLANES * 8
    same_y = (lax.rem(iota((8, span), 1), 8) == iota((8, span), 0)).astype(F32)
    tall = 3 * FITTED * 8
    picked = []
    for g in range(rows // 8):
        out = lax.dot_general(left_ref[g], right_ref[g], (((1,), (1,)), ((), ())), preferred_element_type=F32)
        folded = out[:tall, :span] + out[:tall, span:] + out[tall:, :span]
        picked.append(jnp.sum(folded.reshape(3 * FITTED, 8, span) * same_y[None], axis=1))
    sums = jnp.concatenate(picked, axis=1)
    gap = jnp.zeros((PLANES - FITTED, sums.shape[1]), F32)
    sums = jnp.concatenate([v for m in range(3) for v in (sums[m * FITTED : (m + 1) * FITTED], gap)], axis=0)
    high, low = split(sums)
    lower = (sums - high.astype(F32) - low.astype(F32)).astype(BF)
    total = jnp.dot(jnp.concatenate([high, low, lower], axis=0), maps_ref[...], preferred_element_type=F32)
    total = total[:48] + total[48:96] + total[96:]
    squared = total[:, 2 * LW : 3 * LW] + total[:, 4 * LW :]
    whole = jnp.concatenate(
        [
            total[0:16, 0:LW] + total[16:32, LW : 2 * LW],
            total[16:32, 0:LW] + total[32:48, LW : 2 * LW],
            squared[0:16] + total[16:32, 3 * LW : 4 * LW],
        ],
        axis=0,
    )
    return jnp.where(iota((24, LW), 1) < LW // 2, whole[:24], pltpu.roll(whole[24:], LW // 2, 1))


def unfolded(halves):
    return jnp.concatenate([halves, pltpu.roll(halves, LW // 2, 1)], axis=0)


PIVOTS = [*range(0, 13), *range(16, 28), *range(32, 44)]


def solve(normal):
    sub, lane = iota((48, LW), 0), iota((48, LW), 1)
    live = (lax.rem(sub, 16) < NB) | (sub == ONE_PLANE)
    mat = jnp.where((sub == lane) & live, normal + RIDGE_WEIGHT, normal)
    at = lambda value, k: value[k : k + 1, :]

    def pair(first, second, tops, lows):
        scale = 1.0 / (first[0] * second[1] - first[1] * second[0])
        return [
            ((second[1] * t - first[1] * w) * scale, (first[0] * w - second[0] * t) * scale) for t, w in zip(tops, lows)
        ]

    for i in range(0, NU - 1, 4):
        picks = PIVOTS[i : i + 4]
        columns = [jnp.broadcast_to(mat[:, k : k + 1], (48, LW)) for k in picks]
        rows = [[at(c, k) for c in columns] + [at(mat, k)] for k in picks]
        upper = pair(rows[0], rows[1], rows[0][2:], rows[1][2:])
        rest = [[r[2 + j] - r[0] * t - r[1] * w for j, (t, w) in enumerate(upper)] for r in rows[2:]]
        ((third, fourth),) = pair(rest[0], rest[1], rest[0][2:], rest[1][2:])
        first = upper[2][0] - upper[0][0] * third - upper[1][0] * fourth
        second = upper[2][1] - upper[0][1] * third - upper[1][1] * fourth
        solved = [first, second, third, fourth]
        left = mat
        for c, r in zip(columns, solved):
            left = left - c * r
        for k, r in zip(picks, solved):
            left = jnp.where(sub == k, r, left)
        mat = left
    k = PIVOTS[-1]
    column = jnp.broadcast_to(mat[:, k : k + 1], (48, LW))
    row = at(mat, k) / at(column, k)
    mat = jnp.where(sub == k, row, mat - column * row)
    return mat[:, SCI_PLANE : SCI_PLANE + 1]


def coeff_row(answer):
    sub, lane = iota((48, LW), 0), iota((48, LW), 1)
    kind, base = sub // 16, lax.rem(sub, 16)
    goes = jnp.where(base < NB, kind * NB + base, jnp.where(sub == ONE_PLANE, NU - 1, -1))
    return jnp.sum(jnp.where(goes == lane, answer, 0.0), axis=0, keepdims=True)


def apply_model(answer, resp_ref, sci_ref, out_ref, first_row, rows, total_rows, cols):
    wide = jnp.broadcast_to(answer, (48, LW))
    lift = lambda i: jnp.broadcast_to(wide[i : i + 1, :], (8, LW))
    blocks = cols // LW
    const = lift(ONE_PLANE)
    for g in range(rows // 8):
        y = (2.0 / total_rows) * (first_row + 8 * g + iota((8, LW), 0)).astype(F32) - 1.0
        level = [lift(b) + y * lift(32 + b) for b in range(NB)]
        slope = [lift(16 + b) for b in range(NB)]

        def body(k, carry):
            flat = const
            tilt = jnp.zeros((8, LW), F32)
            for b in range(NB):
                r = resp_ref[b, k, 8 * g : 8 * g + 8, :]
                flat = flat + level[b] * r
                tilt = tilt + slope[b] * r
            at = pl.multiple_of(k * LW, LW)
            x = (k * LW + iota((8, LW), 1)).astype(F32) * (2.0 / cols) - 1.0
            out_ref[0, 8 * g : 8 * g + 8, pl.ds(at, LW)] = sci_ref[k, 8 * g : 8 * g + 8, :] - (flat + x * tilt)
            return carry

        lax.fori_loop(0, blocks, body, 0, unroll=4)


def kernel(
    dets, strips,
    sci_ref, tmpl_ref, row_in, col_in, srow_in, scol_in,
    out_ref, coef_ref,
    row_ref, col_ref, srow_ref, scol_ref,
    frame, pad, row_table, col_table, stamp_table, win_hi, win_lo, resp, stamp_win, stamp_resp, left, right, maps, parts, sci_buf, sky, sci,
    main_send, main_recv, up_send, up_recv, down_send, down_recv, part_send, part_recv, own_sem, sci_sem, small_sem,
):
    _, rows, cols = sci_ref.shape
    width = tmpl_ref.shape[2]
    total_rows = rows * strips
    det, strip = lax.axis_index("det"), lax.axis_index("strip")
    above, below = strip > 0, strip < strips - 1
    first_row = strip * rows

    small = [
        pltpu.make_async_copy(a, b, small_sem.at[i])
        for i, (a, b) in enumerate(((row_in, row_ref), (col_in, col_ref), (srow_in, srow_ref), (scol_in, scol_ref)))
    ]
    for copy in small:
        copy.start()
    here = pl.ds(pl.multiple_of(det * width, width), width)
    own = pltpu.make_async_copy(
        tmpl_ref.at[det], frame.at[pl.ds(HALO, rows), here], own_sem
    )
    own.start()
    sci_copy = pltpu.make_async_copy(sci_ref.at[0], sci_buf, sci_sem)
    sci_copy.start()

    barrier = pltpu.get_barrier_semaphore()

    def greet(target_det, target_strip):
        pl.semaphore_signal(barrier, inc=1, device_id=(target_det, target_strip), device_id_type=MESH)

    for i in range(1, dets):
        greet(lax.rem(det + i, dets), strip)

    @pl.when(above)
    def _():
        for i in range(dets):
            greet(lax.rem(det + i, dets), strip - 1)

    @pl.when(below)
    def _():
        for i in range(dets):
            greet(lax.rem(det + i, dets), strip + 1)

    for i in range(2, strips - 1):
        other = lax.rem(strip + i, strips)

        @pl.when((other != strip - 1) & (other != strip + 1))
        def _():
            greet(det, other)

    @pl.when(strip == 0)
    def _():
        greet(det, strips - 1)

    @pl.when(strip == strips - 1)
    def _():
        greet(det, 0)

    ends = jnp.where(above & below, 0, 1)
    count = (dets - 1) + dets * (2 - ends) + (strips - 3 + ends)
    pl.semaphore_wait(barrier, count)


    def main_copy(i):
        target = lax.rem(det + dets - i, dets)
        return pltpu.make_async_remote_copy(
            tmpl_ref.at[target], frame.at[pl.ds(HALO, rows), here],
            main_send.at[i], main_recv.at[i], device_id=(target, strip), device_id_type=MESH,
        )

    ups = ((0, 8), (8, KH - 8))
    downs = ((rows - 8, 8), (rows - KH, KH - 8))

    def up_copy(i, p):
        target = lax.rem(det + dets - i, dets)
        at, size = ups[p]
        return pltpu.make_async_remote_copy(
            tmpl_ref.at[target, pl.ds(at, size), :], frame.at[pl.ds(HALO + rows + at, size), here],
            up_send.at[p, i], up_recv.at[p, i], device_id=(target, strip - 1), device_id_type=MESH,
        )

    def down_copy(i, p):
        target = lax.rem(det + dets - i, dets)
        at, size = downs[p]
        return pltpu.make_async_remote_copy(
            tmpl_ref.at[target, pl.ds(at, size), :], frame.at[pl.ds(HALO - rows + at, size), here],
            down_send.at[p, i], down_recv.at[p, i], device_id=(target, strip + 1), device_id_type=MESH,
        )

    for i in range(dets):
        if i:
            main_copy(i).start()

        @pl.when(above)
        def _():
            up_copy(i, 0).start()
            up_copy(i, 1).start()

        @pl.when(below)
        def _():
            down_copy(i, 0).start()
            down_copy(i, 1).start()

    blocks = cols // LW
    sky[0] = jnp.zeros((2 * HALO + rows, LW), F32)
    sky[blocks + 1] = jnp.zeros((2 * HALO + rows, LW), F32)
    sci[blocks] = jnp.zeros((rows, LW), F32)
    for copy in small:
        copy.wait()
    build_row_table(row_ref, pad, row_table, rows)
    build_col_tables(col_ref, pad, col_table, stamp_table)
    build_maps(maps, first_row, rows, total_rows)
    sci_copy.wait()
    for k in range(blocks):
        sci[k] = sci_buf[:, k * LW : (k + 1) * LW]
    held = held_rows(LW, first_row, rows, total_rows)
    windows = (win_hi, win_lo)
    half = width // LW

    def received(i):
        @pl.when(above)
        def _():
            for p in range(2):
                down_copy(i, p).wait_recv()

        @pl.when(below)
        def _():
            for p in range(2):
                up_copy(i, p).wait_recv()

        first = half * lax.rem(det + i, dets)
        for t in range(half):
            sky[first + t + 1] = jnp.where(held, frame[:, pl.ds(pl.multiple_of((first + t) * LW, LW), LW)], 0.0)

    def place(n):
        return lax.rem(half * det + 1 + n, blocks + 1)

    def arrive(i, carry):
        main_copy(i).wait_recv()
        received(i)
        row_stage(sky, row_table, windows, [place(half * (i - 1) + t) for t in range(half)], rows)
        return carry

    own.wait()
    received(0)
    lax.fori_loop(1, dets - 1, arrive, 0)
    main_copy(dets - 1).wait_recv()
    received(dets - 1)
    stamp_responses(sky, row_table, stamp_table, stamp_win, stamp_resp, scol_ref, rows, cols)
    pack_stamps(stamp_resp, sci, srow_ref, scol_ref, left, right, first_row, rows, cols)
    parts[strip] = normal_part(left, right, maps, rows)

    def part_copy(i):
        return pltpu.make_async_remote_copy(
            parts.at[strip], parts.at[strip], part_send.at[i], part_recv.at[i],
            device_id=(det, lax.rem(strip + i, strips)), device_id_type=MESH,
        )

    for i in range(1, strips):
        part_copy(i).start()
    done = half * (dets - 2)
    row_stage(sky, row_table, windows, [place(done + t) for t in range(2)], rows)
    row_stage(sky, row_table, windows, [place(done + 2 + t) for t in range(2)], rows)
    row_stage(sky, row_table, windows, [place(blocks)], rows)
    col_stage(windows, col_table, resp, rows, cols)
    for i in range(1, strips):
        source = lax.rem(strip + strips - i, strips)
        part_copy(i).wait_send()
        pltpu.make_async_remote_copy(
            parts.at[source], parts.at[source], part_send.at[i], part_recv.at[i],
            device_id=(det, source), device_id_type=MESH,
        ).wait_recv()
    for i in range(dets):
        if i:
            main_copy(i).wait_send()

        @pl.when(above)
        def _():
            for p in range(2):
                up_copy(i, p).wait_send()

        @pl.when(below)
        def _():
            for p in range(2):
                down_copy(i, p).wait_send()

    normal = parts[0]
    for i in range(1, strips):
        normal = normal + parts[i]
    answer = solve(unfolded(normal))
    coef_ref[...] = coeff_row(answer)[:, :NU]
    apply_model(answer, resp, sci, out_ref, first_row, rows, total_rows, cols)


def local(dets, strips, science, template, row_taps, col_taps, stamp_rows, stamp_cols):
    _, rows, cols = science.shape
    blocks = cols // LW
    stamps = stamp_rows.shape[1]
    packed = stamps // 2 * LW
    any_space = pl.BlockSpec(memory_space=pl.ANY)
    vmem = pl.BlockSpec(memory_space=pltpu.VMEM)
    hbm = pl.BlockSpec(memory_space=pltpu.HBM)
    dma = pltpu.SemaphoreType.DMA
    results = (jax.ShapeDtypeStruct(science.shape, F32), jax.ShapeDtypeStruct((1, NU), F32))
    return pl.pallas_call(
        functools.partial(kernel, dets, strips),
        out_shape=(pltpu.VMEM(science.shape, F32), pltpu.VMEM((1, NU), F32)),
        in_specs=[hbm] * 6,
        out_specs=(vmem, vmem),
        scratch_shapes=[
            pltpu.VMEM((NB, KS), F32),
            pltpu.VMEM((NB, KS), F32),
            pltpu.SMEM((1, stamps), jnp.int32),
            pltpu.SMEM((1, stamps), jnp.int32),
            pltpu.VMEM((rows + 2 * HALO, cols), F32),
            pltpu.VMEM((16, LW), F32),
            pltpu.VMEM((NB * rows, 256), BF),
            pltpu.VMEM((NB, 256, 256), BF),
            pltpu.VMEM((NB, 256, 256), BF),
            pltpu.VMEM((NB, blocks + 2, rows, 256), BF),
            pltpu.VMEM((NB, blocks + 2, rows, 256), BF),
            pltpu.VMEM((NB, blocks, rows, LW), F32),
            pltpu.VMEM((NB, stamps // 2, rows, 256), BF),
            pltpu.VMEM((NB, stamps // 2, rows, LW), F32),
            pltpu.VMEM((rows // 8, 6 * FITTED * 8, packed), BF),
            pltpu.VMEM((rows // 8, 2 * PLANES * 8, packed), BF),
            pltpu.VMEM((rows * PLANES, 5 * LW), BF),
            pltpu.VMEM((strips, 24, LW), F32),
            pltpu.VMEM((rows, cols), F32),
            pltpu.VMEM((blocks + 2, rows + 2 * HALO, LW), F32),
            pltpu.VMEM((blocks + 1, rows, LW), F32),
            dma((dets,)), dma((dets,)), dma((2, dets)), dma((2, dets)), dma((2, dets)), dma((2, dets)),
            dma((strips,)), dma((strips,)), dma, dma, dma((4,)),
        ],
        compiler_params=pltpu.CompilerParams(
            collective_id=0, has_side_effects=True, vmem_limit_bytes=53 * 1024 * 1024
        ),
    )(
        science,
        template,
        *[pltpu.with_memory_space_constraint(v, pltpu.HBM) for v in (row_taps, col_taps, stamp_rows, stamp_cols)],
    )


def solution(mesh):
    return jax.shard_map(
        functools.partial(local, mesh.shape["det"], mesh.shape["strip"]),
        mesh=mesh,
        in_specs=(
            P("det", "strip", None),
            P(None, "strip", "det"),
            P(),
            P(),
            P("det", None),
            P("det", None),
        ),
        out_specs=(P("det", "strip", None), P("det", None)),
        check_vma=False,
    )
```
